128 devices in a mesh: lon: 16 (over z_lo, x, core), lat: 8 (over z_hi, y).
Axes of the slice: x: 4, y: 4, z: 4 (z_hi: 2, z_lo: 2; z = z_hi * 2 + z_lo), core: 2. Of those that a mesh axis runs over, the one named last changes fastest.
Arguments:
- field: bfloat16 [32, 16384, 128], P('lat', 'lon'), may hold values from -6 to 6
- conv_weight: bfloat16 [2, 3, 3, 3, 128, 128], replicated, may hold values from -0.1875 to 0.1875
- conv_bias: float32 [2, 3, 128], replicated, may hold values from -3 to 3
- spec_real: bfloat16 [2, 128, 128, 128], P(None, 'lon'), may hold values from -1.5 to 1.5
- spec_imag: bfloat16 [2, 128, 128, 128], P(None, 'lon'), may hold values from -1.5 to 1.5
Outputs:
- result: bfloat16 [32, 16384, 128], P('lat', 'lon')
The draws below stay inside these ranges and needn't reach their ends.
All inputs are finite; a program needn't handle non-finite values.
Results may differ from the reference program's by a relative error of at most 0.0045.
Values may be sent and summed in bfloat16 or wider, within the bound.
A program may use at most 64 MiB of HBM per device.

```python
import math
import jax
import jax.numpy as jnp
from jax import lax

C = 128
MODES = 128
BLOCKS = 2
CONVS = 3
NLAT = 32
NLON = 16384


def block_levels(key, extent, split, least, high):
    level = 1.0
    for dim, shards_of in split:
        draws = jax.random.uniform(jax.random.fold_in(jax.random.fold_in(key, 6), dim), (shards_of,), jnp.float32, least / len(split), high / len(split))
        level = level * jnp.repeat(jnp.exp(draws), extent[dim] // shards_of).reshape((-1,) + (1,) * (len(extent) - 1 - dim))
    return level


def scatter_about(rng, dims, width, bound, split=(), kind=jnp.bfloat16):
    entries = width * jax.random.normal(rng, dims, jnp.float32)
    if split:
        entries = entries * block_levels(rng, dims, split, -0.22, 0.18)
    return jnp.clip(entries, -bound, bound).astype(kind)


def setup_inputs(seed: int = 0) -> dict:
    seeds = jax.random.split(jax.random.key(seed), 6)
    field = scatter_about(seeds[0], (NLAT, NLON, C), 1.0, 6.0, ((0, 8), (1, 16)))
    conv_weight = scatter_about(seeds[1], (BLOCKS, CONVS, 3, 3, C, C), (9 * C) ** -0.5, 0.1875)
    conv_bias = scatter_about(seeds[2], (BLOCKS, CONVS, C), 0.5, 3.0, (), jnp.float32)
    spec_real = scatter_about(seeds[3], (BLOCKS, MODES, C, C), (C // 8) ** -0.5, 1.5, ((1, 16),))
    spec_imag = scatter_about(seeds[4], (BLOCKS, MODES, C, C), (C // 8) ** -0.5, 1.5, ((1, 16),))
    return {"field": field, "conv_weight": conv_weight, "conv_bias": conv_bias, "spec_real": spec_real, "spec_imag": spec_imag}


def make_tables(lon_total, mode_count):
    cells = jnp.arange(lon_total, dtype=jnp.int32)
    waves = jnp.arange(mode_count, dtype=jnp.int32)
    product = cells[:, None] * waves[None, :] % lon_total
    theta = product.astype(jnp.float32) * (2.0 * math.pi / lon_total)
    full = jnp.stack([jnp.cos(theta), -jnp.sin(theta)], axis=2)
    basis = full.reshape(lon_total, 2 * mode_count)
    weights = jnp.where(waves == 0, 1.0, 2.0).astype(jnp.float32)
    inverse = (full * weights[None, :, None]).reshape(lon_total, 2 * mode_count)
    return (basis, inverse)

def convolve(state, kernels, bias):
    padded = jnp.pad(state, ((1, 1), (0, 0), (0, 0)))
    padded = jnp.concatenate([padded[:, -1:], padded, padded[:, :1]], axis=1)
    rows_out = state.shape[0]
    cols_out = state.shape[1]
    running = jnp.zeros(state.shape[:2] + (kernels.shape[3],), jnp.float32)
    for tap_a in range(3):
        for tap_d in range(3):
            window = padded[tap_a:tap_a + rows_out, tap_d:tap_d + cols_out].astype(jnp.float32)
            running = running + jnp.einsum('rnc,cd->rnd', window, kernels[tap_a, tap_d].astype(jnp.float32))
    return jax.nn.silu(running + bias).astype(jnp.bfloat16)

def mix_modes(spectrum, real_weight, imag_weight):
    halves = spectrum.reshape(real_weight.shape[0], 2, spectrum.shape[1], spectrum.shape[2])
    real_in = halves[:, 0]
    imag_in = halves[:, 1]
    wr = real_weight.astype(jnp.float32)
    wi = imag_weight.astype(jnp.float32)
    high = lax.Precision.HIGHEST
    real_out = jnp.einsum('klc,kcd->kld', real_in, wr, precision=high) - jnp.einsum('klc,kcd->kld', imag_in, wi, precision=high)
    imag_out = jnp.einsum('klc,kcd->kld', real_in, wi, precision=high) + jnp.einsum('klc,kcd->kld', imag_in, wr, precision=high)
    stacked = jnp.stack([real_out, imag_out], axis=1)
    return stacked.reshape(spectrum.shape)

def reference(field, conv_weight, conv_bias, spec_real, spec_imag):
    basis, inverse = make_tables(NLON, MODES)
    scale = 1.0 / math.sqrt(NLON)
    high = lax.Precision.HIGHEST
    state = field
    for block_index in range(BLOCKS):
        hidden = state
        for layer_index in range(CONVS):
            hidden = convolve(hidden, conv_weight[block_index, layer_index], conv_bias[block_index, layer_index])
        spectrum = jnp.einsum('nj,lnc->jlc', basis, hidden.astype(jnp.float32), precision=high) * scale
        mixed = mix_modes(spectrum, spec_real[block_index], spec_imag[block_index])
        spectral = jnp.einsum('nj,jlc->lnc', inverse, mixed, precision=high) * scale
        state = jnp.tanh(state.astype(jnp.float32) + hidden.astype(jnp.float32) + spectral).astype(jnp.bfloat16)
    return state
```

```python
import math

import jax
import jax.numpy as jnp
import numpy as np
from jax import lax
from jax.experimental import pallas as pl
from jax.experimental.pallas import tpu as pltpu
from jax.sharding import PartitionSpec as P

BLOCKS = 2
CONVS = 3
LON_DEVICES = 16
LAT_DEVICES = 8
CHIPS = 8
COLS = 1024
STRIPS = 16
TILES = 64
ROWS = 4
CH = 128
OWNED = 8
EXT = 70
STEP = 17
F32 = jnp.float32
BF16 = jnp.bfloat16
MESH = pl.DeviceIdType.MESH


def tables():
    total = LON_DEVICES * COLS
    tile, strip = np.meshgrid(np.arange(TILES), np.arange(STRIPS), indexing="ij")
    cell = (strip * TILES + tile).reshape(-1)
    core, chip, part, low = np.meshgrid(
        np.arange(2), np.arange(CHIPS), np.arange(2), np.arange(OWNED), indexing="ij"
    )
    mode = (OWNED * (2 * chip + core) + low).reshape(-1)
    part = part.reshape(-1)
    theta = 2.0 * np.pi / total * ((mode[:, None] * cell[None, :]) % total)
    full = np.where(part[:, None] == 0, np.cos(theta), -np.sin(theta))
    weight = np.where(mode == 0, 1.0, 2.0)[:, None] / total

    def split(table):
        table = table.astype(np.float32)
        hi = table.astype(jnp.bfloat16)
        return hi, (table - hi.astype(np.float32)).astype(jnp.bfloat16)

    forward = np.concatenate(split(full), axis=0)
    inverse = np.concatenate(split((full * weight).T), axis=1)
    phi = 2.0 * np.pi / 16.0 * ((np.arange(16)[:, None] * np.arange(OWNED)[None, :]) % 16)
    turn = np.stack([np.cos(phi), np.sin(phi)], axis=1).astype(np.float32)
    turn = np.broadcast_to(turn[..., None], (16, 2, OWNED, CH)).copy()
    return forward, inverse, turn


def split2(value):
    hi = value.astype(BF16)
    return hi, (value - hi.astype(F32)).astype(BF16)


def kernel(field, cw, cb, sr, si, ft, iv, tw, out,
           f_v, cw_v, cb_v, sr_v, si_v, ft_v, iv_v, tw_v, T, SW, X, H1, H2, H3, ST, S,
           PART, DR, RSEND, RRECV, G,
           in_sem, lon_s, lon_r, lat_s, lat_r, d_s, d_r, rs_s, rs_r, ag_s, ag_r, fw_s, fw_r):
    d = lax.axis_index("lon")
    lt = lax.axis_index("lat")
    core = lax.rem(d, 2)
    chip = lax.div(d, 2)
    sibling = chip * 2 + 1 - core
    right = lax.rem(d + 1, LON_DEVICES)
    left = lax.rem(d + LON_DEVICES - 1, LON_DEVICES)
    outer = jnp.where(core == 0, left, right)
    has_up = lt > 0
    has_down = lt < LAT_DEVICES - 1

    loads = [
        pltpu.make_async_copy(src, dst, in_sem.at[i])
        for i, (src, dst) in enumerate(
            [(field, f_v), (cw, cw_v), (cb, cb_v), (sr, sr_v), (si, si_v), (ft, ft_v),
             (iv, iv_v), (tw, tw_v)]
        )
    ]
    for load in loads:
        load.start()

    barrier = pltpu.get_barrier_semaphore()
    pl.semaphore_signal(barrier, inc=1, device_id={"lon": sibling}, device_id_type=MESH)
    pl.semaphore_signal(barrier, inc=1, device_id={"lon": outer}, device_id_type=MESH)
    for j in range(1, CHIPS):
        peer = lax.rem(chip + j, CHIPS) * 2 + core
        pl.semaphore_signal(barrier, inc=1, device_id={"lon": peer}, device_id_type=MESH)

    @pl.when(has_up)
    def _():
        pl.semaphore_signal(barrier, inc=1, device_id={"lat": lt - 1}, device_id_type=MESH)

    @pl.when(has_down)
    def _():
        pl.semaphore_signal(barrier, inc=1, device_id={"lat": lt + 1}, device_id_type=MESH)

    @pl.when(jnp.logical_not(has_up))
    def _():
        for b in range(BLOCKS):
            X[b, 0:3] = jnp.zeros((3, EXT, STRIPS, CH), BF16)

    @pl.when(jnp.logical_not(has_down))
    def _():
        for b in range(BLOCKS):
            X[b, 7:10] = jnp.zeros((3, EXT, STRIPS, CH), BF16)

    loads[0].wait()
    for row in range(ROWS):
        S[row] = f_v[row].astype(F32)
        for q in range(TILES):
            X[0, 3 + row, 3 + q] = S[row, pl.ds(q, STRIPS, stride=TILES), :].astype(BF16)

    pl.semaphore_wait(
        barrier, CHIPS + 1 + has_up.astype(jnp.int32) + has_down.astype(jnp.int32)
    )

    loads[1].wait()
    loads[2].wait()
    zero = jnp.zeros((CH, CH), BF16)

    def build(i, _):
        b = lax.div(i, CONVS)
        layer = lax.rem(i, CONVS)
        for tap in range(3):
            w0, w1, w2 = (cw_v[b, layer, a, tap] for a in range(3))
            for r, (first, second) in enumerate(((w0, zero), (w1, w0), (w2, w1), (zero, w2))):
                rows = pl.ds((tap * 4 + r) * CH, CH)
                T[i, rows, 0:CH] = first
                T[i, rows, CH:2 * CH] = second
        return 0

    lax.fori_loop(0, BLOCKS * CONVS, build, 0)

    loads[3].wait()
    loads[4].wait()

    def build_spec(i, _):
        b = lax.div(i, OWNED)
        m = lax.rem(i, OWNED)
        wr = sr_v[b, m]
        wi = si_v[b, m]
        SW[i, 0:CH, 0:CH] = wr
        SW[i, 0:CH, CH:2 * CH] = wi
        SW[i, CH:2 * CH, 0:CH] = -wi
        SW[i, CH:2 * CH, CH:2 * CH] = wr
        return 0

    lax.fori_loop(0, BLOCKS * OWNED, build_spec, 0)
    for load in loads[5:]:
        load.wait()

    cos = tw_v[d, 0]
    sin = tw_v[d, 1]
    flip = (1 - 2 * core).astype(F32)
    up_mask = has_up.astype(F32)
    down_mask = has_down.astype(F32)
    strip = lax.broadcasted_iota(jnp.int32, (STRIPS, CH), 0)
    sub = lax.rem(lax.broadcasted_iota(jnp.int32, (ROWS * OWNED, 2 * CH), 0), OWNED)

    def convolve(source, target, index, layer, b, at, to, pairs, masks):
        bias = cb_v[b, pl.ds(layer, 1), :]
        for pair in range(pairs):
            lhs = jnp.concatenate(
                [source(2 * pair + r, at + tap).reshape(STEP * STRIPS, CH)
                 for tap in range(3) for r in range(4)],
                axis=1,
            )
            total = jnp.dot(lhs, T[index], preferred_element_type=F32)
            for o in range(2):
                half = 0.5 * (total[:, o * CH:(o + 1) * CH] + bias)
                value = half * jnp.tanh(half) + half
                mask = masks.get(2 * pair + o)
                if mask is not None:
                    value = value * mask
                target[2 * pair + o, pl.ds(to, STEP)] = value.astype(BF16).reshape(
                    STEP, STRIPS, CH
                )

    def block(b, _):
        to_right = pltpu.make_async_remote_copy(
            src_ref=X.at[b, 3:7, 64:67], dst_ref=ST.at[b, 0],
            send_sem=lon_s.at[0], recv_sem=lon_r.at[b, 0],
            device_id={"lon": right}, device_id_type=MESH)
        to_left = pltpu.make_async_remote_copy(
            src_ref=X.at[b, 3:7, 3:6], dst_ref=ST.at[b, 1],
            send_sem=lon_s.at[1], recv_sem=lon_r.at[b, 1],
            device_id={"lon": left}, device_id_type=MESH)
        to_right.start()
        to_left.start()
        to_right.wait()
        to_left.wait()
        for row in range(ROWS):
            for j in range(3):
                own = X[b, 3 + row, 64 + j].astype(F32)
                other = ST[b, 0, row, j].astype(F32)
                tile = jnp.where(strip == 0, pltpu.roll(other, 1, 0), pltpu.roll(own, 1, 0))
                X[b, 3 + row, j] = tile.astype(BF16)
                own = X[b, 3 + row, 3 + j].astype(F32)
                other = ST[b, 1, row, j].astype(F32)
                tile = jnp.where(
                    strip == STRIPS - 1,
                    pltpu.roll(other, STRIPS - 1, 0), pltpu.roll(own, STRIPS - 1, 0))
                X[b, 3 + row, 67 + j] = tile.astype(BF16)

        def down_copy(first, count, slot):
            return pltpu.make_async_remote_copy(
                src_ref=X.at[b, 4:7, pl.ds(first, count)],
                dst_ref=X.at[b, 0:3, pl.ds(first, count)],
                send_sem=lat_s.at[0, slot], recv_sem=lat_r.at[b, 0, slot],
                device_id={"lat": lt + 1}, device_id_type=MESH)

        def up_copy(first, count, slot):
            return pltpu.make_async_remote_copy(
                src_ref=X.at[b, 3:6, pl.ds(first, count)],
                dst_ref=X.at[b, 7:10, pl.ds(first, count)],
                send_sem=lat_s.at[1, slot], recv_sem=lat_r.at[b, 1, slot],
                device_id={"lat": lt - 1}, device_id_type=MESH)

        pieces = [(0, 2, 4)] + [(2 + STEP * c, STEP, c) for c in range(4)]

        @pl.when(has_down)
        def _():
            for piece in pieces:
                down_copy(*piece).start()

        @pl.when(has_up)
        def _():
            for piece in pieces:
                up_copy(*piece).start()

        @pl.when(has_up)
        def _():
            down_copy(*pieces[0]).wait_recv()

        @pl.when(has_down)
        def _():
            up_copy(*pieces[0]).wait_recv()

        def chunk(c, _):
            @pl.when(has_up)
            def _():
                down_copy(2 + STEP * c, STEP, c).wait_recv()

            @pl.when(has_down)
            def _():
                up_copy(2 + STEP * c, STEP, c).wait_recv()

            base = STEP * c
            convolve(lambda r, t: X[b, r, pl.ds(t, STEP)], H1, b * CONVS, 0, b, base,
                     base + 2, 4, {0: up_mask, 1: up_mask, 6: down_mask, 7: down_mask})
            convolve(lambda r, t: H1[r, pl.ds(t, STEP)], H2, b * CONVS + 1, 1, b, base,
                     base + 2, 3, {0: up_mask, 5: down_mask})
            convolve(lambda r, t: H2[r, pl.ds(t, STEP)], H3, b * CONVS + 2, 2, b, base,
                     base, 2, {})
            return 0

        lax.fori_loop(0, 4, chunk, 0)

        for half in range(2):
            rhs = jnp.concatenate(
                [H3[2 * half + l, 4:68].reshape(COLS, CH) for l in range(2)], axis=1)
            both = jnp.dot(ft_v[...], rhs, preferred_element_type=F32)
            total = both[0:256] + both[256:512]
            for o in range(2):
                for ch in range(CHIPS):
                    first = (o * CHIPS + ch) * 16
                    for l in range(2):
                        re = total[first:first + 8, l * CH:(l + 1) * CH]
                        im = total[first + 8:first + 16, l * CH:(l + 1) * CH]
                        new_re = re * cos + im * sin
                        new_im = im * cos - re * sin
                        if o == 1:
                            new_re = new_re * flip
                            new_im = new_im * flip
                        lanes = pl.ds((2 * half + l) * CH, CH)
                        PART[o, ch, 0:8, lanes] = new_re
                        PART[o, ch, 8:16, lanes] = new_im

        swap = pltpu.make_async_remote_copy(
            src_ref=PART.at[1 - core], dst_ref=DR.at[b],
            send_sem=d_s.at[0], recv_sem=d_r.at[b],
            device_id={"lon": sibling}, device_id_type=MESH)
        swap.start()
        swap.wait()
        RSEND[...] = PART[core] + DR[b]

        def scatter(j):
            peer = lax.rem(chip + j, CHIPS)
            return pltpu.make_async_remote_copy(
                src_ref=RSEND.at[peer], dst_ref=RRECV.at[b, j - 1],
                send_sem=rs_s.at[j - 1], recv_sem=rs_r.at[b, j - 1],
                device_id={"lon": peer * 2 + core}, device_id_type=MESH)

        for j in range(1, CHIPS):
            scatter(j).start()
        spectrum = RSEND[chip]
        for j in range(1, CHIPS):
            scatter(j).wait()
        for j in range(1, CHIPS):
            spectrum = spectrum + RRECV[b, j - 1]

        lhs = jnp.concatenate(
            [jnp.concatenate([spectrum[0:8, l * CH:(l + 1) * CH],
                              spectrum[8:16, l * CH:(l + 1) * CH]], axis=1)
             for l in range(ROWS)], axis=0)
        lhs = jnp.concatenate(split2(lhs), axis=0)
        mixed = jnp.zeros((ROWS * OWNED, 2 * CH), F32)
        for m in range(OWNED):
            both = jnp.dot(lhs, SW[b * OWNED + m], preferred_element_type=F32)
            mixed = jnp.where(sub == m, both[0:32] + both[32:64], mixed)
        for l in range(ROWS):
            G[b, core, chip, :, l * CH:(l + 1) * CH] = jnp.concatenate(
                [mixed[8 * l:8 * l + 8, 0:CH], mixed[8 * l:8 * l + 8, CH:2 * CH]], axis=0
            ).astype(BF16)

        def gather(j):
            peer = lax.rem(chip + j, CHIPS)
            return pltpu.make_async_remote_copy(
                src_ref=G.at[b, core, chip], dst_ref=G.at[b, core, chip],
                send_sem=ag_s.at[j - 1], recv_sem=ag_r.at[b, j - 1],
                device_id={"lon": peer * 2 + core}, device_id_type=MESH)

        for j in range(1, CHIPS):
            gather(j).start()

        def arrived(j):
            peer = lax.rem(chip + CHIPS - j, CHIPS)
            return pltpu.make_async_remote_copy(
                src_ref=G.at[b, core, peer], dst_ref=G.at[b, core, peer],
                send_sem=ag_s.at[j - 1], recv_sem=ag_r.at[b, j - 1],
                device_id={"lon": peer * 2 + core}, device_id_type=MESH)

        for j in range(1, CHIPS):
            arrived(j).wait_recv()
        forward = pltpu.make_async_remote_copy(
            src_ref=G.at[b, core], dst_ref=G.at[b, core],
            send_sem=fw_s.at[0], recv_sem=fw_r.at[b],
            device_id={"lon": sibling}, device_id_type=MESH)
        forward.start()
        back = pltpu.make_async_remote_copy(
            src_ref=G.at[b, 1 - core], dst_ref=G.at[b, 1 - core],
            send_sem=fw_s.at[0], recv_sem=fw_r.at[b],
            device_id={"lon": sibling}, device_id_type=MESH)
        back.wait_recv()

        his = []
        los = []
        for o in range(2):
            for ch in range(CHIPS):
                parts = []
                for l in range(ROWS):
                    value = G[b, o, ch, :, l * CH:(l + 1) * CH].astype(F32)
                    re = value[0:8]
                    im = value[8:16]
                    new_re = re * cos - im * sin
                    new_im = re * sin + im * cos
                    if o == 1:
                        new_re = new_re * flip
                        new_im = new_im * flip
                    parts.append(jnp.concatenate([new_re, new_im], axis=0))
                hi, lo = split2(jnp.concatenate(parts, axis=1))
                his.append(hi)
                los.append(lo)
        hi = jnp.concatenate(his, axis=0)
        lo = jnp.concatenate(los, axis=0)
        rhs = jnp.concatenate([hi, hi, lo], axis=0)

        def finish(c, _):
            rows = pl.ds(c * 256, 256)
            table = iv_v[rows, :]
            lhs = jnp.concatenate([table, table[:, 0:256]], axis=1)
            spectral = jnp.dot(lhs, rhs, preferred_element_type=F32)
            for l in range(ROWS):
                x = X[b, 3 + l, pl.ds(3 + 16 * c, 16)].reshape(256, CH).astype(F32)
                h = H3[l, pl.ds(4 + 16 * c, 16)].reshape(256, CH).astype(F32)
                value = jnp.tanh(x + h + spectral[:, l * CH:(l + 1) * CH])
                X[b + 1, 3 + l, pl.ds(3 + 16 * c, 16)] = value.astype(BF16).reshape(
                    16, STRIPS, CH)
            return 0

        lax.fori_loop(0, 4, finish, 0)

        @pl.when(has_down)
        def _():
            for piece in pieces:
                down_copy(*piece).wait_send()

        @pl.when(has_up)
        def _():
            for piece in pieces:
                up_copy(*piece).wait_send()

        for j in range(1, CHIPS):
            gather(j).wait_send()
        forward.wait_send()
        return 0

    lax.fori_loop(0, BLOCKS, block, 0)

    for row in range(ROWS):
        for q in range(TILES):
            S[row, pl.ds(q, STRIPS, stride=TILES), :] = X[BLOCKS, 3 + row, 3 + q].astype(F32)
        f_v[row] = S[row].astype(BF16)
    store = pltpu.make_async_copy(f_v, out, in_sem.at[0])
    store.start()
    store.wait()


def per_device(field, conv_weight, conv_bias, spec_real, spec_imag):
    forward, inverse, turn = tables()
    args = (field, conv_weight, conv_bias, spec_real, spec_imag,
            jnp.asarray(forward), jnp.asarray(inverse), jnp.asarray(turn))
    tile = (STRIPS, CH)
    dma = pltpu.SemaphoreType.DMA
    return pl.pallas_call(
        kernel,
        out_shape=jax.ShapeDtypeStruct(field.shape, BF16),
        in_specs=[pl.BlockSpec(memory_space=pl.ANY)] * len(args),
        out_specs=pl.BlockSpec(memory_space=pl.ANY),
        scratch_shapes=[pltpu.VMEM(a.shape, a.dtype) for a in args] + [
            pltpu.VMEM((BLOCKS * CONVS, 12 * CH, 2 * CH), BF16),
            pltpu.VMEM((BLOCKS * OWNED, 2 * CH, 2 * CH), BF16),
            pltpu.VMEM((BLOCKS + 1, 10, EXT) + tile, BF16),
            pltpu.VMEM((8, EXT) + tile, BF16),
            pltpu.VMEM((6, EXT) + tile, BF16),
            pltpu.VMEM((4, EXT) + tile, BF16),
            pltpu.VMEM((BLOCKS, 2, ROWS, 3) + tile, BF16),
            pltpu.VMEM((ROWS, COLS, CH), F32),
            pltpu.VMEM((2, CHIPS, 16, ROWS * CH), F32),
            pltpu.VMEM((BLOCKS, CHIPS, 16, ROWS * CH), F32),
            pltpu.VMEM((CHIPS, 16, ROWS * CH), F32),
            pltpu.VMEM((BLOCKS, CHIPS - 1, 16, ROWS * CH), F32),
            pltpu.VMEM((BLOCKS, 2, CHIPS, 16, ROWS * CH), BF16),
            dma((8,)), dma((2,)), dma((BLOCKS, 2)), dma((2, 5)), dma((BLOCKS, 2, 5)),
            dma((1,)), dma((BLOCKS,)),
            dma((CHIPS - 1,)), dma((BLOCKS, CHIPS - 1)),
            dma((CHIPS - 1,)), dma((BLOCKS, CHIPS - 1)),
            dma((1,)), dma((BLOCKS,)),
        ],
        compiler_params=pltpu.CompilerParams(
            collective_id=0, has_side_effects=True, vmem_limit_bytes=62 * 1024 * 1024),
    )(*args)


def solution(mesh):
    return jax.shard_map(
        per_device,
        mesh=mesh,
        in_specs=(
            P("lat", "lon", None),
            P(),
            P(),
            P(None, "lon", None, None),
            P(None, "lon", None, None),
        ),
        out_specs=P("lat", "lon", None),
        check_vma=False,
    )
```

```python
import contextlib

import jax
import jax.numpy as jnp
import numpy as np
from jax import lax
from jax.experimental import pallas as pl
from jax.experimental.pallas import tpu as pltpu
from jax.sharding import PartitionSpec as P

BLOCKS = 2
CONVS = 3
LON_DEVICES = 16
LAT_DEVICES = 8
CHIPS = 8
COLS = 1024
STRIPS = 16
TILES = 64
ROWS = 4
CH = 128
OWNED = 8
EXT = 70
STEP = 17
F32 = jnp.float32
BF16 = jnp.bfloat16
MESH = pl.DeviceIdType.MESH


def scope(name):
    return contextlib.nullcontext()


def tables():
    total = LON_DEVICES * COLS
    tile, strip = np.meshgrid(np.arange(TILES), np.arange(STRIPS), indexing="ij")
    cell = (strip * TILES + tile).reshape(-1)
    core, chip, part, low = np.meshgrid(
        np.arange(2), np.arange(CHIPS), np.arange(2), np.arange(OWNED), indexing="ij"
    )
    mode = (OWNED * (2 * chip + core) + low).reshape(-1)
    part = part.reshape(-1)
    theta = 2.0 * np.pi / total * ((mode[:, None] * cell[None, :]) % total)
    full = np.where(part[:, None] == 0, np.cos(theta), -np.sin(theta))
    weight = np.where(mode == 0, 1.0, 2.0)[:, None] / total

    def split(table):
        table = table.astype(np.float32)
        hi = table.astype(jnp.bfloat16)
        return hi, (table - hi.astype(np.float32)).astype(jnp.bfloat16)

    forward = np.concatenate(split(full), axis=0)
    inverse = np.concatenate(split((full * weight).T), axis=1)
    phi = 2.0 * np.pi / 16.0 * ((np.arange(16)[:, None] * np.arange(OWNED)[None, :]) % 16)
    turn = np.stack([np.cos(phi), np.sin(phi)], axis=1).astype(np.float32)
    turn = np.broadcast_to(turn[..., None], (16, 2, OWNED, CH)).copy()
    return forward, inverse, turn


def split2(value):
    hi = value.astype(BF16)
    return hi, (value - hi.astype(F32)).astype(BF16)


def kernel(field, cw, cb, sr, si, ft, iv, tw, out,
           f_v, cw_v, cb_v, sr_v, si_v, ft_v, iv_v, tw_v, T, SW, X, H1, H2, H3, ST, S,
           PART, DR, RSEND, RRECV, G,
           in_sem, lon_s, lon_r, lat_s, lat_r, d_s, d_r, rs_s, rs_r, ag_s, ag_r, fw_s, fw_r):
    d = lax.axis_index("lon")
    lt = lax.axis_index("lat")
    core = lax.rem(d, 2)
    chip = lax.div(d, 2)
    sibling = chip * 2 + 1 - core
    right = lax.rem(d + 1, LON_DEVICES)
    left = lax.rem(d + LON_DEVICES - 1, LON_DEVICES)
    outer = jnp.where(core == 0, left, right)
    has_up = lt > 0
    has_down = lt < LAT_DEVICES - 1

    loads = [
        pltpu.make_async_copy(src, dst, in_sem.at[i])
        for i, (src, dst) in enumerate(
            [(field, f_v), (cw, cw_v), (cb, cb_v), (sr, sr_v), (si, si_v), (ft, ft_v),
             (iv, iv_v), (tw, tw_v)]
        )
    ]
    for load in loads:
        load.start()

    barrier = pltpu.get_barrier_semaphore()
    pl.semaphore_signal(barrier, inc=1, device_id={"lon": sibling}, device_id_type=MESH)
    pl.semaphore_signal(barrier, inc=1, device_id={"lon": outer}, device_id_type=MESH)
    for j in range(1, CHIPS):
        peer = lax.rem(chip + j, CHIPS) * 2 + core
        pl.semaphore_signal(barrier, inc=1, device_id={"lon": peer}, device_id_type=MESH)

    @pl.when(has_up)
    def _():
        pl.semaphore_signal(barrier, inc=1, device_id={"lat": lt - 1}, device_id_type=MESH)

    @pl.when(has_down)
    def _():
        pl.semaphore_signal(barrier, inc=1, device_id={"lat": lt + 1}, device_id_type=MESH)

    @pl.when(jnp.logical_not(has_up))
    def _():
        for b in range(BLOCKS):
            X[b, 0:3] = jnp.zeros((3, EXT, STRIPS, CH), BF16)

    @pl.when(jnp.logical_not(has_down))
    def _():
        for b in range(BLOCKS):
            X[b, 7:10] = jnp.zeros((3, EXT, STRIPS, CH), BF16)

    with scope("permute_in"):
        loads[0].wait()
        for row in range(ROWS):
            S[row] = f_v[row].astype(F32)
            for q in range(TILES):
                X[0, 3 + row, 3 + q] = S[row, pl.ds(q, STRIPS, stride=TILES), :].astype(BF16)

    with scope("barrier"):
        pl.semaphore_wait(
            barrier, CHIPS + 1 + has_up.astype(jnp.int32) + has_down.astype(jnp.int32)
        )

    def build_weights():
        loads[1].wait()
        loads[2].wait()
        zero = jnp.zeros((CH, CH), BF16)

        def build(i, _):
            b = lax.div(i, CONVS)
            layer = lax.rem(i, CONVS)
            for tap in range(3):
                w0, w1, w2 = (cw_v[b, layer, a, tap] for a in range(3))
                for r, (first, second) in enumerate(((w0, zero), (w1, w0), (w2, w1), (zero, w2))):
                    rows = pl.ds((tap * 4 + r) * CH, CH)
                    T[i, rows, 0:CH] = first
                    T[i, rows, CH:2 * CH] = second
            return 0

        lax.fori_loop(0, BLOCKS * CONVS, build, 0)

        loads[3].wait()
        loads[4].wait()

        def build_spec(i, _):
            b = lax.div(i, OWNED)
            m = lax.rem(i, OWNED)
            wr = sr_v[b, m]
            wi = si_v[b, m]
            SW[i, 0:CH, 0:CH] = wr
            SW[i, 0:CH, CH:2 * CH] = wi
            SW[i, CH:2 * CH, 0:CH] = -wi
            SW[i, CH:2 * CH, CH:2 * CH] = wr
            return 0

        lax.fori_loop(0, BLOCKS * OWNED, build_spec, 0)
        for load in loads[5:7]:
            load.wait()

    loads[7].wait()
    cos = tw_v[d, 0]
    sin = tw_v[d, 1]
    flip = (1 - 2 * core).astype(F32)
    up_mask = has_up.astype(F32)
    down_mask = has_down.astype(F32)
    strip = lax.broadcasted_iota(jnp.int32, (STRIPS, CH), 0)
    sub = lax.rem(lax.broadcasted_iota(jnp.int32, (ROWS * OWNED, 2 * CH), 0), OWNED)

    def convolve(source, target, index, layer, b, at, to, pairs, masks):
        bias = cb_v[layer, pl.ds(b, 1), :]
        for pair in range(pairs):
            lhs = jnp.concatenate(
                [source(2 * pair + r, at + tap).reshape(STEP * STRIPS, CH)
                 for tap in range(3) for r in range(4)], axis=1)
            total = jnp.dot(lhs, T[index], preferred_element_type=F32)
            for o in range(2):
                half = 0.5 * (total[:, o * CH:(o + 1) * CH] + bias)
                value = half * jnp.tanh(half) + half
                mask = masks.get(2 * pair + o)
                if mask is not None:
                    value = value * mask
                target[2 * pair + o, pl.ds(to, STEP)] = value.astype(BF16).reshape(
                    STEP, STRIPS, CH
                )

    def result(c):
        return pltpu.make_async_copy(
            X.at[BLOCKS, 3:7, pl.ds(3 + 16 * c, 16)], out.at[:, pl.ds(16 * c, 16)], in_sem.at[c])

    def block(b, _):
        to_right = pltpu.make_async_remote_copy(
            src_ref=X.at[b, 3:7, 64:67], dst_ref=ST.at[b, 0],
            send_sem=lon_s.at[0], recv_sem=lon_r.at[b, 0],
            device_id={"lon": right}, device_id_type=MESH)
        to_left = pltpu.make_async_remote_copy(
            src_ref=X.at[b, 3:7, 3:6], dst_ref=ST.at[b, 1],
            send_sem=lon_s.at[1], recv_sem=lon_r.at[b, 1],
            device_id={"lon": left}, device_id_type=MESH)
        to_right.start()
        to_left.start()
        def down_copy(first, count, slot):
            return pltpu.make_async_remote_copy(
                src_ref=X.at[b, 4:7, pl.ds(first, count)],
                dst_ref=X.at[b, 0:3, pl.ds(first, count)],
                send_sem=lat_s.at[0, slot], recv_sem=lat_r.at[b, 0, slot],
                device_id={"lat": lt + 1}, device_id_type=MESH)

        def up_copy(first, count, slot):
            return pltpu.make_async_remote_copy(
                src_ref=X.at[b, 3:6, pl.ds(first, count)],
                dst_ref=X.at[b, 7:10, pl.ds(first, count)],
                send_sem=lat_s.at[1, slot], recv_sem=lat_r.at[b, 1, slot],
                device_id={"lat": lt - 1}, device_id_type=MESH)

        pieces = [(17, 19, 0), (36, 17, 1), (53, 17, 2), (0, 17, 3)]

        def start(some):
            @pl.when(has_down)
            def _():
                for piece in some:
                    down_copy(*piece).start()

            @pl.when(has_up)
            def _():
                for piece in some:
                    up_copy(*piece).start()

        start(pieces[:2])
        with scope("lonwait"):
            to_right.wait()
            to_left.wait()
        with scope("halo"):
            for row in range(ROWS):
                for j in range(3):
                    own = X[b, 3 + row, 64 + j].astype(F32)
                    other = ST[b, 0, row, j].astype(F32)
                    tile = jnp.where(strip == 0, pltpu.roll(other, 1, 0), pltpu.roll(own, 1, 0))
                    X[b, 3 + row, j] = tile.astype(BF16)
                    own = X[b, 3 + row, 3 + j].astype(F32)
                    other = ST[b, 1, row, j].astype(F32)
                    tile = jnp.where(
                        strip == STRIPS - 1,
                        pltpu.roll(other, STRIPS - 1, 0), pltpu.roll(own, STRIPS - 1, 0))
                    X[b, 3 + row, 67 + j] = tile.astype(BF16)
        start(pieces[2:])

        @pl.when(b == 0)
        def _():
            with scope("build"):
                build_weights()

        def arrive(first, count, slot):
            @pl.when(has_up)
            def _():
                down_copy(first, count, slot).wait_recv()

            @pl.when(has_down)
            def _():
                up_copy(first, count, slot).wait_recv()

        def chunk(c, _):
            with scope("latwait"):
                @pl.when(c == 0)
                def _():
                    arrive(*pieces[0])

                @pl.when(c > 0)
                def _():
                    arrive(jnp.where(c == 3, 0, 19 + STEP * c), STEP, c)

            last = (c == 3).astype(jnp.int32)
            s1 = jnp.where(c == 3, 1, 18 + STEP * c)
            s2 = s1 - 1 + 2 * last
            s3 = s1 - 2 + 4 * last
            with scope("conv1"):
                convolve(lambda r, t: X[b, r, pl.ds(t, STEP)], H1, b * CONVS, 0, b, s1 - 1, s1, 4,
                         {0: up_mask, 1: up_mask, 6: down_mask, 7: down_mask})
            with scope("conv2"):
                convolve(lambda r, t: H1[r, pl.ds(t, STEP)], H2, b * CONVS + 1, 1, b, s2 - 1, s2, 3,
                         {0: up_mask, 5: down_mask})
            with scope("conv3"):
                convolve(lambda r, t: H2[r, pl.ds(t, STEP)], H3, b * CONVS + 2, 2, b, s3 - 1, s3, 2,
                         {})
            return 0

        lax.fori_loop(0, 4, chunk, 0)

        with scope("dft"):
            for half in range(2):
                rhs = jnp.concatenate(
                    [H3[2 * half + l, 3:67].reshape(COLS, CH) for l in range(2)], axis=1)
                both = jnp.dot(ft_v[...], rhs, preferred_element_type=F32)
                total = both[0:256] + both[256:512]
                for o in range(2):
                    for ch in range(CHIPS):
                        first = (o * CHIPS + ch) * 16
                        for l in range(2):
                            re = total[first:first + 8, l * CH:(l + 1) * CH]
                            im = total[first + 8:first + 16, l * CH:(l + 1) * CH]
                            new_re = re * cos + im * sin
                            new_im = im * cos - re * sin
                            if o == 1:
                                new_re = new_re * flip
                                new_im = new_im * flip
                            lanes = pl.ds((2 * half + l) * CH, CH)
                            PART[o, ch, 0:8, lanes] = new_re
                            PART[o, ch, 8:16, lanes] = new_im

        swap = pltpu.make_async_remote_copy(
            src_ref=PART.at[1 - core], dst_ref=DR.at[b],
            send_sem=d_s.at[0], recv_sem=d_r.at[b],
            device_id={"lon": sibling}, device_id_type=MESH)
        swap.start()
        with scope("swapwait"):
            swap.wait()
        RSEND[...] = PART[core] + DR[b]

        def scatter(j):
            peer = lax.rem(chip + j, CHIPS)
            return pltpu.make_async_remote_copy(
                src_ref=RSEND.at[peer], dst_ref=RRECV.at[b, j - 1],
                send_sem=rs_s.at[j - 1], recv_sem=rs_r.at[b, j - 1],
                device_id={"lon": peer * 2 + core}, device_id_type=MESH)

        for j in range(1, CHIPS):
            scatter(j).start()
        spectrum = RSEND[chip]
        with scope("rswait"):
            for j in range(1, CHIPS):
                scatter(j).wait()
        for j in range(1, CHIPS):
            spectrum = spectrum + RRECV[b, j - 1]

        with scope("mix"):
            lhs = jnp.concatenate(
                [jnp.concatenate([spectrum[0:8, l * CH:(l + 1) * CH],
                                  spectrum[8:16, l * CH:(l + 1) * CH]], axis=1)
                 for l in range(ROWS)], axis=0)
            lhs = jnp.concatenate(split2(lhs), axis=0)
            mixed = jnp.zeros((ROWS * OWNED, 2 * CH), F32)
            for m in range(OWNED):
                both = jnp.dot(lhs, SW[b * OWNED + m], preferred_element_type=F32)
                mixed = jnp.where(sub == m, both[0:32] + both[32:64], mixed)
            for l in range(ROWS):
                G[b, core, chip, :, l * CH:(l + 1) * CH] = jnp.concatenate(
                    [mixed[8 * l:8 * l + 8, 0:CH], mixed[8 * l:8 * l + 8, CH:2 * CH]], axis=0
                ).astype(BF16)

        def gather(j):
            peer = lax.rem(chip + j, CHIPS)
            return pltpu.make_async_remote_copy(
                src_ref=G.at[b, core, chip], dst_ref=G.at[b, core, chip],
                send_sem=ag_s.at[j - 1], recv_sem=ag_r.at[b, j - 1],
                device_id={"lon": peer * 2 + core}, device_id_type=MESH)

        for j in range(1, CHIPS):
            gather(j).start()

        def arrived(j):
            peer = lax.rem(chip + CHIPS - j, CHIPS)
            return pltpu.make_async_remote_copy(
                src_ref=G.at[b, core, peer], dst_ref=G.at[b, core, peer],
                send_sem=ag_s.at[j - 1], recv_sem=ag_r.at[b, j - 1],
                device_id={"lon": peer * 2 + core}, device_id_type=MESH)

        with scope("agwait"):
            for j in range(1, CHIPS):
                arrived(j).wait_recv()
        forward = pltpu.make_async_remote_copy(
            src_ref=G.at[b, core], dst_ref=G.at[b, core],
            send_sem=fw_s.at[0], recv_sem=fw_r.at[b],
            device_id={"lon": sibling}, device_id_type=MESH)
        forward.start()
        back = pltpu.make_async_remote_copy(
            src_ref=G.at[b, 1 - core], dst_ref=G.at[b, 1 - core],
            send_sem=fw_s.at[0], recv_sem=fw_r.at[b],
            device_id={"lon": sibling}, device_id_type=MESH)
        with scope("fwwait"):
            back.wait_recv()

        his = []
        los = []
        for o in range(2):
            for ch in range(CHIPS):
                parts = []
                for l in range(ROWS):
                    value = G[b, o, ch, :, l * CH:(l + 1) * CH].astype(F32)
                    re = value[0:8]
                    im = value[8:16]
                    new_re = re * cos - im * sin
                    new_im = re * sin + im * cos
                    if o == 1:
                        new_re = new_re * flip
                        new_im = new_im * flip
                    parts.append(jnp.concatenate([new_re, new_im], axis=0))
                hi, lo = split2(jnp.concatenate(parts, axis=1))
                his.append(hi)
                los.append(lo)
        hi = jnp.concatenate(his, axis=0)
        lo = jnp.concatenate(los, axis=0)
        rhs = jnp.concatenate([hi, hi, lo], axis=0)

        def finish(c, _):
            rows = pl.ds(c * 256, 256)
            table = iv_v[rows, :]
            lhs = jnp.concatenate([table, table[:, 0:256]], axis=1)
            spectral = jnp.dot(lhs, rhs, preferred_element_type=F32)
            for l in range(ROWS):
                x = X[b, 3 + l, pl.ds(3 + 16 * c, 16)].reshape(256, CH).astype(F32)
                h = H3[l, pl.ds(3 + 16 * c, 16)].reshape(256, CH).astype(F32)
                value = jnp.tanh(x + h + spectral[:, l * CH:(l + 1) * CH])
                X[b + 1, 3 + l, pl.ds(3 + 16 * c, 16)] = value.astype(BF16).reshape(
                    16, STRIPS, CH)

            @pl.when(b == BLOCKS - 1)
            def _():
                result(c).start()

            return 0

        with scope("finish"):
            lax.fori_loop(0, 4, finish, 0)

        @pl.when(has_down)
        def _():
            for piece in pieces:
                down_copy(*piece).wait_send()

        @pl.when(has_up)
        def _():
            for piece in pieces:
                up_copy(*piece).wait_send()

        for j in range(1, CHIPS):
            gather(j).wait_send()
        forward.wait_send()
        return 0

    lax.fori_loop(0, BLOCKS, block, 0)

    with scope("store"):
        for c in range(4):
            result(c).wait()


def restore(strips):
    return jnp.transpose(strips, (0, 2, 1, 3)).reshape(ROWS, COLS, CH)


def per_device(field, conv_weight, conv_bias, spec_real, spec_imag):
    forward, inverse, turn = tables()
    args = (field, conv_weight, jnp.transpose(conv_bias, (1, 0, 2)), spec_real, spec_imag,
            jnp.asarray(forward), jnp.asarray(inverse), jnp.asarray(turn))
    tile = (STRIPS, CH)
    dma = pltpu.SemaphoreType.DMA
    strips = pl.pallas_call(
        kernel,
        out_shape=jax.ShapeDtypeStruct((ROWS, TILES) + tile, BF16),
        in_specs=[pl.BlockSpec(memory_space=pl.ANY)] * len(args),
        out_specs=pl.BlockSpec(memory_space=pl.ANY),
        scratch_shapes=[pltpu.VMEM(a.shape, a.dtype) for a in args] + [
            pltpu.VMEM((BLOCKS * CONVS, 12 * CH, 2 * CH), BF16),
            pltpu.VMEM((BLOCKS * OWNED, 2 * CH, 2 * CH), BF16),
            pltpu.VMEM((BLOCKS + 1, 10, EXT) + tile, BF16),
            pltpu.VMEM((8, EXT) + tile, BF16),
            pltpu.VMEM((6, EXT) + tile, BF16),
            pltpu.VMEM((4, EXT) + tile, BF16),
            pltpu.VMEM((BLOCKS, 2, ROWS, 3) + tile, BF16),
            pltpu.VMEM((ROWS, COLS, CH), F32),
            pltpu.VMEM((2, CHIPS, 16, ROWS * CH), F32),
            pltpu.VMEM((BLOCKS, CHIPS, 16, ROWS * CH), F32),
            pltpu.VMEM((CHIPS, 16, ROWS * CH), F32),
            pltpu.VMEM((BLOCKS, CHIPS - 1, 16, ROWS * CH), F32),
            pltpu.VMEM((BLOCKS, 2, CHIPS, 16, ROWS * CH), BF16),
            dma((8,)), dma((2,)), dma((BLOCKS, 2)), dma((2, 5)), dma((BLOCKS, 2, 5)),
            dma((1,)), dma((BLOCKS,)),
            dma((CHIPS - 1,)), dma((BLOCKS, CHIPS - 1)),
            dma((CHIPS - 1,)), dma((BLOCKS, CHIPS - 1)),
            dma((1,)), dma((BLOCKS,)),
        ],
        compiler_params=pltpu.CompilerParams(
            collective_id=0, has_side_effects=True, vmem_limit_bytes=62 * 1024 * 1024),
    )(*args)
    return restore(strips)


def solution(mesh):
    return jax.shard_map(
        per_device,
        mesh=mesh,
        in_specs=(
            P("lat", "lon", None),
            P(),
            P(),
            P(None, "lon", None, None),
            P(None, "lon", None, None),
        ),
        out_specs=P("lat", "lon", None),
        check_vma=False,
    )
```

```python
import contextlib

import jax
import jax.numpy as jnp
import numpy as np
from jax import lax
from jax.experimental import pallas as pl
from jax.experimental.pallas import tpu as pltpu
from jax.sharding import PartitionSpec as P

BLOCKS = 2
CONVS = 3
LON_DEVICES = 16
LAT_DEVICES = 8
HALF = 4
CHIPS = 8
COLS = 1024
STRIPS = 16
TILES = 64
ROWS = 4
CH = 128
OWNED = 8
EXT = 70
STEP = 17
F32 = jnp.float32
BF16 = jnp.bfloat16
MESH = pl.DeviceIdType.MESH


def scope(name):
    return contextlib.nullcontext()


def tables():
    total = LON_DEVICES * COLS
    tile, strip = np.meshgrid(np.arange(TILES), np.arange(STRIPS), indexing="ij")
    cell = (strip * TILES + tile).reshape(-1)
    core, chip, part, low = np.meshgrid(
        np.arange(2), np.arange(CHIPS), np.arange(2), np.arange(OWNED), indexing="ij"
    )
    mode = (OWNED * (2 * chip + core) + low).reshape(-1)
    part = part.reshape(-1)
    theta = 2.0 * np.pi / total * ((mode[:, None] * cell[None, :]) % total)
    full = np.where(part[:, None] == 0, np.cos(theta), -np.sin(theta))
    weight = np.where(mode == 0, 1.0, 2.0)[:, None] / total

    def split(table):
        table = table.astype(np.float32)
        hi = table.astype(jnp.bfloat16)
        return hi, (table - hi.astype(np.float32)).astype(jnp.bfloat16)

    forward = np.concatenate(split(full), axis=0)
    inverse = np.concatenate(split((full * weight).T), axis=1)
    phi = 2.0 * np.pi / 16.0 * ((np.arange(16)[:, None] * np.arange(OWNED)[None, :]) % 16)
    turn = np.stack([np.cos(phi), np.sin(phi)], axis=1).astype(np.float32)
    turn = np.broadcast_to(turn[..., None], (16, 2, OWNED, CH)).copy()
    return forward, inverse, turn


def split2(value):
    hi = value.astype(BF16)
    return hi, (value - hi.astype(F32)).astype(BF16)


def kernel(field, cw, cb, sr, si, ft, iv, tw, out,
           f_v, cw_v, cb_v, sr_v, si_v, ft_v, iv_v, tw_v, T, SW, X, H1, H2, H3, ST, S,
           PART, DR, RSEND, RRECV, G, HH, GH,
           in_sem, lon_s, lon_r, lat_s, lat_r, d_s, d_r, rs_s, rs_r, ag_s, ag_r, fw_s, fw_r,
           h_s, h_r, g_s, g_r, gf_s, gf_r,
           RX, RH, lend_s, lend_r, relay_s, relay_r):
    d = lax.axis_index("lon")
    lt = lax.axis_index("lat")
    core = lax.rem(d, 2)
    chip = lax.div(d, 2)
    sibling = chip * 2 + 1 - core
    right = lax.rem(d + 1, LON_DEVICES)
    left = lax.rem(d + LON_DEVICES - 1, LON_DEVICES)
    outer = jnp.where(core == 0, left, right)
    across = lax.rem(lt + HALF, LAT_DEVICES)
    wrap = jnp.where(lt < HALF, HALF - 1 - lt, 3 * HALF - 1 - lt)
    outermost = jnp.logical_or(lax.rem(lt, HALF) == 0, lax.rem(lt, HALF) == HALF - 1)
    has_up = lt > 0
    has_down = lt < LAT_DEVICES - 1

    loads = [
        pltpu.make_async_copy(src, dst, in_sem.at[i])
        for i, (src, dst) in enumerate(
            [(field, f_v), (cw, cw_v), (cb, cb_v), (sr, sr_v), (si, si_v), (ft, ft_v),
             (iv, iv_v), (tw, tw_v)]
        )
    ]
    for load in loads:
        load.start()

    barrier = pltpu.get_barrier_semaphore()
    pl.semaphore_signal(barrier, inc=1, device_id={"lon": sibling}, device_id_type=MESH)
    pl.semaphore_signal(barrier, inc=1, device_id={"lon": outer}, device_id_type=MESH)
    for j in range(1, CHIPS):
        peer = lax.rem(chip + j, CHIPS) * 2 + core
        pl.semaphore_signal(barrier, inc=1, device_id={"lon": peer}, device_id_type=MESH)

    @pl.when(has_up)
    def _():
        pl.semaphore_signal(barrier, inc=1, device_id={"lat": lt - 1}, device_id_type=MESH)

    @pl.when(has_down)
    def _():
        pl.semaphore_signal(barrier, inc=1, device_id={"lat": lt + 1}, device_id_type=MESH)

    @pl.when(outermost)
    def _():
        pl.semaphore_signal(barrier, inc=1, device_id={"lat": across}, device_id_type=MESH)
        pl.semaphore_signal(barrier, inc=1, device_id={"lat": wrap}, device_id_type=MESH)

    @pl.when(jnp.logical_not(has_up))
    def _():
        for b in range(BLOCKS):
            X[b, 0:3] = jnp.zeros((3, EXT, STRIPS, CH), BF16)

    @pl.when(jnp.logical_not(has_down))
    def _():
        for b in range(BLOCKS):
            X[b, 7:10] = jnp.zeros((3, EXT, STRIPS, CH), BF16)

    def permute(first, last):
        for row in range(ROWS):
            for t in range(first, last):
                X[0, 3 + row, t] = S[row, pl.ds(t - 3, STRIPS, stride=TILES), :].astype(BF16)

    with scope("permute_in"):
        loads[0].wait()
        for row in range(ROWS):
            S[row] = f_v[row].astype(F32)
        permute(9, 20)
    with scope("barrier"):
        pl.semaphore_wait(
            barrier, CHIPS + 1 + has_up.astype(jnp.int32) + has_down.astype(jnp.int32)
            + 2 * outermost.astype(jnp.int32)
        )

    def build_weights():
        loads[1].wait()
        loads[2].wait()
        zero = jnp.zeros((CH, CH), BF16)

        def build(i, _):
            b = lax.div(i, CONVS)
            layer = lax.rem(i, CONVS)
            for tap in range(3):
                w0, w1, w2 = (cw_v[b, layer, a, tap] for a in range(3))
                for r, (first, second) in enumerate(((w0, zero), (w1, w0), (w2, w1), (zero, w2))):
                    rows = pl.ds((tap * 4 + r) * CH, CH)
                    T[i, rows, 0:CH] = first
                    T[i, rows, CH:2 * CH] = second
            return 0

        lax.fori_loop(0, BLOCKS * CONVS, build, 0)

        loads[3].wait()
        loads[4].wait()

        def build_spec(i, _):
            b = lax.div(i, OWNED)
            m = lax.rem(i, OWNED)
            wr = sr_v[b, m]
            wi = si_v[b, m]
            SW[i, 0:CH, 0:CH] = wr
            SW[i, 0:CH, CH:2 * CH] = wi
            SW[i, CH:2 * CH, 0:CH] = -wi
            SW[i, CH:2 * CH, CH:2 * CH] = wr
            return 0

        lax.fori_loop(0, BLOCKS * OWNED, build_spec, 0)
        for load in loads[5:7]:
            load.wait()

    loads[7].wait()
    cos = tw_v[d, 0]
    sin = tw_v[d, 1]
    flip = (1 - 2 * core).astype(F32)
    up_mask = has_up.astype(F32)
    down_mask = has_down.astype(F32)
    strip = lax.broadcasted_iota(jnp.int32, (STRIPS, CH), 0)
    sub = lax.rem(lax.broadcasted_iota(jnp.int32, (ROWS * OWNED, 2 * CH), 0), OWNED)

    def convolve(source, target, b, layer, at, to, step, pairs, masks):
        bias = cb_v[layer, b:b + 1, :]
        for pair in range(pairs):
            lhs = jnp.concatenate(
                [source(2 * pair + r, at + tap).reshape(step * STRIPS, CH)
                 for tap in range(3) for r in range(4)], axis=1)
            total = jnp.dot(lhs, T[b * CONVS + layer], preferred_element_type=F32)
            for o in range(2):
                half = 0.5 * (total[:, o * CH:(o + 1) * CH] + bias)
                value = half * jnp.tanh(half) + half
                mask = masks.get(2 * pair + o)
                if mask is not None:
                    value = value * mask
                target[2 * pair + o, pl.ds(to, step)] = value.astype(BF16).reshape(
                    step, STRIPS, CH
                )

    def three(b, s1, s2, s3, step):
        with scope("conv"):
            convolve(lambda r, t: X[b, r, pl.ds(t, step)], H1, b, 0, s1 - 1, s1, step, 4,
                     {0: up_mask, 1: up_mask, 6: down_mask, 7: down_mask})
            convolve(lambda r, t: H1[r, pl.ds(t, step)], H2, b, 1, s2 - 1, s2, step, 3,
                     {0: up_mask, 5: down_mask})
            convolve(lambda r, t: H2[r, pl.ds(t, step)], H3.at[b], b, 2, s3 - 1, s3, step, 2, {})

    def lon_pair(b, first, count):
        rows = pl.ds(first, count)
        return (
            pltpu.make_async_remote_copy(
                src_ref=X.at[b, rows, 64:67], dst_ref=ST.at[b, 0, rows],
                send_sem=lon_s.at[0], recv_sem=lon_r.at[b, 0],
                device_id={"lon": right}, device_id_type=MESH),
            pltpu.make_async_remote_copy(
                src_ref=X.at[b, rows, 3:6], dst_ref=ST.at[b, 1, rows],
                send_sem=lon_s.at[1], recv_sem=lon_r.at[b, 1],
                device_id={"lon": left}, device_id_type=MESH),
        )

    def lon_halo(b, pair, first, count):
        with scope("lonwait"):
            for copy in pair:
                copy.wait()
        for row in range(first, first + count):
            for j in range(3):
                own = X[b, row, 64 + j].astype(F32)
                other = ST[b, 0, row, j].astype(F32)
                tile = jnp.where(strip == 0, pltpu.roll(other, 1, 0), pltpu.roll(own, 1, 0))
                X[b, row, j] = tile.astype(BF16)
                own = X[b, row, 3 + j].astype(F32)
                other = ST[b, 1, row, j].astype(F32)
                tile = jnp.where(
                    strip == STRIPS - 1,
                    pltpu.roll(other, STRIPS - 1, 0), pltpu.roll(own, STRIPS - 1, 0))
                X[b, row, 67 + j] = tile.astype(BF16)

    def both_ways(down, up):
        def start(*piece):
            @pl.when(has_down)
            def _():
                down(*piece).start()

            @pl.when(has_up)
            def _():
                up(*piece).start()

        def wait_recv(*piece):
            @pl.when(has_up)
            def _():
                down(*piece).wait_recv()

            @pl.when(has_down)
            def _():
                up(*piece).wait_recv()

        def wait_send(*piece):
            @pl.when(has_down)
            def _():
                down(*piece).wait_send()

            @pl.when(has_up)
            def _():
                up(*piece).wait_send()

        return start, wait_recv, wait_send

    def halo_ways(source, target, buffer, down_row, up_row, other_side, sends, recvs, base):
        def direct(way, count, first, tiles, slot):
            at = up_row if way else down_row
            to = other_side if way else 0
            window = pl.ds(first, tiles)
            return pltpu.make_async_remote_copy(
                src_ref=source.at[pl.ds(at, count), window],
                dst_ref=target.at[pl.ds(to, count), window],
                send_sem=sends.at[way, slot], recv_sem=recvs.at[way, slot],
                device_id={"lat": lt + 1 - 2 * way}, device_id_type=MESH)

        def lend(way, first, tiles, slot):
            at = (up_row if way else down_row) + 2
            window = pl.ds(first, tiles)
            return pltpu.make_async_remote_copy(
                src_ref=source.at[at, window], dst_ref=buffer.at[window],
                send_sem=lend_s.at[base + slot], recv_sem=lend_r.at[base + slot],
                device_id={"lat": across}, device_id_type=MESH)

        def relay(way, first, tiles, slot):
            to = (other_side if way else 0) + 2
            window = pl.ds(first, tiles)
            return pltpu.make_async_remote_copy(
                src_ref=buffer.at[window], dst_ref=target.at[to, window],
                send_sem=relay_s.at[base + slot], recv_sem=relay_r.at[base + slot],
                device_id={"lat": wrap}, device_id_type=MESH)

        def start(*piece):
            @pl.when(jnp.logical_and(has_down, lt != HALF - 1))
            def _():
                direct(0, 3, *piece).start()

            @pl.when(lt == HALF - 1)
            def _():
                direct(0, 2, *piece).start()
                lend(0, *piece).start()

            @pl.when(jnp.logical_and(has_up, lt != HALF))
            def _():
                direct(1, 3, *piece).start()

            @pl.when(lt == HALF)
            def _():
                direct(1, 2, *piece).start()
                lend(1, *piece).start()

        def forward(*piece):
            @pl.when(lt == LAT_DEVICES - 1)
            def _():
                lend(0, *piece).wait_recv()
                relay(0, *piece).start()

            @pl.when(lt == 0)
            def _():
                lend(1, *piece).wait_recv()
                relay(1, *piece).start()

        def wait_recv(*piece):
            @pl.when(jnp.logical_and(has_up, lt != HALF))
            def _():
                direct(0, 3, *piece).wait_recv()

            @pl.when(lt == HALF)
            def _():
                direct(0, 2, *piece).wait_recv()
                relay(0, *piece).wait_recv()

            @pl.when(jnp.logical_and(has_down, lt != HALF - 1))
            def _():
                direct(1, 3, *piece).wait_recv()

            @pl.when(lt == HALF - 1)
            def _():
                direct(1, 2, *piece).wait_recv()
                relay(1, *piece).wait_recv()

        def wait_send(*piece):
            @pl.when(jnp.logical_and(has_down, lt != HALF - 1))
            def _():
                direct(0, 3, *piece).wait_send()

            @pl.when(lt == HALF - 1)
            def _():
                direct(0, 2, *piece).wait_send()
                lend(0, *piece).wait_send()

            @pl.when(jnp.logical_and(has_up, lt != HALF))
            def _():
                direct(1, 3, *piece).wait_send()

            @pl.when(lt == HALF)
            def _():
                direct(1, 2, *piece).wait_send()
                lend(1, *piece).wait_send()

            @pl.when(lt == LAT_DEVICES - 1)
            def _():
                relay(0, *piece).wait_send()

            @pl.when(lt == 0)
            def _():
                relay(1, *piece).wait_send()

        return start, forward, wait_recv, wait_send

    def g_down():
        return pltpu.make_async_remote_copy(
            src_ref=G.at[0, core, :, :, CH:4 * CH], dst_ref=GH.at[0, core],
            send_sem=g_s.at[0], recv_sem=g_r.at[0],
            device_id={"lat": lt + 1}, device_id_type=MESH)

    def g_up():
        return pltpu.make_async_remote_copy(
            src_ref=G.at[0, core, :, :, 0:3 * CH], dst_ref=GH.at[1, core],
            send_sem=g_s.at[1], recv_sem=g_r.at[1],
            device_id={"lat": lt - 1}, device_id_type=MESH)

    def g_share(side, half):
        return pltpu.make_async_remote_copy(
            src_ref=GH.at[side, half], dst_ref=GH.at[side, half],
            send_sem=gf_s.at[side], recv_sem=gf_r.at[side],
            device_id={"lon": sibling}, device_id_type=MESH)

    def turned(load):
        his = []
        los = []
        for o in range(2):
            for ch in range(CHIPS):
                parts = []
                for value in load(o, ch):
                    re = value[0:8]
                    im = value[8:16]
                    new_re = re * cos - im * sin
                    new_im = re * sin + im * cos
                    if o == 1:
                        new_re = new_re * flip
                        new_im = new_im * flip
                    parts.append(jnp.concatenate([new_re, new_im], axis=0))
                hi, lo = split2(jnp.concatenate(parts, axis=1))
                his.append(hi)
                los.append(lo)
        hi = jnp.concatenate(his, axis=0)
        lo = jnp.concatenate(los, axis=0)
        return jnp.concatenate([hi, hi, lo], axis=0)

    def inverse(c, rhs):
        table = iv_v[pl.ds(c * 256, 256), :]
        lhs = jnp.concatenate([table, table[:, 0:256]], axis=1)
        return jnp.dot(lhs, rhs, preferred_element_type=F32)

    def result(c):
        return pltpu.make_async_copy(
            X.at[BLOCKS, 3:7, pl.ds(3 + 16 * c, 16)], out.at[:, pl.ds(16 * c, 16)], in_sem.at[c])

    x_pieces = ([(9, 11, 0)] + [(20 + 9 * k, 9, k + 1) for k in range(5)]
                + [(65, 5, 6), (0, 9, 7)])
    h_pieces = [(12, 14, 0), (26, 18, 1), (44, 14, 2), (58, 9, 3), (3, 9, 4)]
    x_start, x_forward, x_wait, x_done = halo_ways(
        X.at[0], X.at[0], RX, 4, 3, 7, lat_s, lat_r, 0)
    h_start, h_forward, h_wait, h_done = halo_ways(
        H3.at[0], HH, RH, 1, 0, 3, h_s, h_r, 8)
    g_start, g_wait, g_done = both_ways(g_down, g_up)

    def first_convolutions():
        x_start(*x_pieces[0])
        permute(20, 67)
        for piece in x_pieces[1:6]:
            x_start(*piece)
        permute(3, 9)
        pair = lon_pair(0, 3, 4)
        for copy in pair:
            copy.start()
        lon_halo(0, pair, 3, 4)
        for piece in x_pieces[6:]:
            x_start(*piece)
        with scope("build"):
            build_weights()

        x_forward(*x_pieces[0])
        x_forward(*x_pieces[1])

        def chunk(k, _):
            @pl.when(k < 4)
            def _():
                x_forward(29 + 9 * k, 9, k + 2)

            for p in range(6, 8):
                @pl.when(k == p - 2)
                def _():
                    x_forward(*x_pieces[p])

            @pl.when(k == 6)
            def _():
                h_forward(*h_pieces[0])

            with scope("latwait"):
                @pl.when(k == 0)
                def _():
                    x_wait(*x_pieces[0])

                @pl.when(jnp.logical_and(k > 0, k < 6))
                def _():
                    x_wait(11 + 9 * k, 9, k)

                @pl.when(k == 6)
                def _():
                    x_wait(*x_pieces[6])

                @pl.when(k == 7)
                def _():
                    x_wait(*x_pieces[7])

            for p in range(3):
                @pl.when(k == 2 * p + 2)
                def _():
                    h_start(*h_pieces[p])

            s1 = jnp.where(k < 6, 10 + 9 * k, jnp.where(k == 6, 60, 1))
            shift = jnp.where(k == 7, 1, -1)
            three(0, s1, s1 + shift, s1 + 2 * shift, 9)
            return 0

        lax.fori_loop(0, 8, chunk, 0)

    def second_convolutions():
        with scope("gwait"):
            g_wait()
            for side, present in ((0, has_up), (1, has_down)):
                @pl.when(present)
                def _():
                    g_share(side, core).start()
        with scope("hwait"):
            for piece in h_pieces:
                h_wait(*piece)
        with scope("sharewait"):
            for side, present in ((0, has_up), (1, has_down)):
                @pl.when(present)
                def _():
                    g_share(side, 1 - core).wait_recv()
        rhs = turned(lambda o, ch: [
            GH[side, o, ch, :, l * CH:(l + 1) * CH].astype(F32)
            for side in range(2) for l in range(3)])

        def rows(c, _):
            spectral = inverse(c, rhs)
            tiles = pl.ds(3 + 16 * c, 16)
            for side, present in ((0, has_up), (1, has_down)):
                @pl.when(present)
                def _():
                    for l in range(3):
                        x = X[0, 7 * side + l, tiles].reshape(256, CH).astype(F32)
                        h = HH[3 * side + l, tiles].reshape(256, CH).astype(F32)
                        lanes = slice((3 * side + l) * CH, (3 * side + l + 1) * CH)
                        value = jnp.tanh(x + h + spectral[:, lanes])
                        X[1, 7 * side + l, tiles] = value.astype(BF16).reshape(16, STRIPS, CH)
            return 0

        with scope("halorows"):
            lax.fori_loop(0, 4, rows, 0)
        pair = lon_pair(1, 0, 10)
        for copy in pair:
            copy.start()

        def chunk(c, _):
            @pl.when(c == 2)
            def _():
                lon_halo(1, pair, 0, 10)

            s1 = jnp.where(c == 3, 1, 18 + STEP * c)
            shift = jnp.where(c == 3, 1, -1)
            three(1, s1, s1 + shift, s1 + 2 * shift, STEP)
            return 0

        lax.fori_loop(0, 4, chunk, 0)

    def spectral_part(b):
        with scope("dft"):
            for half in range(2):
                rhs = jnp.concatenate(
                    [H3[b, 2 * half + l, 3:67].reshape(COLS, CH) for l in range(2)], axis=1)
                both = jnp.dot(ft_v[...], rhs, preferred_element_type=F32)
                total = both[0:256] + both[256:512]
                for o in range(2):
                    for ch in range(CHIPS):
                        first = (o * CHIPS + ch) * 16
                        for l in range(2):
                            re = total[first:first + 8, l * CH:(l + 1) * CH]
                            im = total[first + 8:first + 16, l * CH:(l + 1) * CH]
                            new_re = re * cos + im * sin
                            new_im = im * cos - re * sin
                            if o == 1:
                                new_re = new_re * flip
                                new_im = new_im * flip
                            lanes = pl.ds((2 * half + l) * CH, CH)
                            PART[o, ch, 0:8, lanes] = new_re
                            PART[o, ch, 8:16, lanes] = new_im

        if b == 0:
            h_start(*h_pieces[3])
            h_start(*h_pieces[4])
            h_forward(*h_pieces[1])
        swap = pltpu.make_async_remote_copy(
            src_ref=PART.at[1 - core], dst_ref=DR.at[b],
            send_sem=d_s.at[0], recv_sem=d_r.at[b],
            device_id={"lon": sibling}, device_id_type=MESH)
        swap.start()
        with scope("swapwait"):
            swap.wait()
        RSEND[...] = PART[core] + DR[b]

        def scatter(j):
            peer = lax.rem(chip + j, CHIPS)
            return pltpu.make_async_remote_copy(
                src_ref=RSEND.at[peer], dst_ref=RRECV.at[b, j - 1],
                send_sem=rs_s.at[j - 1], recv_sem=rs_r.at[b, j - 1],
                device_id={"lon": peer * 2 + core}, device_id_type=MESH)

        for j in range(1, CHIPS):
            scatter(j).start()
        spectrum = RSEND[chip]
        with scope("rswait"):
            for j in range(1, CHIPS):
                scatter(j).wait()
        for j in range(1, CHIPS):
            spectrum = spectrum + RRECV[b, j - 1]

        if b == 0:
            for piece in h_pieces[2:]:
                h_forward(*piece)
        with scope("mix"):
            lhs = jnp.concatenate(
                [jnp.concatenate([spectrum[0:8, l * CH:(l + 1) * CH],
                                  spectrum[8:16, l * CH:(l + 1) * CH]], axis=1)
                 for l in range(ROWS)], axis=0)
            lhs = jnp.concatenate(split2(lhs), axis=0)
            mixed = jnp.zeros((ROWS * OWNED, 2 * CH), F32)
            for m in range(OWNED):
                both = jnp.dot(lhs, SW[b * OWNED + m], preferred_element_type=F32)
                mixed = jnp.where(sub == m, both[0:32] + both[32:64], mixed)
            for l in range(ROWS):
                G[b, core, chip, :, l * CH:(l + 1) * CH] = jnp.concatenate(
                    [mixed[8 * l:8 * l + 8, 0:CH], mixed[8 * l:8 * l + 8, CH:2 * CH]], axis=0
                ).astype(BF16)

        def gather(j):
            peer = lax.rem(chip + j, CHIPS)
            return pltpu.make_async_remote_copy(
                src_ref=G.at[b, core, chip], dst_ref=G.at[b, core, chip],
                send_sem=ag_s.at[j - 1], recv_sem=ag_r.at[b, j - 1],
                device_id={"lon": peer * 2 + core}, device_id_type=MESH)

        for j in range(1, CHIPS):
            gather(j).start()

        def arrived(j):
            peer = lax.rem(chip + CHIPS - j, CHIPS)
            return pltpu.make_async_remote_copy(
                src_ref=G.at[b, core, peer], dst_ref=G.at[b, core, peer],
                send_sem=ag_s.at[j - 1], recv_sem=ag_r.at[b, j - 1],
                device_id={"lon": peer * 2 + core}, device_id_type=MESH)

        with scope("agwait"):
            for j in range(1, CHIPS):
                arrived(j).wait_recv()
        forward = pltpu.make_async_remote_copy(
            src_ref=G.at[b, core], dst_ref=G.at[b, core],
            send_sem=fw_s.at[0], recv_sem=fw_r.at[b],
            device_id={"lon": sibling}, device_id_type=MESH)
        forward.start()
        if b == 0:
            g_start()
        back = pltpu.make_async_remote_copy(
            src_ref=G.at[b, 1 - core], dst_ref=G.at[b, 1 - core],
            send_sem=fw_s.at[0], recv_sem=fw_r.at[b],
            device_id={"lon": sibling}, device_id_type=MESH)
        with scope("fwwait"):
            back.wait_recv()

        rhs = turned(lambda o, ch: [
            G[b, o, ch, :, l * CH:(l + 1) * CH].astype(F32) for l in range(ROWS)])

        def finish(c, _):
            spectral = inverse(c, rhs)
            for l in range(ROWS):
                x = X[b, 3 + l, pl.ds(3 + 16 * c, 16)].reshape(256, CH).astype(F32)
                h = H3[b, l, pl.ds(3 + 16 * c, 16)].reshape(256, CH).astype(F32)
                value = jnp.tanh(x + h + spectral[:, l * CH:(l + 1) * CH])
                X[b + 1, 3 + l, pl.ds(3 + 16 * c, 16)] = value.astype(BF16).reshape(
                    16, STRIPS, CH)

            if b == BLOCKS - 1:
                result(c).start()

            return 0

        with scope("finish"):
            lax.fori_loop(0, 4, finish, 0)

        for j in range(1, CHIPS):
            gather(j).wait_send()
        forward.wait_send()

    first_convolutions()
    spectral_part(0)
    second_convolutions()
    spectral_part(1)

    for piece in x_pieces:
        x_done(*piece)
    for piece in h_pieces:
        h_done(*piece)
    g_done()
    for side, present in ((0, has_up), (1, has_down)):
        @pl.when(present)
        def _():
            g_share(side, core).wait_send()
    with scope("store"):
        for c in range(4):
            result(c).wait()


def restore(strips):
    return jnp.transpose(strips, (0, 2, 1, 3)).reshape(ROWS, COLS, CH)


def per_device(field, conv_weight, conv_bias, spec_real, spec_imag):
    forward, inverse, turn = tables()
    args = (field, conv_weight, jnp.transpose(conv_bias, (1, 0, 2)), spec_real, spec_imag,
            jnp.asarray(forward), jnp.asarray(inverse), jnp.asarray(turn))
    tile = (STRIPS, CH)
    dma = pltpu.SemaphoreType.DMA
    strips = pl.pallas_call(
        kernel,
        out_shape=jax.ShapeDtypeStruct((ROWS, TILES) + tile, BF16),
        in_specs=[pl.BlockSpec(memory_space=pl.ANY)] * len(args),
        out_specs=pl.BlockSpec(memory_space=pl.ANY),
        scratch_shapes=[pltpu.VMEM(a.shape, a.dtype) for a in args] + [
            pltpu.VMEM((BLOCKS * CONVS, 12 * CH, 2 * CH), BF16),
            pltpu.VMEM((BLOCKS * OWNED, 2 * CH, 2 * CH), BF16),
            pltpu.VMEM((BLOCKS + 1, 10, EXT) + tile, BF16),
            pltpu.VMEM((8, EXT) + tile, BF16),
            pltpu.VMEM((6, EXT) + tile, BF16),
            pltpu.VMEM((BLOCKS, 4, EXT) + tile, BF16),
            pltpu.VMEM((BLOCKS, 2, 10, 3) + tile, BF16),
            pltpu.VMEM((ROWS, COLS, CH), F32),
            pltpu.VMEM((2, CHIPS, 16, ROWS * CH), F32),
            pltpu.VMEM((BLOCKS, CHIPS, 16, ROWS * CH), F32),
            pltpu.VMEM((CHIPS, 16, ROWS * CH), F32),
            pltpu.VMEM((BLOCKS, CHIPS - 1, 16, ROWS * CH), F32),
            pltpu.VMEM((BLOCKS, 2, CHIPS, 16, ROWS * CH), BF16),
            pltpu.VMEM((6, EXT) + tile, BF16),
            pltpu.VMEM((2, 2, CHIPS, 16, 3 * CH), BF16),
            dma((8,)), dma((2,)), dma((BLOCKS, 2)), dma((2, 8)), dma((2, 8)),
            dma((1,)), dma((BLOCKS,)),
            dma((CHIPS - 1,)), dma((BLOCKS, CHIPS - 1)),
            dma((CHIPS - 1,)), dma((BLOCKS, CHIPS - 1)),
            dma((1,)), dma((BLOCKS,)),
            dma((2, 5)), dma((2, 5)), dma((2,)), dma((2,)), dma((2,)), dma((2,)),
            pltpu.VMEM((EXT,) + tile, BF16), pltpu.VMEM((EXT,) + tile, BF16),
            dma((13,)), dma((13,)), dma((13,)), dma((13,)),
        ],
        compiler_params=pltpu.CompilerParams(
            collective_id=0, has_side_effects=True, vmem_limit_bytes=62 * 1024 * 1024),
    )(*args)
    return restore(strips)


def solution(mesh):
    return jax.shard_map(
        per_device,
        mesh=mesh,
        in_specs=(
            P("lat", "lon", None),
            P(),
            P(),
            P(None, "lon", None, None),
            P(None, "lon", None, None),
        ),
        out_specs=P("lat", "lon", None),
        check_vma=False,
    )
```

```python
import contextlib

import jax
import jax.numpy as jnp
import numpy as np
from jax import lax
from jax.experimental import pallas as pl
from jax.experimental.pallas import tpu as pltpu
from jax.sharding import PartitionSpec as P

BLOCKS = 2
CONVS = 3
LON_DEVICES = 16
LAT_DEVICES = 8
HALF = 4
CHIPS = 8
COLS = 1024
STRIPS = 16
TILES = 64
ROWS = 4
CH = 128
OWNED = 8
EXT = 70
STEP = 17
F32 = jnp.float32
BF16 = jnp.bfloat16
MESH = pl.DeviceIdType.MESH


def scope(name):
    return contextlib.nullcontext()


def tables():
    total = LON_DEVICES * COLS
    tile, strip = np.meshgrid(np.arange(TILES), np.arange(STRIPS), indexing="ij")
    cell = (strip * TILES + tile).reshape(-1)
    core, chip, part, low = np.meshgrid(
        np.arange(2), np.arange(CHIPS), np.arange(2), np.arange(OWNED), indexing="ij"
    )
    mode = (OWNED * (2 * chip + core) + low).reshape(-1)
    part = part.reshape(-1)
    theta = 2.0 * np.pi / total * ((mode[:, None] * cell[None, :]) % total)
    full = np.where(part[:, None] == 0, np.cos(theta), -np.sin(theta))
    weight = np.where(mode == 0, 1.0, 2.0)[:, None] / total

    def split(table):
        table = table.astype(np.float32)
        hi = table.astype(jnp.bfloat16)
        return hi, (table - hi.astype(np.float32)).astype(jnp.bfloat16)

    forward = np.concatenate(split(full), axis=0)
    inverse = np.concatenate(split((full * weight).T), axis=1)
    phi = 2.0 * np.pi / 16.0 * ((np.arange(16)[:, None] * np.arange(OWNED)[None, :]) % 16)
    turn = np.stack([np.cos(phi), np.sin(phi)], axis=1).astype(np.float32)
    turn = np.broadcast_to(turn[..., None], (16, 2, OWNED, CH)).copy()
    return forward, inverse, turn


def split2(value):
    hi = value.astype(BF16)
    return hi, (value - hi.astype(F32)).astype(BF16)


def kernel(field, cw, cb, sr, si, ft, iv, tw, out,
           f_v, cw_v, cb_v, sr_v, si_v, ft_v, iv_v, tw_v, T, SW, X, H1, H2, H3, ST, S,
           PART, DR, RSEND, RRECV, G, HH, GH,
           in_sem, lon_s, lon_r, lat_s, lat_r, d_s, d_r, rs_s, rs_r, ag_s, ag_r, fw_s, fw_r,
           h_s, h_r, g_s, g_r, gf_s, gf_r,
           RX, RH, lend_s, lend_r, relay_s, relay_r):
    d = lax.axis_index("lon")
    lt = lax.axis_index("lat")
    core = lax.rem(d, 2)
    chip = lax.div(d, 2)
    sibling = chip * 2 + 1 - core
    right = lax.rem(d + 1, LON_DEVICES)
    left = lax.rem(d + LON_DEVICES - 1, LON_DEVICES)
    outer = jnp.where(core == 0, left, right)
    across = lax.rem(lt + HALF, LAT_DEVICES)
    wrap = jnp.where(lt < HALF, HALF - 1 - lt, 3 * HALF - 1 - lt)
    outermost = jnp.logical_or(lax.rem(lt, HALF) == 0, lax.rem(lt, HALF) == HALF - 1)
    has_up = lt > 0
    has_down = lt < LAT_DEVICES - 1

    loads = [
        pltpu.make_async_copy(src, dst, in_sem.at[i])
        for i, (src, dst) in enumerate(
            [(field, f_v), (cw, cw_v), (cb, cb_v), (sr, sr_v), (si, si_v), (ft, ft_v),
             (iv, iv_v), (tw, tw_v)]
        )
    ]
    for load in loads:
        load.start()

    barrier = pltpu.get_barrier_semaphore()
    pl.semaphore_signal(barrier, inc=1, device_id={"lon": sibling}, device_id_type=MESH)
    pl.semaphore_signal(barrier, inc=1, device_id={"lon": outer}, device_id_type=MESH)
    for j in range(1, CHIPS):
        peer = lax.rem(chip + j, CHIPS) * 2 + core
        pl.semaphore_signal(barrier, inc=1, device_id={"lon": peer}, device_id_type=MESH)

    @pl.when(has_up)
    def _():
        pl.semaphore_signal(barrier, inc=1, device_id={"lat": lt - 1}, device_id_type=MESH)

    @pl.when(has_down)
    def _():
        pl.semaphore_signal(barrier, inc=1, device_id={"lat": lt + 1}, device_id_type=MESH)

    @pl.when(outermost)
    def _():
        pl.semaphore_signal(barrier, inc=1, device_id={"lat": across}, device_id_type=MESH)
        pl.semaphore_signal(barrier, inc=1, device_id={"lat": wrap}, device_id_type=MESH)

    @pl.when(jnp.logical_not(has_up))
    def _():
        for b in range(BLOCKS):
            X[b, 0:3] = jnp.zeros((3, EXT, STRIPS, CH), BF16)

    @pl.when(jnp.logical_not(has_down))
    def _():
        for b in range(BLOCKS):
            X[b, 7:10] = jnp.zeros((3, EXT, STRIPS, CH), BF16)

    def permute(first, last):
        for row in range(ROWS):
            for t in range(first, last):
                X[0, 3 + row, t] = S[row, pl.ds(t - 3, STRIPS, stride=TILES), :].astype(BF16)

    with scope("permute_in"):
        loads[0].wait()
        for row in range(ROWS):
            S[row] = f_v[row].astype(F32)
        permute(9, 20)
    with scope("barrier"):
        pl.semaphore_wait(
            barrier, CHIPS + 1 + has_up.astype(jnp.int32) + has_down.astype(jnp.int32)
            + 2 * outermost.astype(jnp.int32)
        )

    def build_weights():
        loads[1].wait()
        loads[2].wait()
        zero = jnp.zeros((CH, CH), BF16)

        def build(i, _):
            b = lax.div(i, CONVS)
            layer = lax.rem(i, CONVS)
            for tap in range(3):
                w0, w1, w2 = (cw_v[b, layer, a, tap] for a in range(3))
                for r, (first, second) in enumerate(((w0, zero), (w1, w0), (w2, w1), (zero, w2))):
                    rows = pl.ds((tap * 4 + r) * CH, CH)
                    T[i, rows, 0:CH] = first
                    T[i, rows, CH:2 * CH] = second
            return 0

        lax.fori_loop(0, BLOCKS * CONVS, build, 0)

        loads[3].wait()
        loads[4].wait()

        def build_spec(i, _):
            b = lax.div(i, OWNED)
            m = lax.rem(i, OWNED)
            wr = sr_v[b, m]
            wi = si_v[b, m]
            SW[i, 0:CH, 0:CH] = wr
            SW[i, 0:CH, CH:2 * CH] = wi
            SW[i, CH:2 * CH, 0:CH] = -wi
            SW[i, CH:2 * CH, CH:2 * CH] = wr
            return 0

        lax.fori_loop(0, BLOCKS * OWNED, build_spec, 0)
        for load in loads[5:7]:
            load.wait()

    loads[7].wait()
    cos = tw_v[d, 0]
    sin = tw_v[d, 1]
    flip = (1 - 2 * core).astype(F32)
    up_mask = has_up.astype(F32)
    down_mask = has_down.astype(F32)
    strip = lax.broadcasted_iota(jnp.int32, (STRIPS, CH), 0)
    sub = lax.rem(lax.broadcasted_iota(jnp.int32, (ROWS * OWNED, 2 * CH), 0), OWNED)

    def convolve(source, target, b, layer, at, to, step, pairs, masks):
        bias = cb_v[layer, b:b + 1, :]
        for pair in range(pairs):
            lhs = jnp.concatenate(
                [source(2 * pair + r, at + tap).reshape(step * STRIPS, CH)
                 for tap in range(3) for r in range(4)], axis=1)
            total = jnp.dot(lhs, T[b * CONVS + layer], preferred_element_type=F32)
            for o in range(2):
                half = 0.5 * (total[:, o * CH:(o + 1) * CH] + bias)
                value = half * jnp.tanh(half) + half
                mask = masks.get(2 * pair + o)
                if mask is not None:
                    value = value * mask
                target[2 * pair + o, pl.ds(to, step)] = value.astype(BF16).reshape(
                    step, STRIPS, CH
                )

    def three(b, s1, s2, s3, step):
        with scope("conv"):
            convolve(lambda r, t: X[b, r, pl.ds(t, step)], H1, b, 0, s1 - 1, s1, step, 4,
                     {0: up_mask, 1: up_mask, 6: down_mask, 7: down_mask})
            convolve(lambda r, t: H1[r, pl.ds(t, step)], H2, b, 1, s2 - 1, s2, step, 3,
                     {0: up_mask, 5: down_mask})
            convolve(lambda r, t: H2[r, pl.ds(t, step)], H3.at[b], b, 2, s3 - 1, s3, step, 2, {})

    def lon_pair(b, first, count, slot):
        rows = pl.ds(first, count)
        return (
            pltpu.make_async_remote_copy(
                src_ref=X.at[b, rows, 64:67], dst_ref=ST.at[b, 0, rows],
                send_sem=lon_s.at[slot, 0], recv_sem=lon_r.at[slot, 0],
                device_id={"lon": right}, device_id_type=MESH),
            pltpu.make_async_remote_copy(
                src_ref=X.at[b, rows, 3:6], dst_ref=ST.at[b, 1, rows],
                send_sem=lon_s.at[slot, 1], recv_sem=lon_r.at[slot, 1],
                device_id={"lon": left}, device_id_type=MESH),
        )

    def lon_halo(b, pair, first, count):
        with scope("lonwait"):
            for copy in pair:
                copy.wait()
        for row in range(first, first + count):
            for j in range(3):
                own = X[b, row, 64 + j].astype(F32)
                other = ST[b, 0, row, j].astype(F32)
                tile = jnp.where(strip == 0, pltpu.roll(other, 1, 0), pltpu.roll(own, 1, 0))
                X[b, row, j] = tile.astype(BF16)
                own = X[b, row, 3 + j].astype(F32)
                other = ST[b, 1, row, j].astype(F32)
                tile = jnp.where(
                    strip == STRIPS - 1,
                    pltpu.roll(other, STRIPS - 1, 0), pltpu.roll(own, STRIPS - 1, 0))
                X[b, row, 67 + j] = tile.astype(BF16)

    def both_ways(down, up):
        def start(*piece):
            @pl.when(has_down)
            def _():
                down(*piece).start()

            @pl.when(has_up)
            def _():
                up(*piece).start()

        def wait_recv(*piece):
            @pl.when(has_up)
            def _():
                down(*piece).wait_recv()

            @pl.when(has_down)
            def _():
                up(*piece).wait_recv()

        def wait_send(*piece):
            @pl.when(has_down)
            def _():
                down(*piece).wait_send()

            @pl.when(has_up)
            def _():
                up(*piece).wait_send()

        return start, wait_recv, wait_send

    def halo_ways(source, target, buffer, down_row, up_row, other_side, sends, recvs, base, skip):
        def direct(way, count, first, tiles, slot):
            at = up_row if way else down_row
            to = other_side if way else 0
            window = pl.ds(first, tiles)
            return pltpu.make_async_remote_copy(
                src_ref=source.at[pl.ds(at, count), window],
                dst_ref=target.at[pl.ds(to, count), window],
                send_sem=sends.at[way, slot], recv_sem=recvs.at[way, slot],
                device_id={"lat": lt + 1 - 2 * way}, device_id_type=MESH)

        def lend(way, first, tiles, slot):
            at = (up_row if way else down_row) + 2
            window = pl.ds(first, tiles)
            return pltpu.make_async_remote_copy(
                src_ref=source.at[at, window], dst_ref=buffer.at[window],
                send_sem=lend_s.at[base + slot], recv_sem=lend_r.at[base + slot],
                device_id={"lat": across}, device_id_type=MESH)

        def relay(way, first, tiles, slot):
            to = (other_side if way else 0) + 2
            window = pl.ds(first, tiles)
            return pltpu.make_async_remote_copy(
                src_ref=buffer.at[window], dst_ref=target.at[to, window],
                send_sem=relay_s.at[base + slot], recv_sem=relay_r.at[base + slot],
                device_id={"lat": wrap}, device_id_type=MESH)

        def plain(piece):
            return isinstance(piece[2], int) and piece[2] < skip

        def each(piece, down, down_split, up, up_split):
            if plain(piece):
                pl.when(has_down)(down)
                pl.when(has_up)(up)
                return
            pl.when(jnp.logical_and(has_down, lt != HALF - 1))(down)
            pl.when(lt == HALF - 1)(down_split)
            pl.when(jnp.logical_and(has_up, lt != HALF))(up)
            pl.when(lt == HALF)(up_split)

        def start(*piece):
            def split(way):
                direct(way, 2, *piece).start()
                lend(way, *piece).start()

            each(piece, lambda: direct(0, 3, *piece).start(), lambda: split(0),
                 lambda: direct(1, 3, *piece).start(), lambda: split(1))

        def forward(*piece):
            @pl.when(lt == LAT_DEVICES - 1)
            def _():
                lend(0, *piece).wait_recv()
                relay(0, *piece).start()

            @pl.when(lt == 0)
            def _():
                lend(1, *piece).wait_recv()
                relay(1, *piece).start()

        def wait_recv(*piece):
            def split(way):
                direct(way, 2, *piece).wait_recv()
                relay(way, *piece).wait_recv()

            each(piece, lambda: direct(1, 3, *piece).wait_recv(), lambda: split(1),
                 lambda: direct(0, 3, *piece).wait_recv(), lambda: split(0))

        def wait_send(*piece):
            def split(way):
                direct(way, 2, *piece).wait_send()
                lend(way, *piece).wait_send()

            each(piece, lambda: direct(0, 3, *piece).wait_send(), lambda: split(0),
                 lambda: direct(1, 3, *piece).wait_send(), lambda: split(1))
            if not plain(piece):
                @pl.when(lt == LAT_DEVICES - 1)
                def _():
                    relay(0, *piece).wait_send()

                @pl.when(lt == 0)
                def _():
                    relay(1, *piece).wait_send()

        return start, forward, wait_recv, wait_send

    def g_down():
        return pltpu.make_async_remote_copy(
            src_ref=G.at[0, core, :, :, CH:4 * CH], dst_ref=GH.at[0, core],
            send_sem=g_s.at[0], recv_sem=g_r.at[0],
            device_id={"lat": lt + 1}, device_id_type=MESH)

    def g_up():
        return pltpu.make_async_remote_copy(
            src_ref=G.at[0, core, :, :, 0:3 * CH], dst_ref=GH.at[1, core],
            send_sem=g_s.at[1], recv_sem=g_r.at[1],
            device_id={"lat": lt - 1}, device_id_type=MESH)

    def g_share(side, half):
        return pltpu.make_async_remote_copy(
            src_ref=GH.at[side, half], dst_ref=GH.at[side, half],
            send_sem=gf_s.at[side], recv_sem=gf_r.at[side],
            device_id={"lon": sibling}, device_id_type=MESH)

    def turned(load):
        his = []
        los = []
        for o in range(2):
            for ch in range(CHIPS):
                parts = []
                for value in load(o, ch):
                    re = value[0:8]
                    im = value[8:16]
                    new_re = re * cos - im * sin
                    new_im = re * sin + im * cos
                    if o == 1:
                        new_re = new_re * flip
                        new_im = new_im * flip
                    parts.append(jnp.concatenate([new_re, new_im], axis=0))
                hi, lo = split2(jnp.concatenate(parts, axis=1))
                his.append(hi)
                los.append(lo)
        hi = jnp.concatenate(his, axis=0)
        lo = jnp.concatenate(los, axis=0)
        return jnp.concatenate([hi, hi, lo], axis=0)

    def inverse(c, rhs):
        table = iv_v[pl.ds(c * 256, 256), :]
        lhs = jnp.concatenate([table, table[:, 0:256]], axis=1)
        return jnp.dot(lhs, rhs, preferred_element_type=F32)

    def result(c):
        return pltpu.make_async_copy(
            X.at[BLOCKS, 3:7, pl.ds(3 + 16 * c, 16)], out.at[:, pl.ds(16 * c, 16)], in_sem.at[c])

    x_pieces = ([(9, 11, 0)] + [(20 + 9 * k, 9, k + 1) for k in range(5)]
                + [(65, 5, 6), (0, 9, 7)])
    h_pieces = [(12, 14, 0), (26, 18, 1), (44, 14, 2), (58, 9, 3), (3, 9, 4)]
    x_start, x_forward, x_wait, x_done = halo_ways(
        X.at[0], X.at[0], RX, 4, 3, 7, lat_s, lat_r, 0, 2)
    h_start, h_forward, h_wait, h_done = halo_ways(
        H3.at[0], HH, RH, 1, 0, 3, h_s, h_r, 8, 0)
    g_start, g_wait, g_done = both_ways(g_down, g_up)

    def first_convolutions():
        x_start(*x_pieces[0])
        permute(20, 67)
        for piece in x_pieces[1:6]:
            x_start(*piece)
        permute(3, 9)
        pair = lon_pair(0, 3, 4, 0)
        for copy in pair:
            copy.start()
        lon_halo(0, pair, 3, 4)
        for piece in x_pieces[6:]:
            x_start(*piece)
        with scope("build"):
            build_weights()

        def chunk(k, _):
            @pl.when(k < 4)
            def _():
                x_forward(29 + 9 * k, 9, k + 2)

            for p in range(6, 8):
                @pl.when(k == p - 2)
                def _():
                    x_forward(*x_pieces[p])

            @pl.when(k == 6)
            def _():
                h_forward(*h_pieces[0])

            with scope("latwait"):
                @pl.when(k == 0)
                def _():
                    x_wait(*x_pieces[0])

                @pl.when(k == 1)
                def _():
                    x_wait(*x_pieces[1])

                @pl.when(jnp.logical_and(k > 1, k < 6))
                def _():
                    x_wait(11 + 9 * k, 9, k)

                @pl.when(k == 6)
                def _():
                    x_wait(*x_pieces[6])

                @pl.when(k == 7)
                def _():
                    x_wait(*x_pieces[7])

            for p in range(3):
                @pl.when(k == 2 * p + 2)
                def _():
                    h_start(*h_pieces[p])

            s1 = jnp.where(k < 6, 10 + 9 * k, jnp.where(k == 6, 60, 1))
            shift = jnp.where(k == 7, 1, -1)
            three(0, s1, s1 + shift, s1 + 2 * shift, 9)
            return 0

        lax.fori_loop(0, 8, chunk, 0)

    def second_convolutions():
        own = lon_pair(1, 3, 4, 1)
        for copy in own:
            copy.start()
        with scope("gwait"):
            g_wait()
            for side, present in ((0, has_up), (1, has_down)):
                @pl.when(present)
                def _():
                    g_share(side, core).start()
        with scope("hwait"):
            for piece in h_pieces:
                h_wait(*piece)
        with scope("sharewait"):
            for side, present in ((0, has_up), (1, has_down)):
                @pl.when(present)
                def _():
                    g_share(side, 1 - core).wait_recv()
        rhs = turned(lambda o, ch: [
            GH[side, o, ch, :, l * CH:(l + 1) * CH].astype(F32)
            for side in range(2) for l in range(3)])

        def rows(c, _):
            spectral = inverse(c, rhs)
            tiles = pl.ds(3 + 16 * c, 16)
            for side, present in ((0, has_up), (1, has_down)):
                @pl.when(present)
                def _():
                    for l in range(3):
                        x = X[0, 7 * side + l, tiles].reshape(256, CH).astype(F32)
                        h = HH[3 * side + l, tiles].reshape(256, CH).astype(F32)
                        lanes = slice((3 * side + l) * CH, (3 * side + l + 1) * CH)
                        value = jnp.tanh(x + h + spectral[:, lanes])
                        X[1, 7 * side + l, tiles] = value.astype(BF16).reshape(16, STRIPS, CH)
            return 0

        with scope("halorows"):
            lax.fori_loop(0, 4, rows, 0)
        top = lon_pair(1, 0, 3, 2)
        bottom = lon_pair(1, 7, 3, 3)
        for copy in top + bottom:
            copy.start()

        def chunk(c, _):
            @pl.when(c == 2)
            def _():
                lon_halo(1, own, 3, 4)
                lon_halo(1, top, 0, 3)
                lon_halo(1, bottom, 7, 3)

            s1 = jnp.where(c == 3, 1, 18 + STEP * c)
            shift = jnp.where(c == 3, 1, -1)
            three(1, s1, s1 + shift, s1 + 2 * shift, STEP)
            return 0

        lax.fori_loop(0, 4, chunk, 0)

    def spectral_part(b):
        with scope("dft"):
            for half in range(2):
                rhs = jnp.concatenate(
                    [H3[b, 2 * half + l, 3:67].reshape(COLS, CH) for l in range(2)], axis=1)
                both = jnp.dot(ft_v[...], rhs, preferred_element_type=F32)
                total = both[0:256] + both[256:512]
                for o in range(2):
                    for ch in range(CHIPS):
                        first = (o * CHIPS + ch) * 16
                        for l in range(2):
                            re = total[first:first + 8, l * CH:(l + 1) * CH]
                            im = total[first + 8:first + 16, l * CH:(l + 1) * CH]
                            new_re = re * cos + im * sin
                            new_im = im * cos - re * sin
                            if o == 1:
                                new_re = new_re * flip
                                new_im = new_im * flip
                            lanes = pl.ds((2 * half + l) * CH, CH)
                            PART[o, ch, 0:8, lanes] = new_re
                            PART[o, ch, 8:16, lanes] = new_im

        if b == 0:
            h_start(*h_pieces[3])
            h_start(*h_pieces[4])
            h_forward(*h_pieces[1])
        swap = pltpu.make_async_remote_copy(
            src_ref=PART.at[1 - core], dst_ref=DR.at[b],
            send_sem=d_s.at[0], recv_sem=d_r.at[b],
            device_id={"lon": sibling}, device_id_type=MESH)
        swap.start()
        with scope("swapwait"):
            swap.wait()
        RSEND[...] = PART[core] + DR[b]

        def scatter(j):
            peer = lax.rem(chip + j, CHIPS)
            return pltpu.make_async_remote_copy(
                src_ref=RSEND.at[peer], dst_ref=RRECV.at[b, j - 1],
                send_sem=rs_s.at[j - 1], recv_sem=rs_r.at[b, j - 1],
                device_id={"lon": peer * 2 + core}, device_id_type=MESH)

        for j in range(1, CHIPS):
            scatter(j).start()
        spectrum = RSEND[chip]
        if b == 1:
            for piece in x_pieces:
                x_done(*piece)
            for piece in h_pieces:
                h_done(*piece)
            g_done()
            for side, present in ((0, has_up), (1, has_down)):
                @pl.when(present)
                def _():
                    g_share(side, core).wait_send()
        with scope("rswait"):
            for j in range(1, CHIPS):
                scatter(j).wait()
        for j in range(1, CHIPS):
            spectrum = spectrum + RRECV[b, j - 1]

        if b == 0:
            for piece in h_pieces[2:]:
                h_forward(*piece)
        with scope("mix"):
            lhs = jnp.concatenate(
                [jnp.concatenate([spectrum[0:8, l * CH:(l + 1) * CH],
                                  spectrum[8:16, l * CH:(l + 1) * CH]], axis=1)
                 for l in range(ROWS)], axis=0)
            lhs = jnp.concatenate(split2(lhs), axis=0)
            mixed = jnp.zeros((ROWS * OWNED, 2 * CH), F32)
            for m in range(OWNED):
                both = jnp.dot(lhs, SW[b * OWNED + m], preferred_element_type=F32)
                mixed = jnp.where(sub == m, both[0:32] + both[32:64], mixed)
            for l in range(ROWS):
                G[b, core, chip, :, l * CH:(l + 1) * CH] = jnp.concatenate(
                    [mixed[8 * l:8 * l + 8, 0:CH], mixed[8 * l:8 * l + 8, CH:2 * CH]], axis=0
                ).astype(BF16)

        def gather(j):
            peer = lax.rem(chip + j, CHIPS)
            return pltpu.make_async_remote_copy(
                src_ref=G.at[b, core, chip], dst_ref=G.at[b, core, chip],
                send_sem=ag_s.at[j - 1], recv_sem=ag_r.at[b, j - 1],
                device_id={"lon": peer * 2 + core}, device_id_type=MESH)

        for j in range(1, CHIPS):
            gather(j).start()

        def arrived(j):
            peer = lax.rem(chip + CHIPS - j, CHIPS)
            return pltpu.make_async_remote_copy(
                src_ref=G.at[b, core, peer], dst_ref=G.at[b, core, peer],
                send_sem=ag_s.at[j - 1], recv_sem=ag_r.at[b, j - 1],
                device_id={"lon": peer * 2 + core}, device_id_type=MESH)

        with scope("agwait"):
            for j in range(1, CHIPS):
                arrived(j).wait_recv()
        forward = pltpu.make_async_remote_copy(
            src_ref=G.at[b, core], dst_ref=G.at[b, core],
            send_sem=fw_s.at[0], recv_sem=fw_r.at[b],
            device_id={"lon": sibling}, device_id_type=MESH)
        forward.start()
        if b == 0:
            g_start()
        back = pltpu.make_async_remote_copy(
            src_ref=G.at[b, 1 - core], dst_ref=G.at[b, 1 - core],
            send_sem=fw_s.at[0], recv_sem=fw_r.at[b],
            device_id={"lon": sibling}, device_id_type=MESH)
        with scope("fwwait"):
            back.wait_recv()

        rhs = turned(lambda o, ch: [
            G[b, o, ch, :, l * CH:(l + 1) * CH].astype(F32) for l in range(ROWS)])

        def finish(c, _):
            spectral = inverse(c, rhs)
            for l in range(ROWS):
                x = X[b, 3 + l, pl.ds(3 + 16 * c, 16)].reshape(256, CH).astype(F32)
                h = H3[b, l, pl.ds(3 + 16 * c, 16)].reshape(256, CH).astype(F32)
                value = jnp.tanh(x + h + spectral[:, l * CH:(l + 1) * CH])
                X[b + 1, 3 + l, pl.ds(3 + 16 * c, 16)] = value.astype(BF16).reshape(
                    16, STRIPS, CH)

            if b == BLOCKS - 1:
                result(c).start()

            return 0

        with scope("finish"):
            lax.fori_loop(0, 4, finish, 0)

        for j in range(1, CHIPS):
            gather(j).wait_send()
        forward.wait_send()

    first_convolutions()
    spectral_part(0)
    second_convolutions()
    spectral_part(1)

    with scope("store"):
        for c in range(4):
            result(c).wait()


def restore(strips):
    return jnp.transpose(strips, (0, 2, 1, 3)).reshape(ROWS, COLS, CH)


def per_device(field, conv_weight, conv_bias, spec_real, spec_imag):
    forward, inverse, turn = tables()
    args = (field, conv_weight, jnp.transpose(conv_bias, (1, 0, 2)), spec_real, spec_imag,
            jnp.asarray(forward), jnp.asarray(inverse), jnp.asarray(turn))
    tile = (STRIPS, CH)
    dma = pltpu.SemaphoreType.DMA
    strips = pl.pallas_call(
        kernel,
        out_shape=jax.ShapeDtypeStruct((ROWS, TILES) + tile, BF16),
        in_specs=[pl.BlockSpec(memory_space=pl.ANY)] * len(args),
        out_specs=pl.BlockSpec(memory_space=pl.ANY),
        scratch_shapes=[pltpu.VMEM(a.shape, a.dtype) for a in args] + [
            pltpu.VMEM((BLOCKS * CONVS, 12 * CH, 2 * CH), BF16),
            pltpu.VMEM((BLOCKS * OWNED, 2 * CH, 2 * CH), BF16),
            pltpu.VMEM((BLOCKS + 1, 10, EXT) + tile, BF16),
            pltpu.VMEM((8, EXT) + tile, BF16),
            pltpu.VMEM((6, EXT) + tile, BF16),
            pltpu.VMEM((BLOCKS, 4, EXT) + tile, BF16),
            pltpu.VMEM((BLOCKS, 2, 10, 3) + tile, BF16),
            pltpu.VMEM((ROWS, COLS, CH), F32),
            pltpu.VMEM((2, CHIPS, 16, ROWS * CH), F32),
            pltpu.VMEM((BLOCKS, CHIPS, 16, ROWS * CH), F32),
            pltpu.VMEM((CHIPS, 16, ROWS * CH), F32),
            pltpu.VMEM((BLOCKS, CHIPS - 1, 16, ROWS * CH), F32),
            pltpu.VMEM((BLOCKS, 2, CHIPS, 16, ROWS * CH), BF16),
            pltpu.VMEM((6, EXT) + tile, BF16),
            pltpu.VMEM((2, 2, CHIPS, 16, 3 * CH), BF16),
            dma((8,)), dma((4, 2)), dma((4, 2)), dma((2, 8)), dma((2, 8)),
            dma((1,)), dma((BLOCKS,)),
            dma((CHIPS - 1,)), dma((BLOCKS, CHIPS - 1)),
            dma((CHIPS - 1,)), dma((BLOCKS, CHIPS - 1)),
            dma((1,)), dma((BLOCKS,)),
            dma((2, 5)), dma((2, 5)), dma((2,)), dma((2,)), dma((2,)), dma((2,)),
            pltpu.VMEM((EXT,) + tile, BF16), pltpu.VMEM((EXT,) + tile, BF16),
            dma((13,)), dma((13,)), dma((13,)), dma((13,)),
        ],
        compiler_params=pltpu.CompilerParams(
            collective_id=0, has_side_effects=True, vmem_limit_bytes=62 * 1024 * 1024),
    )(*args)
    return restore(strips)


def solution(mesh):
    return jax.shard_map(
        per_device,
        mesh=mesh,
        in_specs=(
            P("lat", "lon", None),
            P(),
            P(),
            P(None, "lon", None, None),
            P(None, "lon", None, None),
        ),
        out_specs=P("lat", "lon", None),
        check_vma=False,
    )
```

```python
import contextlib

import jax
import jax.numpy as jnp
import numpy as np
from jax import lax
from jax.experimental import pallas as pl
from jax.experimental.pallas import tpu as pltpu
from jax.sharding import PartitionSpec as P

BLOCKS = 2
CONVS = 3
LON_DEVICES = 16
LAT_DEVICES = 8
HALF = 4
CHIPS = 8
COLS = 1024
STRIPS = 16
TILES = 64
ROWS = 4
CH = 128
OWNED = 8
EXT = 70
STEP = 17
PEERS = ((1, 2), (0, 2), (1, 1), (1, 3), (0, 1), (0, 3), (1, 0))
F32 = jnp.float32
BF16 = jnp.bfloat16
MESH = pl.DeviceIdType.MESH


def scope(name):
    return contextlib.nullcontext()


def tables():
    total = LON_DEVICES * COLS
    tile, strip = np.meshgrid(np.arange(TILES), np.arange(STRIPS), indexing="ij")
    cell = (strip * TILES + tile).reshape(-1)
    core, chip, part, low = np.meshgrid(
        np.arange(2), np.arange(CHIPS), np.arange(2), np.arange(OWNED), indexing="ij"
    )
    mode = (OWNED * (2 * chip + core) + low).reshape(-1)
    part = part.reshape(-1)
    theta = 2.0 * np.pi / total * ((mode[:, None] * cell[None, :]) % total)
    full = np.where(part[:, None] == 0, np.cos(theta), -np.sin(theta))
    weight = np.where(mode == 0, 1.0, 2.0)[:, None] / total

    def split(table):
        table = table.astype(np.float32)
        hi = table.astype(jnp.bfloat16)
        return hi, (table - hi.astype(np.float32)).astype(jnp.bfloat16)

    forward = np.concatenate(split(full), axis=0)
    inverse = np.concatenate(split((full * weight).T), axis=1)
    phi = 2.0 * np.pi / 16.0 * ((np.arange(16)[:, None] * np.arange(OWNED)[None, :]) % 16)
    turn = np.stack([np.cos(phi), np.sin(phi)], axis=1).astype(np.float32)
    turn = np.broadcast_to(turn[..., None], (16, 2, OWNED, CH)).copy()
    return forward, inverse, turn


def split2(value):
    hi = value.astype(BF16)
    return hi, (value - hi.astype(F32)).astype(BF16)


def kernel(field, cw, cb, sr, si, ft, iv, tw, out,
           f_v, cw_v, cb_v, sr_v, si_v, ft_v, iv_v, tw_v, T, SW, X, H1, H2, H3, ST, S,
           PART, DR, RSEND, RRECV, G, HH, GH,
           in_sem, lon_s, lon_r, lat_s, lat_r, d_s, d_r, rs_s, rs_r, ag_s, ag_r, fw_s, fw_r,
           h_s, h_r, g_s, g_r, gf_s, gf_r,
           RX, RH, edge_s, edge_r):
    d = lax.axis_index("lon")
    lt = lax.axis_index("lat")
    core = lax.rem(d, 2)
    chip = lax.div(d, 2)
    sibling = chip * 2 + 1 - core
    right = lax.rem(d + 1, LON_DEVICES)
    left = lax.rem(d + LON_DEVICES - 1, LON_DEVICES)
    outer = jnp.where(core == 0, left, right)
    across = lax.rem(lt + HALF, LAT_DEVICES)
    wrap = jnp.where(lt < HALF, HALF - 1 - lt, 3 * HALF - 1 - lt)
    outermost = jnp.logical_or(lax.rem(lt, HALF) == 0, lax.rem(lt, HALF) == HALF - 1)
    has_up = lt > 0
    has_down = lt < LAT_DEVICES - 1

    loads = [
        pltpu.make_async_copy(src, dst, in_sem.at[i])
        for i, (src, dst) in enumerate(
            [(field, f_v), (cw, cw_v), (cb, cb_v), (sr, sr_v), (si, si_v), (ft, ft_v),
             (iv, iv_v), (tw, tw_v)]
        )
    ]
    for load in loads:
        load.start()

    barrier = pltpu.get_barrier_semaphore()
    pl.semaphore_signal(barrier, inc=1, device_id={"lon": sibling}, device_id_type=MESH)
    pl.semaphore_signal(barrier, inc=1, device_id={"lon": outer}, device_id_type=MESH)

    def peer_at(dz, dx):
        z = lax.div(chip, 4)
        return (1 - z if dz else z) * 4 + lax.rem(chip + dx, 4)

    for where in PEERS:
        pl.semaphore_signal(
            barrier, inc=1, device_id={"lon": peer_at(*where) * 2 + core}, device_id_type=MESH)

    @pl.when(has_up)
    def _():
        pl.semaphore_signal(barrier, inc=1, device_id={"lat": lt - 1}, device_id_type=MESH)

    @pl.when(has_down)
    def _():
        pl.semaphore_signal(barrier, inc=1, device_id={"lat": lt + 1}, device_id_type=MESH)

    @pl.when(outermost)
    def _():
        pl.semaphore_signal(barrier, inc=1, device_id={"lat": across}, device_id_type=MESH)
        pl.semaphore_signal(barrier, inc=1, device_id={"lat": wrap}, device_id_type=MESH)

    @pl.when(jnp.logical_not(has_up))
    def _():
        for b in range(BLOCKS):
            X[b, 0:3] = jnp.zeros((3, EXT, STRIPS, CH), BF16)

    @pl.when(jnp.logical_not(has_down))
    def _():
        for b in range(BLOCKS):
            X[b, 7:10] = jnp.zeros((3, EXT, STRIPS, CH), BF16)

    def permute(first, last):
        for row in range(ROWS):
            for t in range(first, last):
                X[0, 3 + row, t] = S[row, pl.ds(t - 3, STRIPS, stride=TILES), :].astype(BF16)

    with scope("permute_in"):
        loads[0].wait()
        for row in range(ROWS):
            S[row] = f_v[row].astype(F32)
        permute(9, 20)
    with scope("barrier"):
        pl.semaphore_wait(
            barrier, CHIPS + 1 + has_up.astype(jnp.int32) + has_down.astype(jnp.int32)
            + 2 * outermost.astype(jnp.int32)
        )

    def build_weights():
        loads[1].wait()
        loads[2].wait()
        zero = jnp.zeros((CH, CH), BF16)

        def build(i, _):
            b = lax.div(i, CONVS)
            layer = lax.rem(i, CONVS)
            for tap in range(3):
                w0, w1, w2 = (cw_v[b, layer, a, tap] for a in range(3))
                for r, (first, second) in enumerate(((w0, zero), (w1, w0), (w2, w1), (zero, w2))):
                    rows = pl.ds((tap * 4 + r) * CH, CH)
                    T[i, rows, 0:CH] = first
                    T[i, rows, CH:2 * CH] = second
            return 0

        lax.fori_loop(0, BLOCKS * CONVS, build, 0)

        loads[3].wait()
        loads[4].wait()

        def build_spec(i, _):
            b = lax.div(i, OWNED)
            m = lax.rem(i, OWNED)
            wr = sr_v[b, m]
            wi = si_v[b, m]
            SW[i, 0:CH, 0:CH] = wr
            SW[i, 0:CH, CH:2 * CH] = wi
            SW[i, CH:2 * CH, 0:CH] = -wi
            SW[i, CH:2 * CH, CH:2 * CH] = wr
            return 0

        lax.fori_loop(0, BLOCKS * OWNED, build_spec, 0)
        for load in loads[5:7]:
            load.wait()

    loads[7].wait()
    cos = tw_v[d, 0]
    sin = tw_v[d, 1]
    flip = (1 - 2 * core).astype(F32)
    up_mask = has_up.astype(F32)
    down_mask = has_down.astype(F32)
    strip = lax.broadcasted_iota(jnp.int32, (STRIPS, CH), 0)
    sub = lax.rem(lax.broadcasted_iota(jnp.int32, (ROWS * OWNED, 2 * CH), 0), OWNED)

    def convolve(source, target, b, layer, starts, step, pairs, masks):
        bias = cb_v[layer, b:b + 1, :]
        size = step * STRIPS
        for pair in range(pairs):
            lhs = jnp.concatenate(
                [jnp.concatenate(
                    [source(2 * pair + r, start - 1 + tap).reshape(size, CH)
                     for start in starts], axis=0)
                 for tap in range(3) for r in range(4)], axis=1)
            total = jnp.dot(lhs, T[b * CONVS + layer], preferred_element_type=F32)
            for o in range(2):
                half = 0.5 * (total[:, o * CH:(o + 1) * CH] + bias)
                value = half * jnp.tanh(half) + half
                mask = masks.get(2 * pair + o)
                if mask is not None:
                    value = value * mask
                value = value.astype(BF16)
                for i, start in enumerate(starts):
                    target[2 * pair + o, pl.ds(start, step)] = value[
                        i * size:(i + 1) * size].reshape(step, STRIPS, CH)

    def three(b, s1, s2, s3, step):
        with scope("conv"):
            convolve(lambda r, t: X[b, r, pl.ds(t, step)], H1, b, 0, s1, step, 4,
                     {0: up_mask, 1: up_mask, 6: down_mask, 7: down_mask})
            convolve(lambda r, t: H1[r, pl.ds(t, step)], H2, b, 1, s2, step, 3,
                     {0: up_mask, 5: down_mask})
            convolve(lambda r, t: H2[r, pl.ds(t, step)], H3.at[b], b, 2, s3, step, 2, {})

    def lon_pair(b, first, count, slot):
        rows = pl.ds(first, count)
        return (
            pltpu.make_async_remote_copy(
                src_ref=X.at[b, rows, 64:67], dst_ref=ST.at[b, 0, rows],
                send_sem=lon_s.at[slot, 0], recv_sem=lon_r.at[slot, 0],
                device_id={"lon": right}, device_id_type=MESH),
            pltpu.make_async_remote_copy(
                src_ref=X.at[b, rows, 3:6], dst_ref=ST.at[b, 1, rows],
                send_sem=lon_s.at[slot, 1], recv_sem=lon_r.at[slot, 1],
                device_id={"lon": left}, device_id_type=MESH),
        )

    def lon_halo(b, pair, first, count):
        with scope("lonwait"):
            for copy in pair:
                copy.wait()
        for row in range(first, first + count):
            for j in range(3):
                own = X[b, row, 64 + j].astype(F32)
                other = ST[b, 0, row, j].astype(F32)
                tile = jnp.where(strip == 0, pltpu.roll(other, 1, 0), pltpu.roll(own, 1, 0))
                X[b, row, j] = tile.astype(BF16)
                own = X[b, row, 3 + j].astype(F32)
                other = ST[b, 1, row, j].astype(F32)
                tile = jnp.where(
                    strip == STRIPS - 1,
                    pltpu.roll(other, STRIPS - 1, 0), pltpu.roll(own, STRIPS - 1, 0))
                X[b, row, 67 + j] = tile.astype(BF16)

    def both_ways(down, up):
        def start(*piece):
            @pl.when(has_down)
            def _():
                down(*piece).start()

            @pl.when(has_up)
            def _():
                up(*piece).start()

        def wait_recv(*piece):
            @pl.when(has_up)
            def _():
                down(*piece).wait_recv()

            @pl.when(has_down)
            def _():
                up(*piece).wait_recv()

        def wait_send(*piece):
            @pl.when(has_down)
            def _():
                down(*piece).wait_send()

            @pl.when(has_up)
            def _():
                up(*piece).wait_send()

        return start, wait_recv, wait_send

    def halo_ways(source, target, buffer, down_row, up_row, other_side, sends, recvs, base, skip):
        def direct(way, count, first, tiles, slot):
            at = up_row if way else down_row
            to = other_side if way else 0
            window = pl.ds(first, tiles)
            return pltpu.make_async_remote_copy(
                src_ref=source.at[pl.ds(at, count), window],
                dst_ref=target.at[pl.ds(to, count), window],
                send_sem=sends.at[way, slot], recv_sem=recvs.at[way, slot],
                device_id={"lat": lt + 1 - 2 * way}, device_id_type=MESH)

        def lend(way, first, tiles, slot):
            at = (up_row if way else down_row) + 2
            window = pl.ds(first, tiles)
            return pltpu.make_async_remote_copy(
                src_ref=source.at[at, window], dst_ref=buffer.at[window],
                send_sem=edge_s.at[base + slot], recv_sem=edge_r.at[base + slot],
                device_id={"lat": across}, device_id_type=MESH)

        def relay(way, first, tiles, slot):
            to = (other_side if way else 0) + 2
            window = pl.ds(first, tiles)
            return pltpu.make_async_remote_copy(
                src_ref=buffer.at[window], dst_ref=target.at[to, window],
                send_sem=edge_s.at[base + slot], recv_sem=edge_r.at[base + slot],
                device_id={"lat": wrap}, device_id_type=MESH)

        def plain(piece):
            return isinstance(piece[2], int) and piece[2] < skip

        def each(piece, down, down_split, up, up_split):
            if plain(piece):
                pl.when(has_down)(down)
                pl.when(has_up)(up)
                return
            pl.when(jnp.logical_and(has_down, lt != HALF - 1))(down)
            pl.when(lt == HALF - 1)(down_split)
            pl.when(jnp.logical_and(has_up, lt != HALF))(up)
            pl.when(lt == HALF)(up_split)

        def start(*piece):
            def split(way):
                direct(way, 2, *piece).start()
                lend(way, *piece).start()

            each(piece, lambda: direct(0, 3, *piece).start(), lambda: split(0),
                 lambda: direct(1, 3, *piece).start(), lambda: split(1))

        def forward(*piece):
            @pl.when(lt == LAT_DEVICES - 1)
            def _():
                lend(0, *piece).wait_recv()
                relay(0, *piece).start()

            @pl.when(lt == 0)
            def _():
                lend(1, *piece).wait_recv()
                relay(1, *piece).start()

        def wait_recv(*piece):
            def split(way):
                direct(way, 2, *piece).wait_recv()
                relay(way, *piece).wait_recv()

            each(piece, lambda: direct(1, 3, *piece).wait_recv(), lambda: split(1),
                 lambda: direct(0, 3, *piece).wait_recv(), lambda: split(0))

        def wait_send(*piece):
            def split(way):
                direct(way, 2, *piece).wait_send()
                lend(way, *piece).wait_send()

            each(piece, lambda: direct(0, 3, *piece).wait_send(), lambda: split(0),
                 lambda: direct(1, 3, *piece).wait_send(), lambda: split(1))
            if not plain(piece):
                @pl.when(lt == LAT_DEVICES - 1)
                def _():
                    relay(0, *piece).wait_send()

                @pl.when(lt == 0)
                def _():
                    relay(1, *piece).wait_send()

        return start, forward, wait_recv, wait_send

    def g_down():
        return pltpu.make_async_remote_copy(
            src_ref=G.at[0, core, :, :, CH:4 * CH], dst_ref=GH.at[0, core],
            send_sem=g_s.at[0], recv_sem=g_r.at[0],
            device_id={"lat": lt + 1}, device_id_type=MESH)

    def g_up():
        return pltpu.make_async_remote_copy(
            src_ref=G.at[0, core, :, :, 0:3 * CH], dst_ref=GH.at[1, core],
            send_sem=g_s.at[1], recv_sem=g_r.at[1],
            device_id={"lat": lt - 1}, device_id_type=MESH)

    def g_share(side, half):
        return pltpu.make_async_remote_copy(
            src_ref=GH.at[side, half], dst_ref=GH.at[side, half],
            send_sem=gf_s.at[side], recv_sem=gf_r.at[side],
            device_id={"lon": sibling}, device_id_type=MESH)

    def turned(load):
        his = []
        los = []
        for o in range(2):
            for ch in range(CHIPS):
                parts = []
                for value in load(o, ch):
                    re = value[0:8]
                    im = value[8:16]
                    new_re = re * cos - im * sin
                    new_im = re * sin + im * cos
                    if o == 1:
                        new_re = new_re * flip
                        new_im = new_im * flip
                    parts.append(jnp.concatenate([new_re, new_im], axis=0))
                hi, lo = split2(jnp.concatenate(parts, axis=1))
                his.append(hi)
                los.append(lo)
        hi = jnp.concatenate(his, axis=0)
        lo = jnp.concatenate(los, axis=0)
        return jnp.concatenate([hi, hi, lo], axis=0)

    def inverse(c, rhs):
        table = iv_v[pl.ds(c * 512, 512), :]
        lhs = jnp.concatenate([table, table[:, 0:256]], axis=1)
        return jnp.dot(lhs, rhs, preferred_element_type=F32)

    def result(c):
        return pltpu.make_async_copy(
            X.at[BLOCKS, 3:7, pl.ds(3 + 32 * c, 32)], out.at[:, pl.ds(32 * c, 32)], in_sem.at[c])

    x_pieces = ([(9, 11, 0)] + [(20 + 9 * k, 9, k + 1) for k in range(5)]
                + [(65, 5, 6), (0, 9, 7)])
    h_pieces = [(12, 14, 0), (26, 18, 1), (44, 14, 2), (58, 9, 3), (3, 9, 4)]
    x_start, x_forward, x_wait, x_done = halo_ways(
        X.at[0], X.at[0], RX, 4, 3, 7, lat_s, lat_r, -2, 2)
    h_start, h_forward, h_wait, h_done = halo_ways(
        H3.at[0], HH, RH, 1, 0, 3, h_s, h_r, 6, 0)
    g_start, g_wait, g_done = both_ways(g_down, g_up)

    def first_convolutions():
        x_start(*x_pieces[0])
        permute(20, 67)
        for piece in x_pieces[1:6]:
            x_start(*piece)
        permute(3, 9)
        pair = lon_pair(0, 3, 4, 0)
        for copy in pair:
            copy.start()
        lon_halo(0, pair, 3, 4)
        for piece in x_pieces[6:]:
            x_start(*piece)
        with scope("build"):
            build_weights()

        def chunk(k, _):
            @pl.when(k < 4)
            def _():
                x_forward(29 + 9 * k, 9, k + 2)

            for p in range(6, 8):
                @pl.when(k == p - 2)
                def _():
                    x_forward(*x_pieces[p])

            @pl.when(k == 6)
            def _():
                h_forward(*h_pieces[0])

            with scope("latwait"):
                @pl.when(k == 0)
                def _():
                    x_wait(*x_pieces[0])

                @pl.when(k == 1)
                def _():
                    x_wait(*x_pieces[1])

                @pl.when(jnp.logical_and(k > 1, k < 6))
                def _():
                    x_wait(11 + 9 * k, 9, k)

                @pl.when(k == 6)
                def _():
                    x_wait(*x_pieces[6])

                @pl.when(k == 7)
                def _():
                    x_wait(*x_pieces[7])

            for p in range(3):
                @pl.when(k == 2 * p + 2)
                def _():
                    h_start(*h_pieces[p])

            s1 = jnp.where(k < 6, 10 + 9 * k, jnp.where(k == 6, 60, 1))
            shift = jnp.where(k == 7, 1, -1)
            three(0, [s1], [s1 + shift], [s1 + 2 * shift], 9)
            return 0

        lax.fori_loop(0, 8, chunk, 0)

    def second_convolutions():
        own = lon_pair(1, 3, 4, 1)
        for copy in own:
            copy.start()
        with scope("gwait"):
            g_wait()
            for side, present in ((0, has_up), (1, has_down)):
                @pl.when(present)
                def _():
                    g_share(side, core).start()
        with scope("hwait"):
            for piece in h_pieces:
                h_wait(*piece)
        with scope("sharewait"):
            for side, present in ((0, has_up), (1, has_down)):
                @pl.when(present)
                def _():
                    g_share(side, 1 - core).wait_recv()
        rhs = turned(lambda o, ch: [
            GH[side, o, ch, :, l * CH:(l + 1) * CH].astype(F32)
            for side in range(2) for l in range(3)])

        def rows(c, _):
            spectral = inverse(c, rhs)
            tiles = pl.ds(3 + 32 * c, 32)
            for side, present in ((0, has_up), (1, has_down)):
                @pl.when(present)
                def _():
                    for l in range(3):
                        x = X[0, 7 * side + l, tiles].reshape(512, CH).astype(F32)
                        h = HH[3 * side + l, tiles].reshape(512, CH).astype(F32)
                        lanes = slice((3 * side + l) * CH, (3 * side + l + 1) * CH)
                        value = jnp.tanh(x + h + spectral[:, lanes])
                        X[1, 7 * side + l, tiles] = value.astype(BF16).reshape(32, STRIPS, CH)
            return 0

        with scope("halorows"):
            lax.fori_loop(0, 2, rows, 0)
        top = lon_pair(1, 0, 3, 2)
        bottom = lon_pair(1, 7, 3, 3)
        for copy in top + bottom:
            copy.start()

        def chunk(c, _):
            @pl.when(c == 1)
            def _():
                lon_halo(1, own, 3, 4)
                lon_halo(1, top, 0, 3)
                lon_halo(1, bottom, 7, 3)

            first = 18 + 34 * c
            second = 35 - 34 * c
            shift = 2 * c - 1
            three(1, [first, second], [first - 1, second + shift],
                  [first - 2, second + 2 * shift], STEP)
            return 0

        lax.fori_loop(0, 2, chunk, 0)

    def spectral_part(b):
        with scope("dft"):
            for half in range(2):
                rhs = jnp.concatenate(
                    [H3[b, 2 * half + l, 3:67].reshape(COLS, CH) for l in range(2)], axis=1)
                both = jnp.dot(ft_v[...], rhs, preferred_element_type=F32)
                total = both[0:256] + both[256:512]
                for o in range(2):
                    for ch in range(CHIPS):
                        first = (o * CHIPS + ch) * 16
                        for l in range(2):
                            re = total[first:first + 8, l * CH:(l + 1) * CH]
                            im = total[first + 8:first + 16, l * CH:(l + 1) * CH]
                            new_re = re * cos + im * sin
                            new_im = im * cos - re * sin
                            if o == 1:
                                new_re = new_re * flip
                                new_im = new_im * flip
                            lanes = pl.ds((2 * half + l) * CH, CH)
                            PART[o, ch, 0:8, lanes] = new_re
                            PART[o, ch, 8:16, lanes] = new_im

        if b == 0:
            h_start(*h_pieces[3])
            h_start(*h_pieces[4])
            h_forward(*h_pieces[1])
        swap = pltpu.make_async_remote_copy(
            src_ref=PART.at[1 - core], dst_ref=DR.at[b],
            send_sem=d_s.at[0], recv_sem=d_r.at[b],
            device_id={"lon": sibling}, device_id_type=MESH)
        swap.start()
        with scope("swapwait"):
            swap.wait()
        RSEND[...] = PART[core] + DR[b]

        def scatter(dz, dx):
            peer = peer_at(dz, dx)
            return pltpu.make_async_remote_copy(
                src_ref=RSEND.at[peer], dst_ref=RRECV.at[b, 4 * dz + dx - 1],
                send_sem=rs_s.at[0], recv_sem=rs_r.at[b],
                device_id={"lon": peer * 2 + core}, device_id_type=MESH)

        for where in PEERS:
            scatter(*where).start()
        spectrum = RSEND[chip]
        if b == 1:
            for piece in x_pieces:
                x_done(*piece)
            for piece in h_pieces:
                h_done(*piece)
            g_done()
            for side, present in ((0, has_up), (1, has_down)):
                @pl.when(present)
                def _():
                    g_share(side, core).wait_send()
        with scope("rswait"):
            pltpu.make_async_remote_copy(
                src_ref=RSEND.at[0:CHIPS - 1], dst_ref=RRECV.at[b],
                send_sem=rs_s.at[0], recv_sem=rs_r.at[b],
                device_id={"lon": sibling}, device_id_type=MESH).wait()
        for j in range(1, CHIPS):
            spectrum = spectrum + RRECV[b, j - 1]

        if b == 0:
            for piece in h_pieces[2:]:
                h_forward(*piece)
        with scope("mix"):
            lhs = jnp.concatenate(
                [jnp.concatenate([spectrum[0:8, l * CH:(l + 1) * CH],
                                  spectrum[8:16, l * CH:(l + 1) * CH]], axis=1)
                 for l in range(ROWS)], axis=0)
            lhs = jnp.concatenate(split2(lhs), axis=0)
            mixed = jnp.zeros((ROWS * OWNED, 2 * CH), F32)
            for m in range(OWNED):
                both = jnp.dot(lhs, SW[b * OWNED + m], preferred_element_type=F32)
                mixed = jnp.where(sub == m, both[0:32] + both[32:64], mixed)
            for l in range(ROWS):
                G[b, core, chip, :, l * CH:(l + 1) * CH] = jnp.concatenate(
                    [mixed[8 * l:8 * l + 8, 0:CH], mixed[8 * l:8 * l + 8, CH:2 * CH]], axis=0
                ).astype(BF16)

        def gather(dz, dx):
            return pltpu.make_async_remote_copy(
                src_ref=G.at[b, core, chip], dst_ref=G.at[b, core, chip],
                send_sem=ag_s.at[0], recv_sem=ag_r.at[b],
                device_id={"lon": peer_at(dz, dx) * 2 + core}, device_id_type=MESH)

        for where in PEERS:
            gather(*where).start()

        gathered = pltpu.make_async_remote_copy(
            src_ref=G.at[b, core, 0:CHIPS - 1], dst_ref=G.at[b, core, 0:CHIPS - 1],
            send_sem=ag_s.at[0], recv_sem=ag_r.at[b],
            device_id={"lon": sibling}, device_id_type=MESH)
        with scope("agwait"):
            gathered.wait_recv()
        forward = pltpu.make_async_remote_copy(
            src_ref=G.at[b, core], dst_ref=G.at[b, core],
            send_sem=fw_s.at[0], recv_sem=fw_r.at[b],
            device_id={"lon": sibling}, device_id_type=MESH)
        forward.start()
        if b == 0:
            g_start()
        back = pltpu.make_async_remote_copy(
            src_ref=G.at[b, 1 - core], dst_ref=G.at[b, 1 - core],
            send_sem=fw_s.at[0], recv_sem=fw_r.at[b],
            device_id={"lon": sibling}, device_id_type=MESH)
        with scope("fwwait"):
            back.wait_recv()

        rhs = turned(lambda o, ch: [
            G[b, o, ch, :, l * CH:(l + 1) * CH].astype(F32) for l in range(ROWS)])

        def finish(c, _):
            spectral = inverse(c, rhs)
            for l in range(ROWS):
                x = X[b, 3 + l, pl.ds(3 + 32 * c, 32)].reshape(512, CH).astype(F32)
                h = H3[b, l, pl.ds(3 + 32 * c, 32)].reshape(512, CH).astype(F32)
                value = jnp.tanh(x + h + spectral[:, l * CH:(l + 1) * CH])
                X[b + 1, 3 + l, pl.ds(3 + 32 * c, 32)] = value.astype(BF16).reshape(
                    32, STRIPS, CH)

            if b == BLOCKS - 1:
                result(c).start()

            return 0

        with scope("finish"):
            lax.fori_loop(0, 2, finish, 0)

        gathered.wait_send()
        forward.wait_send()

    first_convolutions()
    spectral_part(0)
    second_convolutions()
    spectral_part(1)

    with scope("store"):
        for c in range(2):
            result(c).wait()


def restore(strips):
    return jnp.transpose(strips, (0, 2, 1, 3)).reshape(ROWS, COLS, CH)


def per_device(field, conv_weight, conv_bias, spec_real, spec_imag):
    forward, inverse, turn = tables()
    args = (field, conv_weight, jnp.transpose(conv_bias, (1, 0, 2)), spec_real, spec_imag,
            jnp.asarray(forward), jnp.asarray(inverse), jnp.asarray(turn))
    tile = (STRIPS, CH)
    dma = pltpu.SemaphoreType.DMA
    strips = pl.pallas_call(
        kernel,
        out_shape=jax.ShapeDtypeStruct((ROWS, TILES) + tile, BF16),
        in_specs=[pl.BlockSpec(memory_space=pl.ANY)] * len(args),
        out_specs=pl.BlockSpec(memory_space=pl.ANY),
        scratch_shapes=[pltpu.VMEM(a.shape, a.dtype) for a in args] + [
            pltpu.VMEM((BLOCKS * CONVS, 12 * CH, 2 * CH), BF16),
            pltpu.VMEM((BLOCKS * OWNED, 2 * CH, 2 * CH), BF16),
            pltpu.VMEM((BLOCKS + 1, 10, EXT) + tile, BF16),
            pltpu.VMEM((8, EXT) + tile, BF16),
            pltpu.VMEM((6, EXT) + tile, BF16),
            pltpu.VMEM((BLOCKS, 4, EXT) + tile, BF16),
            pltpu.VMEM((BLOCKS, 2, 10, 3) + tile, BF16),
            pltpu.VMEM((ROWS, COLS, CH), F32),
            pltpu.VMEM((2, CHIPS, 16, ROWS * CH), F32),
            pltpu.VMEM((BLOCKS, CHIPS, 16, ROWS * CH), F32),
            pltpu.VMEM((CHIPS, 16, ROWS * CH), F32),
            pltpu.VMEM((BLOCKS, CHIPS - 1, 16, ROWS * CH), F32),
            pltpu.VMEM((BLOCKS, 2, CHIPS, 16, ROWS * CH), BF16),
            pltpu.VMEM((6, EXT) + tile, BF16),
            pltpu.VMEM((2, 2, CHIPS, 16, 3 * CH), BF16),
            dma((8,)), dma((4, 2)), dma((4, 2)), dma((2, 8)), dma((2, 8)),
            dma((1,)), dma((BLOCKS,)),
            dma((1,)), dma((BLOCKS,)), dma((1,)), dma((BLOCKS,)),
            dma((1,)), dma((BLOCKS,)),
            dma((2, 5)), dma((2, 5)), dma((2,)), dma((2,)), dma((2,)), dma((2,)),
            pltpu.VMEM((EXT,) + tile, BF16), pltpu.VMEM((EXT,) + tile, BF16),
            dma((11,)), dma((11,)),
        ],
        compiler_params=pltpu.CompilerParams(
            collective_id=0, has_side_effects=True, vmem_limit_bytes=62 * 1024 * 1024),
    )(*args)
    return restore(strips)


def solution(mesh):
    return jax.shard_map(
        per_device,
        mesh=mesh,
        in_specs=(
            P("lat", "lon", None),
            P(),
            P(),
            P(None, "lon", None, None),
            P(None, "lon", None, None),
        ),
        out_specs=P("lat", "lon", None),
        check_vma=False,
    )
```

```python
import contextlib

import jax
import jax.numpy as jnp
import numpy as np
from jax import lax
from jax.experimental import pallas as pl
from jax.experimental.pallas import tpu as pltpu
from jax.sharding import PartitionSpec as P

BLOCKS = 2
CONVS = 3
LON_DEVICES = 16
LAT_DEVICES = 8
HALF = 4
CHIPS = 8
COLS = 1024
STRIPS = 16
TILES = 64
ROWS = 4
CH = 128
OWNED = 8
EXT = 70
STEP = 17
PEERS = ((1, 2), (0, 2), (1, 1), (1, 3), (0, 1), (0, 3), (1, 0))
F32 = jnp.float32
BF16 = jnp.bfloat16
MESH = pl.DeviceIdType.MESH


def scope(name):
    return contextlib.nullcontext()


def tables():
    total = LON_DEVICES * COLS
    tile, strip = np.meshgrid(np.arange(TILES), np.arange(STRIPS), indexing="ij")
    cell = (strip * TILES + tile).reshape(-1)
    core, chip, part, low = np.meshgrid(
        np.arange(2), np.arange(CHIPS), np.arange(2), np.arange(OWNED), indexing="ij"
    )
    mode = (OWNED * (2 * chip + core) + low).reshape(-1)
    part = part.reshape(-1)
    theta = 2.0 * np.pi / total * ((mode[:, None] * cell[None, :]) % total)
    full = np.where(part[:, None] == 0, np.cos(theta), -np.sin(theta))
    weight = np.where(mode == 0, 1.0, 2.0)[:, None] / total

    def split(table):
        table = table.astype(np.float32)
        hi = table.astype(jnp.bfloat16)
        return hi, (table - hi.astype(np.float32)).astype(jnp.bfloat16)

    forward = np.concatenate(split(full), axis=0)
    inverse = np.concatenate(split((full * weight).T), axis=1)
    phi = 2.0 * np.pi / 16.0 * ((np.arange(16)[:, None] * np.arange(OWNED)[None, :]) % 16)
    turn = np.stack([np.cos(phi), np.sin(phi)], axis=1).astype(np.float32)
    turn = np.broadcast_to(turn[..., None], (16, 2, OWNED, CH)).copy()
    return forward, inverse, turn


def split2(value):
    hi = value.astype(BF16)
    return hi, (value - hi.astype(F32)).astype(BF16)


def kernel(field, cw, cb, sr, si, ft, iv, tw, out,
           f_v, cw_v, cb_v, sr_v, si_v, ft_v, iv_v, tw_v, T, SW, X, H1, H2, H3, ST, S,
           PART, DR, RSEND, RRECV, G, HH, GH,
           in_sem, lon_s, lon_r, lat_s, lat_r, d_s, d_r, rs_s, rs_r, ag_s, ag_r, fw_s, fw_r,
           h_s, h_r, g_s, g_r, gf_s, gf_r,
           RX, RH, edge_s, edge_r):
    d = lax.axis_index("lon")
    lt = lax.axis_index("lat")
    core = lax.rem(d, 2)
    chip = lax.div(d, 2)
    sibling = chip * 2 + 1 - core
    right = lax.rem(d + 1, LON_DEVICES)
    left = lax.rem(d + LON_DEVICES - 1, LON_DEVICES)
    outer = jnp.where(core == 0, left, right)
    across = lax.rem(lt + HALF, LAT_DEVICES)
    wrap = jnp.where(lt < HALF, HALF - 1 - lt, 3 * HALF - 1 - lt)
    outermost = jnp.logical_or(lax.rem(lt, HALF) == 0, lax.rem(lt, HALF) == HALF - 1)
    has_up = lt > 0
    has_down = lt < LAT_DEVICES - 1

    loads = [
        pltpu.make_async_copy(src, dst, in_sem.at[i])
        for i, (src, dst) in enumerate(
            [(field, f_v), (cw, cw_v), (cb, cb_v), (sr, sr_v), (si, si_v), (ft, ft_v),
             (iv, iv_v), (tw, tw_v)]
        )
    ]
    barrier = pltpu.get_barrier_semaphore()
    pl.semaphore_signal(barrier, inc=1, device_id={"lon": sibling}, device_id_type=MESH)
    pl.semaphore_signal(barrier, inc=1, device_id={"lon": outer}, device_id_type=MESH)

    def peer_at(dz, dx):
        z = lax.div(chip, 4)
        return (1 - z if dz else z) * 4 + lax.rem(chip + dx, 4)

    for where in PEERS:
        pl.semaphore_signal(
            barrier, inc=1, device_id={"lon": peer_at(*where) * 2 + core}, device_id_type=MESH)

    @pl.when(has_up)
    def _():
        pl.semaphore_signal(barrier, inc=1, device_id={"lat": lt - 1}, device_id_type=MESH)

    @pl.when(has_down)
    def _():
        pl.semaphore_signal(barrier, inc=1, device_id={"lat": lt + 1}, device_id_type=MESH)

    @pl.when(outermost)
    def _():
        pl.semaphore_signal(barrier, inc=1, device_id={"lat": across}, device_id_type=MESH)
        pl.semaphore_signal(barrier, inc=1, device_id={"lat": wrap}, device_id_type=MESH)

    for load in loads:
        load.start()

    @pl.when(jnp.logical_not(has_up))
    def _():
        for b in range(BLOCKS):
            X[b, 0:3] = jnp.zeros((3, EXT, STRIPS, CH), BF16)

    @pl.when(jnp.logical_not(has_down))
    def _():
        for b in range(BLOCKS):
            X[b, 7:10] = jnp.zeros((3, EXT, STRIPS, CH), BF16)

    def permute(first, last):
        for row in range(ROWS):
            for t in range(first, last):
                X[0, 3 + row, t] = S[row, pl.ds(t - 3, STRIPS, stride=TILES), :].astype(BF16)

    with scope("permute_in"):
        loads[0].wait()
        for row in range(ROWS):
            S[row] = f_v[row].astype(F32)
        permute(9, 20)
    with scope("barrier"):
        pl.semaphore_wait(
            barrier, CHIPS + 1 + has_up.astype(jnp.int32) + has_down.astype(jnp.int32)
            + 2 * outermost.astype(jnp.int32)
        )

    def build_weights():
        loads[1].wait()
        loads[2].wait()
        zero = jnp.zeros((CH, CH), BF16)

        def build(i, _):
            b = lax.div(i, CONVS)
            layer = lax.rem(i, CONVS)
            for tap in range(3):
                w0, w1, w2 = (cw_v[b, layer, a, tap] for a in range(3))
                for r, (first, second) in enumerate(((w0, zero), (w1, w0), (w2, w1), (zero, w2))):
                    rows = pl.ds((tap * 4 + r) * CH, CH)
                    T[i, rows, 0:CH] = first
                    T[i, rows, CH:2 * CH] = second
            return 0

        lax.fori_loop(0, BLOCKS * CONVS, build, 0)

        loads[3].wait()
        loads[4].wait()

        def build_spec(i, _):
            b = lax.div(i, OWNED)
            m = lax.rem(i, OWNED)
            wr = sr_v[b, m]
            wi = si_v[b, m]
            SW[i, 0:CH, 0:CH] = wr
            SW[i, 0:CH, CH:2 * CH] = wi
            SW[i, CH:2 * CH, 0:CH] = -wi
            SW[i, CH:2 * CH, CH:2 * CH] = wr
            return 0

        lax.fori_loop(0, BLOCKS * OWNED, build_spec, 0)
        for load in loads[5:7]:
            load.wait()

    loads[7].wait()
    cos = tw_v[d, 0]
    sin = tw_v[d, 1]
    flip = (1 - 2 * core).astype(F32)
    up_mask = has_up.astype(F32)
    down_mask = has_down.astype(F32)
    strip = lax.broadcasted_iota(jnp.int32, (STRIPS, CH), 0)
    sub = lax.rem(lax.broadcasted_iota(jnp.int32, (ROWS * OWNED, 2 * CH), 0), OWNED)

    def convolve(source, target, b, layer, starts, step, pairs, masks):
        bias = cb_v[layer, b:b + 1, :]
        size = step * STRIPS
        for pair in range(pairs):
            lhs = jnp.concatenate(
                [jnp.concatenate(
                    [source(2 * pair + r, start - 1 + tap).reshape(size, CH)
                     for start in starts], axis=0)
                 for tap in range(3) for r in range(4)], axis=1)
            total = jnp.dot(lhs, T[b * CONVS + layer], preferred_element_type=F32)
            for o in range(2):
                half = 0.5 * (total[:, o * CH:(o + 1) * CH] + bias)
                value = half * jnp.tanh(half) + half
                mask = masks.get(2 * pair + o)
                if mask is not None:
                    value = value * mask
                value = value.astype(BF16)
                for i, start in enumerate(starts):
                    target[2 * pair + o, pl.ds(start, step)] = value[
                        i * size:(i + 1) * size].reshape(step, STRIPS, CH)

    def three(b, s1, s2, s3, step):
        with scope("conv"):
            convolve(lambda r, t: X[b, r, pl.ds(t, step)], H1, b, 0, s1, step, 4,
                     {0: up_mask, 1: up_mask, 6: down_mask, 7: down_mask})
            convolve(lambda r, t: H1[r, pl.ds(t, step)], H2, b, 1, s2, step, 3,
                     {0: up_mask, 5: down_mask})
            convolve(lambda r, t: H2[r, pl.ds(t, step)], H3.at[b], b, 2, s3, step, 2, {})

    def lon_pair(b, first, count, slot):
        rows = pl.ds(first, count)
        return (
            pltpu.make_async_remote_copy(
                src_ref=X.at[b, rows, 64:67], dst_ref=ST.at[b, 0, rows],
                send_sem=lon_s.at[slot, 0], recv_sem=lon_r.at[slot, 0],
                device_id={"lon": right}, device_id_type=MESH),
            pltpu.make_async_remote_copy(
                src_ref=X.at[b, rows, 3:6], dst_ref=ST.at[b, 1, rows],
                send_sem=lon_s.at[slot, 1], recv_sem=lon_r.at[slot, 1],
                device_id={"lon": left}, device_id_type=MESH),
        )

    def lon_halo(b, pair, first, count):
        with scope("lonwait"):
            for copy in pair:
                copy.wait()
        for row in range(first, first + count):
            for j in range(3):
                own = X[b, row, 64 + j].astype(F32)
                other = ST[b, 0, row, j].astype(F32)
                tile = jnp.where(strip == 0, pltpu.roll(other, 1, 0), pltpu.roll(own, 1, 0))
                X[b, row, j] = tile.astype(BF16)
                own = X[b, row, 3 + j].astype(F32)
                other = ST[b, 1, row, j].astype(F32)
                tile = jnp.where(
                    strip == STRIPS - 1,
                    pltpu.roll(other, STRIPS - 1, 0), pltpu.roll(own, STRIPS - 1, 0))
                X[b, row, 67 + j] = tile.astype(BF16)

    def both_ways(down, up):
        def start(*piece):
            @pl.when(has_down)
            def _():
                down(*piece).start()

            @pl.when(has_up)
            def _():
                up(*piece).start()

        def wait_recv(*piece):
            @pl.when(has_up)
            def _():
                down(*piece).wait_recv()

            @pl.when(has_down)
            def _():
                up(*piece).wait_recv()

        def wait_send(*piece):
            @pl.when(has_down)
            def _():
                down(*piece).wait_send()

            @pl.when(has_up)
            def _():
                up(*piece).wait_send()

        return start, wait_recv, wait_send

    def halo_ways(source, target, buffer, down_row, up_row, other_side, sends, recvs, base, skip):
        def direct(way, count, first, tiles, slot):
            at = up_row if way else down_row
            to = other_side if way else 0
            window = pl.ds(first, tiles)
            return pltpu.make_async_remote_copy(
                src_ref=source.at[pl.ds(at, count), window],
                dst_ref=target.at[pl.ds(to, count), window],
                send_sem=sends.at[way, slot], recv_sem=recvs.at[way, slot],
                device_id={"lat": lt + 1 - 2 * way}, device_id_type=MESH)

        def lend(way, first, tiles, slot):
            at = (up_row if way else down_row) + 2
            window = pl.ds(first, tiles)
            return pltpu.make_async_remote_copy(
                src_ref=source.at[at, window], dst_ref=buffer.at[window],
                send_sem=edge_s.at[base + slot], recv_sem=edge_r.at[base + slot],
                device_id={"lat": across}, device_id_type=MESH)

        def relay(way, first, tiles, slot):
            to = (other_side if way else 0) + 2
            window = pl.ds(first, tiles)
            return pltpu.make_async_remote_copy(
                src_ref=buffer.at[window], dst_ref=target.at[to, window],
                send_sem=edge_s.at[base + slot], recv_sem=edge_r.at[base + slot],
                device_id={"lat": wrap}, device_id_type=MESH)

        def plain(piece):
            return isinstance(piece[2], int) and piece[2] < skip

        def each(piece, down, down_split, up, up_split):
            if plain(piece):
                pl.when(has_down)(down)
                pl.when(has_up)(up)
                return
            pl.when(jnp.logical_and(has_down, lt != HALF - 1))(down)
            pl.when(lt == HALF - 1)(down_split)
            pl.when(jnp.logical_and(has_up, lt != HALF))(up)
            pl.when(lt == HALF)(up_split)

        def start(*piece):
            def split(way):
                direct(way, 2, *piece).start()
                lend(way, *piece).start()

            each(piece, lambda: direct(0, 3, *piece).start(), lambda: split(0),
                 lambda: direct(1, 3, *piece).start(), lambda: split(1))

        def forward(*piece):
            @pl.when(lt == LAT_DEVICES - 1)
            def _():
                lend(0, *piece).wait_recv()
                relay(0, *piece).start()

            @pl.when(lt == 0)
            def _():
                lend(1, *piece).wait_recv()
                relay(1, *piece).start()

        def wait_recv(*piece):
            def split(way):
                direct(way, 2, *piece).wait_recv()
                relay(way, *piece).wait_recv()

            each(piece, lambda: direct(1, 3, *piece).wait_recv(), lambda: split(1),
                 lambda: direct(0, 3, *piece).wait_recv(), lambda: split(0))

        def wait_send(*piece):
            def split(way):
                direct(way, 2, *piece).wait_send()
                lend(way, *piece).wait_send()

            each(piece, lambda: direct(0, 3, *piece).wait_send(), lambda: split(0),
                 lambda: direct(1, 3, *piece).wait_send(), lambda: split(1))
            if not plain(piece):
                @pl.when(lt == LAT_DEVICES - 1)
                def _():
                    relay(0, *piece).wait_send()

                @pl.when(lt == 0)
                def _():
                    relay(1, *piece).wait_send()

        return start, forward, wait_recv, wait_send

    def g_down():
        return pltpu.make_async_remote_copy(
            src_ref=G.at[0, core, :, :, CH:4 * CH], dst_ref=GH.at[0, core],
            send_sem=g_s.at[0], recv_sem=g_r.at[0],
            device_id={"lat": lt + 1}, device_id_type=MESH)

    def g_up():
        return pltpu.make_async_remote_copy(
            src_ref=G.at[0, core, :, :, 0:3 * CH], dst_ref=GH.at[1, core],
            send_sem=g_s.at[1], recv_sem=g_r.at[1],
            device_id={"lat": lt - 1}, device_id_type=MESH)

    def g_share(side, half):
        return pltpu.make_async_remote_copy(
            src_ref=GH.at[side, half], dst_ref=GH.at[side, half],
            send_sem=gf_s.at[side], recv_sem=gf_r.at[side],
            device_id={"lon": sibling}, device_id_type=MESH)

    def turned(load):
        his = []
        los = []
        for o in range(2):
            for ch in range(CHIPS):
                parts = []
                for value in load(o, ch):
                    re = value[0:8]
                    im = value[8:16]
                    new_re = re * cos - im * sin
                    new_im = re * sin + im * cos
                    if o == 1:
                        new_re = new_re * flip
                        new_im = new_im * flip
                    parts.append(jnp.concatenate([new_re, new_im], axis=0))
                hi, lo = split2(jnp.concatenate(parts, axis=1))
                his.append(hi)
                los.append(lo)
        hi = jnp.concatenate(his, axis=0)
        lo = jnp.concatenate(los, axis=0)
        return jnp.concatenate([hi, hi, lo], axis=0)

    def inverse(c, rhs):
        table = iv_v[pl.ds(c * 512, 512), :]
        lhs = jnp.concatenate([table, table[:, 0:256]], axis=1)
        return jnp.dot(lhs, rhs, preferred_element_type=F32)

    def result(c, l):
        return pltpu.make_async_copy(
            X.at[BLOCKS, 3 + l, pl.ds(3 + 32 * c, 32)], out.at[l, pl.ds(32 * c, 32)],
            in_sem.at[4 * c + l])

    x_pieces = ([(9, 11, 0)] + [(20 + 9 * k, 9, k + 1) for k in range(5)]
                + [(65, 5, 6), (0, 9, 7)])
    h_pieces = [(12, 14, 0), (26, 18, 1), (44, 14, 2), (58, 9, 3), (3, 9, 4)]
    x_start, x_forward, x_wait, x_done = halo_ways(
        X.at[0], X.at[0], RX, 4, 3, 7, lat_s, lat_r, -2, 2)
    h_start, h_forward, h_wait, h_done = halo_ways(
        H3.at[0], HH, RH, 1, 0, 3, h_s, h_r, 6, 0)
    g_start, g_wait, g_done = both_ways(g_down, g_up)

    def first_convolutions():
        x_start(*x_pieces[0])
        permute(20, 67)
        for piece in x_pieces[1:6]:
            x_start(*piece)
        permute(3, 9)
        pair = lon_pair(0, 3, 4, 0)
        for copy in pair:
            copy.start()
        lon_halo(0, pair, 3, 4)
        for piece in x_pieces[6:]:
            x_start(*piece)
        with scope("build"):
            build_weights()

        def chunk(k, _):
            @pl.when(k < 4)
            def _():
                x_forward(29 + 9 * k, 9, k + 2)

            for p in range(6, 8):
                @pl.when(k == p - 2)
                def _():
                    x_forward(*x_pieces[p])

            @pl.when(k == 6)
            def _():
                h_forward(*h_pieces[0])

            with scope("latwait"):
                @pl.when(k == 0)
                def _():
                    x_wait(*x_pieces[0])

                @pl.when(k == 1)
                def _():
                    x_wait(*x_pieces[1])

                @pl.when(jnp.logical_and(k > 1, k < 6))
                def _():
                    x_wait(11 + 9 * k, 9, k)

                @pl.when(k == 6)
                def _():
                    x_wait(*x_pieces[6])

                @pl.when(k == 7)
                def _():
                    x_wait(*x_pieces[7])

            for p in range(3):
                @pl.when(k == 2 * p + 2)
                def _():
                    h_start(*h_pieces[p])

            s1 = jnp.where(k < 6, 10 + 9 * k, jnp.where(k == 6, 60, 1))
            shift = jnp.where(k == 7, 1, -1)
            three(0, [s1], [s1 + shift], [s1 + 2 * shift], 9)
            return 0

        lax.fori_loop(0, 8, chunk, 0)

    def second_convolutions():
        own = lon_pair(1, 3, 4, 1)
        for copy in own:
            copy.start()
        with scope("gwait"):
            g_wait()
            for side, present in ((0, has_up), (1, has_down)):
                @pl.when(present)
                def _():
                    g_share(side, core).start()
        with scope("hwait"):
            for piece in h_pieces:
                h_wait(*piece)
        with scope("sharewait"):
            for side, present in ((0, has_up), (1, has_down)):
                @pl.when(present)
                def _():
                    g_share(side, 1 - core).wait_recv()
        rhs = turned(lambda o, ch: [
            GH[side, o, ch, :, l * CH:(l + 1) * CH].astype(F32)
            for side in range(2) for l in range(3)])

        def rows(c, _):
            spectral = inverse(c, rhs)
            tiles = pl.ds(3 + 32 * c, 32)
            for side, present in ((0, has_up), (1, has_down)):
                @pl.when(present)
                def _():
                    for l in range(3):
                        x = X[0, 7 * side + l, tiles].reshape(512, CH).astype(F32)
                        h = HH[3 * side + l, tiles].reshape(512, CH).astype(F32)
                        lanes = slice((3 * side + l) * CH, (3 * side + l + 1) * CH)
                        value = jnp.tanh(x + h + spectral[:, lanes])
                        X[1, 7 * side + l, tiles] = value.astype(BF16).reshape(32, STRIPS, CH)
            return 0

        with scope("halorows"):
            lax.fori_loop(0, 2, rows, 0)
        top = lon_pair(1, 0, 3, 2)
        bottom = lon_pair(1, 7, 3, 3)
        for copy in top + bottom:
            copy.start()

        def chunk(c, _):
            @pl.when(c == 1)
            def _():
                lon_halo(1, own, 3, 4)
                lon_halo(1, top, 0, 3)
                lon_halo(1, bottom, 7, 3)

            first = 18 + 34 * c
            second = 35 - 34 * c
            shift = 2 * c - 1
            three(1, [first, second], [first - 1, second + shift],
                  [first - 2, second + 2 * shift], STEP)
            return 0

        lax.fori_loop(0, 2, chunk, 0)

    def spectral_part(b):
        with scope("dft"):
            for half in range(2):
                rhs = jnp.concatenate(
                    [H3[b, 2 * half + l, 3:67].reshape(COLS, CH) for l in range(2)], axis=1)
                both = jnp.dot(ft_v[...], rhs, preferred_element_type=F32)
                total = both[0:256] + both[256:512]
                for o in range(2):
                    for ch in range(CHIPS):
                        first = (o * CHIPS + ch) * 16
                        for l in range(2):
                            re = total[first:first + 8, l * CH:(l + 1) * CH]
                            im = total[first + 8:first + 16, l * CH:(l + 1) * CH]
                            new_re = re * cos + im * sin
                            new_im = im * cos - re * sin
                            if o == 1:
                                new_re = new_re * flip
                                new_im = new_im * flip
                            lanes = pl.ds((2 * half + l) * CH, CH)
                            PART[o, ch, 0:8, lanes] = new_re
                            PART[o, ch, 8:16, lanes] = new_im

        if b == 0:
            h_start(*h_pieces[3])
            h_start(*h_pieces[4])
            h_forward(*h_pieces[1])
        swap = pltpu.make_async_remote_copy(
            src_ref=PART.at[1 - core], dst_ref=DR.at[b],
            send_sem=d_s.at[0], recv_sem=d_r.at[b],
            device_id={"lon": sibling}, device_id_type=MESH)
        swap.start()
        with scope("swapwait"):
            swap.wait()
        RSEND[...] = PART[core] + DR[b]

        def scatter(dz, dx):
            peer = peer_at(dz, dx)
            return pltpu.make_async_remote_copy(
                src_ref=RSEND.at[peer], dst_ref=RRECV.at[b, 4 * dz + dx - 1],
                send_sem=rs_s.at[0], recv_sem=rs_r.at[b],
                device_id={"lon": peer * 2 + core}, device_id_type=MESH)

        for where in PEERS:
            scatter(*where).start()
        spectrum = RSEND[chip]
        if b == 1:
            for piece in x_pieces:
                x_done(*piece)
            for piece in h_pieces:
                h_done(*piece)
            g_done()
            for side, present in ((0, has_up), (1, has_down)):
                @pl.when(present)
                def _():
                    g_share(side, core).wait_send()
        with scope("rswait"):
            pltpu.make_async_remote_copy(
                src_ref=RSEND.at[0:CHIPS - 1], dst_ref=RRECV.at[b],
                send_sem=rs_s.at[0], recv_sem=rs_r.at[b],
                device_id={"lon": sibling}, device_id_type=MESH).wait()
        for j in range(1, CHIPS):
            spectrum = spectrum + RRECV[b, j - 1]

        if b == 0:
            for piece in h_pieces[2:]:
                h_forward(*piece)
        with scope("mix"):
            lhs = jnp.concatenate(
                [jnp.concatenate([spectrum[0:8, l * CH:(l + 1) * CH],
                                  spectrum[8:16, l * CH:(l + 1) * CH]], axis=1)
                 for l in range(ROWS)], axis=0)
            lhs = jnp.concatenate(split2(lhs), axis=0)
            mixed = jnp.zeros((ROWS * OWNED, 2 * CH), F32)
            for m in range(OWNED):
                both = jnp.dot(lhs, SW[b * OWNED + m], preferred_element_type=F32)
                mixed = jnp.where(sub == m, both[0:32] + both[32:64], mixed)
            for l in range(ROWS):
                G[b, core, chip, :, l * CH:(l + 1) * CH] = jnp.concatenate(
                    [mixed[8 * l:8 * l + 8, 0:CH], mixed[8 * l:8 * l + 8, CH:2 * CH]], axis=0
                ).astype(BF16)

        def gather(dz, dx):
            return pltpu.make_async_remote_copy(
                src_ref=G.at[b, core, chip], dst_ref=G.at[b, core, chip],
                send_sem=ag_s.at[0], recv_sem=ag_r.at[b],
                device_id={"lon": peer_at(dz, dx) * 2 + core}, device_id_type=MESH)

        for where in PEERS:
            gather(*where).start()

        gathered = pltpu.make_async_remote_copy(
            src_ref=G.at[b, core, 0:CHIPS - 1], dst_ref=G.at[b, core, 0:CHIPS - 1],
            send_sem=ag_s.at[0], recv_sem=ag_r.at[b],
            device_id={"lon": sibling}, device_id_type=MESH)
        with scope("agwait"):
            gathered.wait_recv()
        forward = pltpu.make_async_remote_copy(
            src_ref=G.at[b, core], dst_ref=G.at[b, core],
            send_sem=fw_s.at[0], recv_sem=fw_r.at[b],
            device_id={"lon": sibling}, device_id_type=MESH)
        forward.start()
        if b == 0:
            g_start()
        back = pltpu.make_async_remote_copy(
            src_ref=G.at[b, 1 - core], dst_ref=G.at[b, 1 - core],
            send_sem=fw_s.at[0], recv_sem=fw_r.at[b],
            device_id={"lon": sibling}, device_id_type=MESH)
        with scope("fwwait"):
            back.wait_recv()

        rhs = turned(lambda o, ch: [
            G[b, o, ch, :, l * CH:(l + 1) * CH].astype(F32) for l in range(ROWS)])

        def finish(c, _):
            spectral = inverse(c, rhs)
            for l in range(ROWS):
                x = X[b, 3 + l, pl.ds(3 + 32 * c, 32)].reshape(512, CH).astype(F32)
                h = H3[b, l, pl.ds(3 + 32 * c, 32)].reshape(512, CH).astype(F32)
                value = jnp.tanh(x + h + spectral[:, l * CH:(l + 1) * CH])
                X[b + 1, 3 + l, pl.ds(3 + 32 * c, 32)] = value.astype(BF16).reshape(
                    32, STRIPS, CH)
                if b == BLOCKS - 1:
                    result(c, l).start()


            return 0

        with scope("finish"):
            lax.fori_loop(0, 2, finish, 0)

        gathered.wait_send()
        forward.wait_send()

    first_convolutions()
    spectral_part(0)
    second_convolutions()
    spectral_part(1)

    with scope("store"):
        for c in range(2):
            for l in range(ROWS):
                result(c, l).wait()


def restore(strips):
    return jnp.transpose(strips, (0, 2, 1, 3)).reshape(ROWS, COLS, CH)


def per_device(field, conv_weight, conv_bias, spec_real, spec_imag):
    forward, inverse, turn = tables()
    args = (field, conv_weight, jnp.transpose(conv_bias, (1, 0, 2)), spec_real, spec_imag,
            jnp.asarray(forward), jnp.asarray(inverse), jnp.asarray(turn))
    tile = (STRIPS, CH)
    dma = pltpu.SemaphoreType.DMA
    strips = pl.pallas_call(
        kernel,
        out_shape=jax.ShapeDtypeStruct((ROWS, TILES) + tile, BF16),
        in_specs=[pl.BlockSpec(memory_space=pl.ANY)] * len(args),
        out_specs=pl.BlockSpec(memory_space=pl.ANY),
        scratch_shapes=[pltpu.VMEM(a.shape, a.dtype) for a in args] + [
            pltpu.VMEM((BLOCKS * CONVS, 12 * CH, 2 * CH), BF16),
            pltpu.VMEM((BLOCKS * OWNED, 2 * CH, 2 * CH), BF16),
            pltpu.VMEM((BLOCKS + 1, 10, EXT) + tile, BF16),
            pltpu.VMEM((8, EXT) + tile, BF16),
            pltpu.VMEM((6, EXT) + tile, BF16),
            pltpu.VMEM((BLOCKS, 4, EXT) + tile, BF16),
            pltpu.VMEM((BLOCKS, 2, 10, 3) + tile, BF16),
            pltpu.VMEM((ROWS, COLS, CH), F32),
            pltpu.VMEM((2, CHIPS, 16, ROWS * CH), F32),
            pltpu.VMEM((BLOCKS, CHIPS, 16, ROWS * CH), F32),
            pltpu.VMEM((CHIPS, 16, ROWS * CH), F32),
            pltpu.VMEM((BLOCKS, CHIPS - 1, 16, ROWS * CH), F32),
            pltpu.VMEM((BLOCKS, 2, CHIPS, 16, ROWS * CH), BF16),
            pltpu.VMEM((6, EXT) + tile, BF16),
            pltpu.VMEM((2, 2, CHIPS, 16, 3 * CH), BF16),
            dma((8,)), dma((4, 2)), dma((4, 2)), dma((2, 8)), dma((2, 8)),
            dma((1,)), dma((BLOCKS,)),
            dma((1,)), dma((BLOCKS,)), dma((1,)), dma((BLOCKS,)),
            dma((1,)), dma((BLOCKS,)),
            dma((2, 5)), dma((2, 5)), dma((2,)), dma((2,)), dma((2,)), dma((2,)),
            pltpu.VMEM((EXT,) + tile, BF16), pltpu.VMEM((EXT,) + tile, BF16),
            dma((11,)), dma((11,)),
        ],
        compiler_params=pltpu.CompilerParams(
            collective_id=0, has_side_effects=True, vmem_limit_bytes=62 * 1024 * 1024),
    )(*args)
    return restore(strips)


def solution(mesh):
    return jax.shard_map(
        per_device,
        mesh=mesh,
        in_specs=(
            P("lat", "lon", None),
            P(),
            P(),
            P(None, "lon", None, None),
            P(None, "lon", None, None),
        ),
        out_specs=P("lat", "lon", None),
        check_vma=False,
    )
```

```python
import contextlib

import jax
import jax.numpy as jnp
import numpy as np
from jax import lax
from jax.experimental import pallas as pl
from jax.experimental.pallas import tpu as pltpu
from jax.sharding import PartitionSpec as P

BLOCKS = 2
CONVS = 3
LON_DEVICES = 16
LAT_DEVICES = 8
HALF = 4
CHIPS = 8
COLS = 1024
STRIPS = 16
TILES = 64
ROWS = 4
CH = 128
OWNED = 8
EXT = 70
STEP = 17
PEERS = ((1, 2), (0, 2), (1, 1), (1, 3), (0, 1), (0, 3), (1, 0))
F32 = jnp.float32
BF16 = jnp.bfloat16
MESH = pl.DeviceIdType.MESH


def scope(name):
    return contextlib.nullcontext()


def tables():
    total = LON_DEVICES * COLS
    tile, strip = np.meshgrid(np.arange(TILES), np.arange(STRIPS), indexing="ij")
    cell = (strip * TILES + tile).reshape(-1)
    core, chip, part, low = np.meshgrid(
        np.arange(2), np.arange(CHIPS), np.arange(2), np.arange(OWNED), indexing="ij"
    )
    mode = (OWNED * (2 * chip + core) + low).reshape(-1)
    part = part.reshape(-1)
    theta = 2.0 * np.pi / total * ((mode[:, None] * cell[None, :]) % total)
    full = np.where(part[:, None] == 0, np.cos(theta), -np.sin(theta))
    weight = np.where(mode == 0, 1.0, 2.0)[:, None] / total

    def split(table):
        table = table.astype(np.float32)
        hi = table.astype(jnp.bfloat16)
        return hi, (table - hi.astype(np.float32)).astype(jnp.bfloat16)

    forward = np.concatenate(split(full), axis=0)
    inverse = np.concatenate(split((full * weight).T), axis=1)
    phi = 2.0 * np.pi / 16.0 * ((np.arange(16)[:, None] * np.arange(OWNED)[None, :]) % 16)
    turn = np.stack([np.cos(phi), np.sin(phi)], axis=1).astype(np.float32)
    turn = np.broadcast_to(turn[..., None], (16, 2, OWNED, CH)).copy()
    return forward, inverse, turn


def split2(value):
    hi = value.astype(BF16)
    return hi, (value - hi.astype(F32)).astype(BF16)


def kernel(field, cw, cb, sr, si, ft, iv, tw, out,
           f_v, cw_v, cb_v, sr_v, si_v, ft_v, iv_v, tw_v, T, SW, X, H1, H2, H3, ST, S,
           PART, DR, RSEND, RRECV, G, HH, GH,
           in_sem, lon_s, lon_r, lat_s, lat_r, d_s, d_r, rs_s, rs_r, ag_s, ag_r, fw_s, fw_r,
           h_s, h_r, g_s, g_r, gf_s, gf_r,
           RX, RH, edge_s, edge_r):
    d = lax.axis_index("lon")
    lt = lax.axis_index("lat")
    core = lax.rem(d, 2)
    chip = lax.div(d, 2)
    sibling = chip * 2 + 1 - core
    right = lax.rem(d + 1, LON_DEVICES)
    left = lax.rem(d + LON_DEVICES - 1, LON_DEVICES)
    outer = jnp.where(core == 0, left, right)
    across = lax.rem(lt + HALF, LAT_DEVICES)
    wrap = jnp.where(lt < HALF, HALF - 1 - lt, 3 * HALF - 1 - lt)
    outermost = jnp.logical_or(lax.rem(lt, HALF) == 0, lax.rem(lt, HALF) == HALF - 1)
    has_up = lt > 0
    has_down = lt < LAT_DEVICES - 1

    loads = [
        pltpu.make_async_copy(src, dst, in_sem.at[i])
        for i, (src, dst) in enumerate(
            [(field, f_v), (cw, cw_v), (cb, cb_v), (sr, sr_v), (si, si_v), (ft, ft_v),
             (iv, iv_v), (tw, tw_v)]
        )
    ]
    for load in loads:
        load.start()

    barrier = pltpu.get_barrier_semaphore()
    pl.semaphore_signal(barrier, inc=1, device_id={"lon": sibling}, device_id_type=MESH)
    pl.semaphore_signal(barrier, inc=1, device_id={"lon": outer}, device_id_type=MESH)

    def peer_at(dz, dx):
        z = lax.div(chip, 4)
        return (1 - z if dz else z) * 4 + lax.rem(chip + dx, 4)

    for where in PEERS:
        pl.semaphore_signal(
            barrier, inc=1, device_id={"lon": peer_at(*where) * 2 + core}, device_id_type=MESH)

    @pl.when(has_up)
    def _():
        pl.semaphore_signal(barrier, inc=1, device_id={"lat": lt - 1}, device_id_type=MESH)

    @pl.when(has_down)
    def _():
        pl.semaphore_signal(barrier, inc=1, device_id={"lat": lt + 1}, device_id_type=MESH)

    @pl.when(outermost)
    def _():
        pl.semaphore_signal(barrier, inc=1, device_id={"lat": across}, device_id_type=MESH)
        pl.semaphore_signal(barrier, inc=1, device_id={"lat": wrap}, device_id_type=MESH)

    @pl.when(jnp.logical_not(has_up))
    def _():
        for b in range(BLOCKS):
            X[b, 0:3] = jnp.zeros((3, EXT, STRIPS, CH), BF16)

    @pl.when(jnp.logical_not(has_down))
    def _():
        for b in range(BLOCKS):
            X[b, 7:10] = jnp.zeros((3, EXT, STRIPS, CH), BF16)

    def permute(first, last):
        for row in range(ROWS):
            for t in range(first, last):
                X[0, 3 + row, t] = S[row, pl.ds(t - 3, STRIPS, stride=TILES), :].astype(BF16)

    with scope("permute_in"):
        loads[0].wait()
        for row in range(ROWS):
            S[row] = f_v[row].astype(F32)
        permute(9, 20)
    with scope("barrier"):
        pl.semaphore_wait(
            barrier, CHIPS + 1 + has_up.astype(jnp.int32) + has_down.astype(jnp.int32)
            + 2 * outermost.astype(jnp.int32)
        )

    def build_weights():
        loads[1].wait()
        loads[2].wait()
        zero = jnp.zeros((CH, CH), BF16)

        def build(i, _):
            b = lax.div(i, CONVS)
            layer = lax.rem(i, CONVS)
            for tap in range(3):
                w0, w1, w2 = (cw_v[b, layer, a, tap] for a in range(3))
                for r, (first, second) in enumerate(((w0, zero), (w1, w0), (w2, w1), (zero, w2))):
                    rows = pl.ds((tap * 4 + r) * CH, CH)
                    T[i, rows, 0:CH] = first
                    T[i, rows, CH:2 * CH] = second
            return 0

        lax.fori_loop(0, BLOCKS * CONVS, build, 0)

        loads[3].wait()
        loads[4].wait()

        def build_spec(i, _):
            b = lax.div(i, OWNED)
            m = lax.rem(i, OWNED)
            wr = sr_v[b, m]
            wi = si_v[b, m]
            SW[i, 0:CH, 0:CH] = wr
            SW[i, 0:CH, CH:2 * CH] = wi
            SW[i, CH:2 * CH, 0:CH] = -wi
            SW[i, CH:2 * CH, CH:2 * CH] = wr
            return 0

        lax.fori_loop(0, BLOCKS * OWNED, build_spec, 0)
        for load in loads[5:7]:
            load.wait()

    loads[7].wait()
    cos = tw_v[d, 0]
    sin = tw_v[d, 1]
    flip = (1 - 2 * core).astype(F32)
    up_mask = has_up.astype(F32)
    down_mask = has_down.astype(F32)
    strip = lax.broadcasted_iota(jnp.int32, (STRIPS, CH), 0)
    sub = lax.rem(lax.broadcasted_iota(jnp.int32, (ROWS * OWNED, 2 * CH), 0), OWNED)

    def convolve(source, target, b, layer, starts, step, pairs, masks):
        bias = cb_v[layer, b:b + 1, :]
        size = step * STRIPS
        for pair in range(pairs):
            lhs = jnp.concatenate(
                [jnp.concatenate(
                    [source(2 * pair + r, start - 1 + tap).reshape(size, CH)
                     for start in starts], axis=0)
                 for tap in range(3) for r in range(4)], axis=1)
            total = jnp.dot(lhs, T[b * CONVS + layer], preferred_element_type=F32)
            for o in range(2):
                half = 0.5 * (total[:, o * CH:(o + 1) * CH] + bias)
                value = half * jnp.tanh(half) + half
                mask = masks.get(2 * pair + o)
                if mask is not None:
                    value = value * mask
                value = value.astype(BF16)
                for i, start in enumerate(starts):
                    target[2 * pair + o, pl.ds(start, step)] = value[
                        i * size:(i + 1) * size].reshape(step, STRIPS, CH)

    def three(b, s1, s2, s3, step):
        with scope("conv"):
            convolve(lambda r, t: X[b, r, pl.ds(t, step)], H1, b, 0, s1, step, 4,
                     {0: up_mask, 1: up_mask, 6: down_mask, 7: down_mask})
            convolve(lambda r, t: H1[r, pl.ds(t, step)], H2, b, 1, s2, step, 3,
                     {0: up_mask, 5: down_mask})
            convolve(lambda r, t: H2[r, pl.ds(t, step)], H3.at[b], b, 2, s3, step, 2, {})

    def lon_pair(b, first, count, slot):
        rows = pl.ds(first, count)
        return (
            pltpu.make_async_remote_copy(
                src_ref=X.at[b, rows, 64:67], dst_ref=ST.at[b, 0, rows],
                send_sem=lon_s.at[slot, 0], recv_sem=lon_r.at[slot, 0],
                device_id={"lon": right}, device_id_type=MESH),
            pltpu.make_async_remote_copy(
                src_ref=X.at[b, rows, 3:6], dst_ref=ST.at[b, 1, rows],
                send_sem=lon_s.at[slot, 1], recv_sem=lon_r.at[slot, 1],
                device_id={"lon": left}, device_id_type=MESH),
        )

    def lon_halo(b, pair, first, count):
        with scope("lonwait"):
            for copy in pair:
                copy.wait()
        for row in range(first, first + count):
            for j in range(3):
                own = X[b, row, 64 + j].astype(F32)
                other = ST[b, 0, row, j].astype(F32)
                tile = jnp.where(strip == 0, pltpu.roll(other, 1, 0), pltpu.roll(own, 1, 0))
                X[b, row, j] = tile.astype(BF16)
                own = X[b, row, 3 + j].astype(F32)
                other = ST[b, 1, row, j].astype(F32)
                tile = jnp.where(
                    strip == STRIPS - 1,
                    pltpu.roll(other, STRIPS - 1, 0), pltpu.roll(own, STRIPS - 1, 0))
                X[b, row, 67 + j] = tile.astype(BF16)

    def both_ways(down, up):
        def start(*piece):
            @pl.when(has_down)
            def _():
                down(*piece).start()

            @pl.when(has_up)
            def _():
                up(*piece).start()

        def wait_recv(*piece):
            @pl.when(has_up)
            def _():
                down(*piece).wait_recv()

            @pl.when(has_down)
            def _():
                up(*piece).wait_recv()

        def wait_send(*piece):
            @pl.when(has_down)
            def _():
                down(*piece).wait_send()

            @pl.when(has_up)
            def _():
                up(*piece).wait_send()

        return start, wait_recv, wait_send

    def halo_ways(source, target, buffer, down_row, up_row, other_side, sends, recvs, base, skip):
        def direct(way, count, first, tiles, slot):
            at = up_row if way else down_row
            to = other_side if way else 0
            window = pl.ds(first, tiles)
            return pltpu.make_async_remote_copy(
                src_ref=source.at[pl.ds(at, count), window],
                dst_ref=target.at[pl.ds(to, count), window],
                send_sem=sends.at[way, slot], recv_sem=recvs.at[way, slot],
                device_id={"lat": lt + 1 - 2 * way}, device_id_type=MESH)

        def lend(way, first, tiles, slot):
            at = (up_row if way else down_row) + 2
            window = pl.ds(first, tiles)
            return pltpu.make_async_remote_copy(
                src_ref=source.at[at, window], dst_ref=buffer.at[window],
                send_sem=edge_s.at[base + slot], recv_sem=edge_r.at[base + slot],
                device_id={"lat": across}, device_id_type=MESH)

        def relay(way, first, tiles, slot):
            to = (other_side if way else 0) + 2
            window = pl.ds(first, tiles)
            return pltpu.make_async_remote_copy(
                src_ref=buffer.at[window], dst_ref=target.at[to, window],
                send_sem=edge_s.at[base + slot], recv_sem=edge_r.at[base + slot],
                device_id={"lat": wrap}, device_id_type=MESH)

        def plain(piece):
            return isinstance(piece[2], int) and piece[2] < skip

        def each(piece, down, down_split, up, up_split, middle=True, others=True):
            if plain(piece):
                pl.when(has_down)(down)
                pl.when(has_up)(up)
                return
            if others:
                pl.when(jnp.logical_and(has_down, lt != HALF - 1))(down)
                pl.when(jnp.logical_and(has_up, lt != HALF))(up)
            if middle:
                pl.when(lt == HALF - 1)(down_split)
                pl.when(lt == HALF)(up_split)

        def start(*piece, **which):
            def split(way):
                direct(way, 2, *piece).start()
                lend(way, *piece).start()

            each(piece, lambda: direct(0, 3, *piece).start(), lambda: split(0),
                 lambda: direct(1, 3, *piece).start(), lambda: split(1), **which)

        def forward(*piece):
            @pl.when(lt == LAT_DEVICES - 1)
            def _():
                lend(0, *piece).wait_recv()
                relay(0, *piece).start()

            @pl.when(lt == 0)
            def _():
                lend(1, *piece).wait_recv()
                relay(1, *piece).start()

        def wait_recv(*piece):
            def split(way):
                direct(way, 2, *piece).wait_recv()
                relay(way, *piece).wait_recv()

            each(piece, lambda: direct(1, 3, *piece).wait_recv(), lambda: split(1),
                 lambda: direct(0, 3, *piece).wait_recv(), lambda: split(0))

        def wait_send(*piece):
            def split(way):
                direct(way, 2, *piece).wait_send()
                lend(way, *piece).wait_send()

            each(piece, lambda: direct(0, 3, *piece).wait_send(), lambda: split(0),
                 lambda: direct(1, 3, *piece).wait_send(), lambda: split(1))
            if not plain(piece):
                @pl.when(lt == LAT_DEVICES - 1)
                def _():
                    relay(0, *piece).wait_send()

                @pl.when(lt == 0)
                def _():
                    relay(1, *piece).wait_send()

        return start, forward, wait_recv, wait_send

    def g_down():
        return pltpu.make_async_remote_copy(
            src_ref=G.at[0, core, :, :, CH:4 * CH], dst_ref=GH.at[0, core],
            send_sem=g_s.at[0], recv_sem=g_r.at[0],
            device_id={"lat": lt + 1}, device_id_type=MESH)

    def g_up():
        return pltpu.make_async_remote_copy(
            src_ref=G.at[0, core, :, :, 0:3 * CH], dst_ref=GH.at[1, core],
            send_sem=g_s.at[1], recv_sem=g_r.at[1],
            device_id={"lat": lt - 1}, device_id_type=MESH)

    def g_share(side, half):
        return pltpu.make_async_remote_copy(
            src_ref=GH.at[side, half], dst_ref=GH.at[side, half],
            send_sem=gf_s.at[side], recv_sem=gf_r.at[side],
            device_id={"lon": sibling}, device_id_type=MESH)

    def turned(load):
        his = []
        los = []
        for o in range(2):
            for ch in range(CHIPS):
                parts = []
                for value in load(o, ch):
                    re = value[0:8]
                    im = value[8:16]
                    new_re = re * cos - im * sin
                    new_im = re * sin + im * cos
                    if o == 1:
                        new_re = new_re * flip
                        new_im = new_im * flip
                    parts.append(jnp.concatenate([new_re, new_im], axis=0))
                hi, lo = split2(jnp.concatenate(parts, axis=1))
                his.append(hi)
                los.append(lo)
        hi = jnp.concatenate(his, axis=0)
        lo = jnp.concatenate(los, axis=0)
        return jnp.concatenate([hi, hi, lo], axis=0)

    def inverse(c, rhs):
        table = iv_v[pl.ds(c * 512, 512), :]
        lhs = jnp.concatenate([table, table[:, 0:256]], axis=1)
        return jnp.dot(lhs, rhs, preferred_element_type=F32)

    def result(c):
        return pltpu.make_async_copy(
            X.at[BLOCKS, 3:7, pl.ds(3 + 32 * c, 32)], out.at[:, pl.ds(32 * c, 32)], in_sem.at[c])

    x_pieces = ([(9, 11, 0)] + [(20 + 9 * k, 9, k + 1) for k in range(5)]
                + [(65, 5, 6), (0, 9, 7)])
    h_pieces = [(12, 14, 0), (26, 18, 1), (44, 14, 2), (58, 9, 3), (3, 9, 4)]
    x_start, x_forward, x_wait, x_done = halo_ways(
        X.at[0], X.at[0], RX, 4, 3, 7, lat_s, lat_r, -2, 2)
    h_start, h_forward, h_wait, h_done = halo_ways(
        H3.at[0], HH, RH, 1, 0, 3, h_s, h_r, 6, 0)
    g_start, g_wait, g_done = both_ways(g_down, g_up)

    def first_convolutions():
        x_start(*x_pieces[0])
        permute(20, 67)
        for piece in x_pieces[1:6]:
            x_start(*piece)
        permute(3, 9)
        pair = lon_pair(0, 3, 4, 0)
        for copy in pair:
            copy.start()
        lon_halo(0, pair, 3, 4)
        for piece in x_pieces[6:]:
            x_start(*piece)
        with scope("build"):
            build_weights()

        def chunk(k, _):
            @pl.when(k < 4)
            def _():
                x_forward(29 + 9 * k, 9, k + 2)

            for p in range(6, 8):
                @pl.when(k == p - 2)
                def _():
                    x_forward(*x_pieces[p])

            @pl.when(k == 6)
            def _():
                h_forward(*h_pieces[0])

            with scope("latwait"):
                @pl.when(k == 0)
                def _():
                    x_wait(*x_pieces[0])

                @pl.when(k == 1)
                def _():
                    x_wait(*x_pieces[1])

                @pl.when(jnp.logical_and(k > 1, k < 6))
                def _():
                    x_wait(11 + 9 * k, 9, k)

                @pl.when(k == 6)
                def _():
                    x_wait(*x_pieces[6])

                @pl.when(k == 7)
                def _():
                    x_wait(*x_pieces[7])

            for p in range(3):
                @pl.when(k == 2 * p + 2)
                def _():
                    h_start(*h_pieces[p])

            s1 = jnp.where(k < 6, 10 + 9 * k, jnp.where(k == 6, 60, 1))
            shift = jnp.where(k == 7, 1, -1)
            three(0, [s1], [s1 + shift], [s1 + 2 * shift], 9)
            return 0

        lax.fori_loop(0, 8, chunk, 0)

    def second_convolutions():
        own = lon_pair(1, 3, 4, 1)
        for copy in own:
            copy.start()
        with scope("gwait"):
            g_wait()
            for side, present in ((0, has_up), (1, has_down)):
                @pl.when(present)
                def _():
                    g_share(side, core).start()
        with scope("hwait"):
            for piece in h_pieces:
                h_wait(*piece)
        with scope("sharewait"):
            for side, present in ((0, has_up), (1, has_down)):
                @pl.when(present)
                def _():
                    g_share(side, 1 - core).wait_recv()
        rhs = turned(lambda o, ch: [
            GH[side, o, ch, :, l * CH:(l + 1) * CH].astype(F32)
            for side in range(2) for l in range(3)])

        def rows(c, _):
            spectral = inverse(c, rhs)
            tiles = pl.ds(3 + 32 * c, 32)
            for side, present in ((0, has_up), (1, has_down)):
                @pl.when(present)
                def _():
                    for l in range(3):
                        x = X[0, 7 * side + l, tiles].reshape(512, CH).astype(F32)
                        h = HH[3 * side + l, tiles].reshape(512, CH).astype(F32)
                        lanes = slice((3 * side + l) * CH, (3 * side + l + 1) * CH)
                        value = jnp.tanh(x + h + spectral[:, lanes])
                        X[1, 7 * side + l, tiles] = value.astype(BF16).reshape(32, STRIPS, CH)
            return 0

        with scope("halorows"):
            lax.fori_loop(0, 2, rows, 0)
        top = lon_pair(1, 0, 3, 2)
        bottom = lon_pair(1, 7, 3, 3)
        for copy in top + bottom:
            copy.start()

        def chunk(c, _):
            @pl.when(c == 1)
            def _():
                lon_halo(1, own, 3, 4)
                lon_halo(1, top, 0, 3)
                lon_halo(1, bottom, 7, 3)

            first = 18 + 34 * c
            second = 35 - 34 * c
            shift = 2 * c - 1
            three(1, [first, second], [first - 1, second + shift],
                  [first - 2, second + 2 * shift], STEP)
            return 0

        lax.fori_loop(0, 2, chunk, 0)

    def spectral_part(b):
        with scope("dft"):
            for half in range(2):
                rhs = jnp.concatenate(
                    [H3[b, 2 * half + l, 3:67].reshape(COLS, CH) for l in range(2)], axis=1)
                both = jnp.dot(ft_v[...], rhs, preferred_element_type=F32)
                total = both[0:256] + both[256:512]
                for o in range(2):
                    for ch in range(CHIPS):
                        first = (o * CHIPS + ch) * 16
                        for l in range(2):
                            re = total[first:first + 8, l * CH:(l + 1) * CH]
                            im = total[first + 8:first + 16, l * CH:(l + 1) * CH]
                            new_re = re * cos + im * sin
                            new_im = im * cos - re * sin
                            if o == 1:
                                new_re = new_re * flip
                                new_im = new_im * flip
                            lanes = pl.ds((2 * half + l) * CH, CH)
                            PART[o, ch, 0:8, lanes] = new_re
                            PART[o, ch, 8:16, lanes] = new_im

        if b == 0:
            h_start(*h_pieces[3])
            h_start(*h_pieces[4], others=False)
            h_forward(*h_pieces[1])
        swap = pltpu.make_async_remote_copy(
            src_ref=PART.at[1 - core], dst_ref=DR.at[b],
            send_sem=d_s.at[0], recv_sem=d_r.at[b],
            device_id={"lon": sibling}, device_id_type=MESH)
        swap.start()
        with scope("swapwait"):
            swap.wait()
        RSEND[...] = PART[core] + DR[b]

        def scatter(dz, dx):
            peer = peer_at(dz, dx)
            return pltpu.make_async_remote_copy(
                src_ref=RSEND.at[peer], dst_ref=RRECV.at[b, 4 * dz + dx - 1],
                send_sem=rs_s.at[0], recv_sem=rs_r.at[b],
                device_id={"lon": peer * 2 + core}, device_id_type=MESH)

        for where in PEERS:
            scatter(*where).start()
        spectrum = RSEND[chip]
        if b == 1:
            for piece in x_pieces:
                x_done(*piece)
            for piece in h_pieces:
                h_done(*piece)
            g_done()
            for side, present in ((0, has_up), (1, has_down)):
                @pl.when(present)
                def _():
                    g_share(side, core).wait_send()
        with scope("rswait"):
            pltpu.make_async_remote_copy(
                src_ref=RSEND.at[0:CHIPS - 1], dst_ref=RRECV.at[b],
                send_sem=rs_s.at[0], recv_sem=rs_r.at[b],
                device_id={"lon": sibling}, device_id_type=MESH).wait()
        for j in range(1, CHIPS):
            spectrum = spectrum + RRECV[b, j - 1]

        if b == 0:
            for piece in h_pieces[2:]:
                h_forward(*piece)
        with scope("mix"):
            lhs = jnp.concatenate(
                [jnp.concatenate([spectrum[0:8, l * CH:(l + 1) * CH],
                                  spectrum[8:16, l * CH:(l + 1) * CH]], axis=1)
                 for l in range(ROWS)], axis=0)
            lhs = jnp.concatenate(split2(lhs), axis=0)
            mixed = jnp.zeros((ROWS * OWNED, 2 * CH), F32)
            for m in range(OWNED):
                both = jnp.dot(lhs, SW[b * OWNED + m], preferred_element_type=F32)
                mixed = jnp.where(sub == m, both[0:32] + both[32:64], mixed)
            for l in range(ROWS):
                G[b, core, chip, :, l * CH:(l + 1) * CH] = jnp.concatenate(
                    [mixed[8 * l:8 * l + 8, 0:CH], mixed[8 * l:8 * l + 8, CH:2 * CH]], axis=0
                ).astype(BF16)

        def gather(dz, dx):
            return pltpu.make_async_remote_copy(
                src_ref=G.at[b, core, chip], dst_ref=G.at[b, core, chip],
                send_sem=ag_s.at[0], recv_sem=ag_r.at[b],
                device_id={"lon": peer_at(dz, dx) * 2 + core}, device_id_type=MESH)

        for where in PEERS:
            gather(*where).start()

        gathered = pltpu.make_async_remote_copy(
            src_ref=G.at[b, core, 0:CHIPS - 1], dst_ref=G.at[b, core, 0:CHIPS - 1],
            send_sem=ag_s.at[0], recv_sem=ag_r.at[b],
            device_id={"lon": sibling}, device_id_type=MESH)
        with scope("agwait"):
            gathered.wait_recv()
        forward = pltpu.make_async_remote_copy(
            src_ref=G.at[b, core], dst_ref=G.at[b, core],
            send_sem=fw_s.at[0], recv_sem=fw_r.at[b],
            device_id={"lon": sibling}, device_id_type=MESH)
        forward.start()
        if b == 0:
            g_start()
            h_start(*h_pieces[4], middle=False)
        back = pltpu.make_async_remote_copy(
            src_ref=G.at[b, 1 - core], dst_ref=G.at[b, 1 - core],
            send_sem=fw_s.at[0], recv_sem=fw_r.at[b],
            device_id={"lon": sibling}, device_id_type=MESH)
        with scope("fwwait"):
            back.wait_recv()

        rhs = turned(lambda o, ch: [
            G[b, o, ch, :, l * CH:(l + 1) * CH].astype(F32) for l in range(ROWS)])

        def finish(c, _):
            spectral = inverse(c, rhs)
            for l in range(ROWS):
                x = X[b, 3 + l, pl.ds(3 + 32 * c, 32)].reshape(512, CH).astype(F32)
                h = H3[b, l, pl.ds(3 + 32 * c, 32)].reshape(512, CH).astype(F32)
                value = jnp.tanh(x + h + spectral[:, l * CH:(l + 1) * CH])
                X[b + 1, 3 + l, pl.ds(3 + 32 * c, 32)] = value.astype(BF16).reshape(
                    32, STRIPS, CH)

            if b == BLOCKS - 1:
                result(c).start()

            return 0

        with scope("finish"):
            lax.fori_loop(0, 2, finish, 0)

        gathered.wait_send()
        forward.wait_send()

    first_convolutions()
    spectral_part(0)
    second_convolutions()
    spectral_part(1)

    with scope("store"):
        for c in range(2):
            result(c).wait()


def restore(strips):
    return jnp.transpose(strips, (0, 2, 1, 3)).reshape(ROWS, COLS, CH)


def per_device(field, conv_weight, conv_bias, spec_real, spec_imag):
    forward, inverse, turn = tables()
    args = (field, conv_weight, jnp.transpose(conv_bias, (1, 0, 2)), spec_real, spec_imag,
            jnp.asarray(forward), jnp.asarray(inverse), jnp.asarray(turn))
    tile = (STRIPS, CH)
    dma = pltpu.SemaphoreType.DMA
    strips = pl.pallas_call(
        kernel,
        out_shape=jax.ShapeDtypeStruct((ROWS, TILES) + tile, BF16),
        in_specs=[pl.BlockSpec(memory_space=pl.ANY)] * len(args),
        out_specs=pl.BlockSpec(memory_space=pl.ANY),
        scratch_shapes=[pltpu.VMEM(a.shape, a.dtype) for a in args] + [
            pltpu.VMEM((BLOCKS * CONVS, 12 * CH, 2 * CH), BF16),
            pltpu.VMEM((BLOCKS * OWNED, 2 * CH, 2 * CH), BF16),
            pltpu.VMEM((BLOCKS + 1, 10, EXT) + tile, BF16),
            pltpu.VMEM((8, EXT) + tile, BF16),
            pltpu.VMEM((6, EXT) + tile, BF16),
            pltpu.VMEM((BLOCKS, 4, EXT) + tile, BF16),
            pltpu.VMEM((BLOCKS, 2, 10, 3) + tile, BF16),
            pltpu.VMEM((ROWS, COLS, CH), F32),
            pltpu.VMEM((2, CHIPS, 16, ROWS * CH), F32),
            pltpu.VMEM((BLOCKS, CHIPS, 16, ROWS * CH), F32),
            pltpu.VMEM((CHIPS, 16, ROWS * CH), F32),
            pltpu.VMEM((BLOCKS, CHIPS - 1, 16, ROWS * CH), F32),
            pltpu.VMEM((BLOCKS, 2, CHIPS, 16, ROWS * CH), BF16),
            pltpu.VMEM((6, EXT) + tile, BF16),
            pltpu.VMEM((2, 2, CHIPS, 16, 3 * CH), BF16),
            dma((8,)), dma((4, 2)), dma((4, 2)), dma((2, 8)), dma((2, 8)),
            dma((1,)), dma((BLOCKS,)),
            dma((1,)), dma((BLOCKS,)), dma((1,)), dma((BLOCKS,)),
            dma((1,)), dma((BLOCKS,)),
            dma((2, 5)), dma((2, 5)), dma((2,)), dma((2,)), dma((2,)), dma((2,)),
            pltpu.VMEM((EXT,) + tile, BF16), pltpu.VMEM((EXT,) + tile, BF16),
            dma((11,)), dma((11,)),
        ],
        compiler_params=pltpu.CompilerParams(
            collective_id=0, has_side_effects=True, vmem_limit_bytes=62 * 1024 * 1024),
    )(*args)
    return restore(strips)


def solution(mesh):
    return jax.shard_map(
        per_device,
        mesh=mesh,
        in_specs=(
            P("lat", "lon", None),
            P(),
            P(),
            P(None, "lon", None, None),
            P(None, "lon", None, None),
        ),
        out_specs=P("lat", "lon", None),
        check_vma=False,
    )
```

```python
import contextlib

import jax
import jax.numpy as jnp
import numpy as np
from jax import lax
from jax.experimental import pallas as pl
from jax.experimental.pallas import tpu as pltpu
from jax.sharding import PartitionSpec as P

BLOCKS = 2
CONVS = 3
LON_DEVICES = 16
LAT_DEVICES = 8
HALF = 4
CHIPS = 8
COLS = 1024
STRIPS = 16
TILES = 64
ROWS = 4
CH = 128
OWNED = 8
EXT = 70
STEP = 17
PEERS = ((1, 2), (0, 2), (1, 1), (1, 3), (0, 1), (0, 3), (1, 0))
F32 = jnp.float32
BF16 = jnp.bfloat16
MESH = pl.DeviceIdType.MESH


def scope(name):
    return contextlib.nullcontext()


def tables():
    total = LON_DEVICES * COLS
    tile, strip = np.meshgrid(np.arange(TILES), np.arange(STRIPS), indexing="ij")
    cell = (strip * TILES + tile).reshape(-1)
    core, chip, part, low = np.meshgrid(
        np.arange(2), np.arange(CHIPS), np.arange(2), np.arange(OWNED), indexing="ij"
    )
    mode = (OWNED * (2 * chip + core) + low).reshape(-1)
    part = part.reshape(-1)
    theta = 2.0 * np.pi / total * ((mode[:, None] * cell[None, :]) % total)
    full = np.where(part[:, None] == 0, np.cos(theta), -np.sin(theta))
    weight = np.where(mode == 0, 1.0, 2.0)[:, None] / total

    def split(table):
        table = table.astype(np.float32)
        hi = table.astype(jnp.bfloat16)
        return hi, (table - hi.astype(np.float32)).astype(jnp.bfloat16)

    forward = np.concatenate(split(full), axis=0)
    inverse = np.concatenate(split((full * weight).T), axis=1)
    phi = 2.0 * np.pi / 16.0 * ((np.arange(16)[:, None] * np.arange(OWNED)[None, :]) % 16)
    turn = np.stack([np.cos(phi), np.sin(phi)], axis=1).astype(np.float32)
    turn = np.broadcast_to(turn[..., None], (16, 2, OWNED, CH)).copy()
    return forward, inverse, turn


def split2(value):
    hi = value.astype(BF16)
    return hi, (value - hi.astype(F32)).astype(BF16)


def kernel(field, cw, cb, sr, si, ft, iv, tw, out,
           f_v, cw_v, cb_v, sr_v, si_v, ft_v, iv_v, tw_v, T, SW, X, H1, H2, H3, ST, S,
           PART, DR, RSEND, RRECV, G, HH, GH,
           in_sem, lon_s, lon_r, lat_s, lat_r, d_s, d_r, rs_s, rs_r, ag_s, ag_r, fw_s, fw_r,
           h_s, h_r, g_s, g_r, gf_s, gf_r,
           RX, RH, edge_s, edge_r):
    d = lax.axis_index("lon")
    lt = lax.axis_index("lat")
    core = lax.rem(d, 2)
    chip = lax.div(d, 2)
    sibling = chip * 2 + 1 - core
    right = lax.rem(d + 1, LON_DEVICES)
    left = lax.rem(d + LON_DEVICES - 1, LON_DEVICES)
    outer = jnp.where(core == 0, left, right)
    across = lax.rem(lt + HALF, LAT_DEVICES)
    wrap = jnp.where(lt < HALF, HALF - 1 - lt, 3 * HALF - 1 - lt)
    outermost = jnp.logical_or(lax.rem(lt, HALF) == 0, lax.rem(lt, HALF) == HALF - 1)
    has_up = lt > 0
    has_down = lt < LAT_DEVICES - 1

    loads = [
        pltpu.make_async_copy(src, dst, in_sem.at[i])
        for i, (src, dst) in enumerate(
            [(field, f_v), (cw, cw_v), (cb, cb_v), (sr, sr_v), (si, si_v), (ft, ft_v),
             (iv, iv_v), (tw, tw_v)]
        )
    ]
    barrier = pltpu.get_barrier_semaphore()
    pl.semaphore_signal(barrier, inc=1, device_id={"lon": sibling}, device_id_type=MESH)
    pl.semaphore_signal(barrier, inc=1, device_id={"lon": outer}, device_id_type=MESH)

    def peer_at(dz, dx):
        z = lax.div(chip, 4)
        return (1 - z if dz else z) * 4 + lax.rem(chip + dx, 4)

    for where in PEERS:
        pl.semaphore_signal(
            barrier, inc=1, device_id={"lon": peer_at(*where) * 2 + core}, device_id_type=MESH)

    @pl.when(has_up)
    def _():
        pl.semaphore_signal(barrier, inc=1, device_id={"lat": lt - 1}, device_id_type=MESH)

    @pl.when(has_down)
    def _():
        pl.semaphore_signal(barrier, inc=1, device_id={"lat": lt + 1}, device_id_type=MESH)

    @pl.when(outermost)
    def _():
        pl.semaphore_signal(barrier, inc=1, device_id={"lat": across}, device_id_type=MESH)
        pl.semaphore_signal(barrier, inc=1, device_id={"lat": wrap}, device_id_type=MESH)

    for load in loads:
        load.start()

    @pl.when(jnp.logical_not(has_up))
    def _():
        for b in range(BLOCKS):
            X[b, 0:3] = jnp.zeros((3, EXT, STRIPS, CH), BF16)

    @pl.when(jnp.logical_not(has_down))
    def _():
        for b in range(BLOCKS):
            X[b, 7:10] = jnp.zeros((3, EXT, STRIPS, CH), BF16)

    def permute(first, last):
        for row in range(ROWS):
            for t in range(first, last):
                X[0, 3 + row, t] = S[row, pl.ds(t - 3, STRIPS, stride=TILES), :].astype(BF16)

    with scope("permute_in"):
        loads[0].wait()
        for row in range(ROWS):
            S[row] = f_v[row].astype(F32)
        permute(9, 20)
    with scope("barrier"):
        pl.semaphore_wait(
            barrier, CHIPS + 1 + has_up.astype(jnp.int32) + has_down.astype(jnp.int32)
            + 2 * outermost.astype(jnp.int32)
        )

    def build_weights():
        loads[1].wait()
        loads[2].wait()
        zero = jnp.zeros((CH, CH), BF16)

        def build(i, _):
            b = lax.div(i, CONVS)
            layer = lax.rem(i, CONVS)
            for tap in range(3):
                w0, w1, w2 = (cw_v[b, layer, a, tap] for a in range(3))
                for r, (first, second) in enumerate(((w0, zero), (w1, w0), (w2, w1), (zero, w2))):
                    rows = pl.ds((tap * 4 + r) * CH, CH)
                    T[i, rows, 0:CH] = first
                    T[i, rows, CH:2 * CH] = second
            return 0

        lax.fori_loop(0, BLOCKS * CONVS, build, 0)

        loads[3].wait()
        loads[4].wait()

        def build_spec(i, _):
            b = lax.div(i, OWNED)
            m = lax.rem(i, OWNED)
            wr = sr_v[b, m]
            wi = si_v[b, m]
            SW[i, 0:CH, 0:CH] = wr
            SW[i, 0:CH, CH:2 * CH] = wi
            SW[i, CH:2 * CH, 0:CH] = -wi
            SW[i, CH:2 * CH, CH:2 * CH] = wr
            return 0

        lax.fori_loop(0, BLOCKS * OWNED, build_spec, 0)
        for load in loads[5:7]:
            load.wait()

    loads[7].wait()
    cos = tw_v[d, 0]
    sin = tw_v[d, 1]
    flip = (1 - 2 * core).astype(F32)
    up_mask = has_up.astype(F32)
    down_mask = has_down.astype(F32)
    strip = lax.broadcasted_iota(jnp.int32, (STRIPS, CH), 0)
    sub = lax.rem(lax.broadcasted_iota(jnp.int32, (ROWS * OWNED, 2 * CH), 0), OWNED)

    def convolve(source, target, b, layer, starts, step, pairs, masks):
        bias = cb_v[layer, b:b + 1, :]
        size = step * STRIPS
        for pair in range(pairs):
            lhs = jnp.concatenate(
                [jnp.concatenate(
                    [source(2 * pair + r, start - 1 + tap).reshape(size, CH)
                     for start in starts], axis=0)
                 for tap in range(3) for r in range(4)], axis=1)
            total = jnp.dot(lhs, T[b * CONVS + layer], preferred_element_type=F32)
            for o in range(2):
                half = 0.5 * (total[:, o * CH:(o + 1) * CH] + bias)
                value = half * jnp.tanh(half) + half
                mask = masks.get(2 * pair + o)
                if mask is not None:
                    value = value * mask
                value = value.astype(BF16)
                for i, start in enumerate(starts):
                    target[2 * pair + o, pl.ds(start, step)] = value[
                        i * size:(i + 1) * size].reshape(step, STRIPS, CH)

    def three(b, s1, s2, s3, step):
        with scope("conv"):
            convolve(lambda r, t: X[b, r, pl.ds(t, step)], H1, b, 0, s1, step, 4,
                     {0: up_mask, 1: up_mask, 6: down_mask, 7: down_mask})
            convolve(lambda r, t: H1[r, pl.ds(t, step)], H2, b, 1, s2, step, 3,
                     {0: up_mask, 5: down_mask})
            convolve(lambda r, t: H2[r, pl.ds(t, step)], H3.at[b], b, 2, s3, step, 2, {})

    def lon_pair(b, first, count, slot):
        rows = pl.ds(first, count)
        return (
            pltpu.make_async_remote_copy(
                src_ref=X.at[b, rows, 64:67], dst_ref=ST.at[b, 0, rows],
                send_sem=lon_s.at[slot, 0], recv_sem=lon_r.at[slot, 0],
                device_id={"lon": right}, device_id_type=MESH),
            pltpu.make_async_remote_copy(
                src_ref=X.at[b, rows, 3:6], dst_ref=ST.at[b, 1, rows],
                send_sem=lon_s.at[slot, 1], recv_sem=lon_r.at[slot, 1],
                device_id={"lon": left}, device_id_type=MESH),
        )

    def lon_halo(b, pair, first, count):
        with scope("lonwait"):
            for copy in pair:
                copy.wait()
        for row in range(first, first + count):
            for j in range(3):
                own = X[b, row, 64 + j].astype(F32)
                other = ST[b, 0, row, j].astype(F32)
                tile = jnp.where(strip == 0, pltpu.roll(other, 1, 0), pltpu.roll(own, 1, 0))
                X[b, row, j] = tile.astype(BF16)
                own = X[b, row, 3 + j].astype(F32)
                other = ST[b, 1, row, j].astype(F32)
                tile = jnp.where(
                    strip == STRIPS - 1,
                    pltpu.roll(other, STRIPS - 1, 0), pltpu.roll(own, STRIPS - 1, 0))
                X[b, row, 67 + j] = tile.astype(BF16)

    def both_ways(down, up):
        def start(*piece):
            @pl.when(has_down)
            def _():
                down(*piece).start()

            @pl.when(has_up)
            def _():
                up(*piece).start()

        def wait_recv(*piece):
            @pl.when(has_up)
            def _():
                down(*piece).wait_recv()

            @pl.when(has_down)
            def _():
                up(*piece).wait_recv()

        def wait_send(*piece):
            @pl.when(has_down)
            def _():
                down(*piece).wait_send()

            @pl.when(has_up)
            def _():
                up(*piece).wait_send()

        return start, wait_recv, wait_send

    def halo_ways(source, target, buffer, down_row, up_row, other_side, sends, recvs, base, skip):
        def direct(way, count, first, tiles, slot):
            at = up_row if way else down_row
            to = other_side if way else 0
            window = pl.ds(first, tiles)
            return pltpu.make_async_remote_copy(
                src_ref=source.at[pl.ds(at, count), window],
                dst_ref=target.at[pl.ds(to, count), window],
                send_sem=sends.at[way, slot], recv_sem=recvs.at[way, slot],
                device_id={"lat": lt + 1 - 2 * way}, device_id_type=MESH)

        def lend(way, first, tiles, slot):
            at = (up_row if way else down_row) + 2
            window = pl.ds(first, tiles)
            return pltpu.make_async_remote_copy(
                src_ref=source.at[at, window], dst_ref=buffer.at[window],
                send_sem=edge_s.at[base + slot], recv_sem=edge_r.at[base + slot],
                device_id={"lat": across}, device_id_type=MESH)

        def relay(way, first, tiles, slot):
            to = (other_side if way else 0) + 2
            window = pl.ds(first, tiles)
            return pltpu.make_async_remote_copy(
                src_ref=buffer.at[window], dst_ref=target.at[to, window],
                send_sem=edge_s.at[base + slot], recv_sem=edge_r.at[base + slot],
                device_id={"lat": wrap}, device_id_type=MESH)

        def plain(piece):
            return isinstance(piece[2], int) and piece[2] < skip

        def each(piece, down, down_split, up, up_split):
            if plain(piece):
                pl.when(has_down)(down)
                pl.when(has_up)(up)
                return
            pl.when(jnp.logical_and(has_down, lt != HALF - 1))(down)
            pl.when(lt == HALF - 1)(down_split)
            pl.when(jnp.logical_and(has_up, lt != HALF))(up)
            pl.when(lt == HALF)(up_split)

        def start(*piece):
            def split(way):
                direct(way, 2, *piece).start()
                lend(way, *piece).start()

            each(piece, lambda: direct(0, 3, *piece).start(), lambda: split(0),
                 lambda: direct(1, 3, *piece).start(), lambda: split(1))

        def forward(*piece):
            @pl.when(lt == LAT_DEVICES - 1)
            def _():
                lend(0, *piece).wait_recv()
                relay(0, *piece).start()

            @pl.when(lt == 0)
            def _():
                lend(1, *piece).wait_recv()
                relay(1, *piece).start()

        def wait_recv(*piece):
            def split(way):
                direct(way, 2, *piece).wait_recv()
                relay(way, *piece).wait_recv()

            each(piece, lambda: direct(1, 3, *piece).wait_recv(), lambda: split(1),
                 lambda: direct(0, 3, *piece).wait_recv(), lambda: split(0))

        def wait_send(*piece):
            def split(way):
                direct(way, 2, *piece).wait_send()
                lend(way, *piece).wait_send()

            each(piece, lambda: direct(0, 3, *piece).wait_send(), lambda: split(0),
                 lambda: direct(1, 3, *piece).wait_send(), lambda: split(1))
            if not plain(piece):
                @pl.when(lt == LAT_DEVICES - 1)
                def _():
                    relay(0, *piece).wait_send()

                @pl.when(lt == 0)
                def _():
                    relay(1, *piece).wait_send()

        return start, forward, wait_recv, wait_send

    def g_down():
        return pltpu.make_async_remote_copy(
            src_ref=G.at[0, core, :, :, CH:4 * CH], dst_ref=GH.at[0, core],
            send_sem=g_s.at[0], recv_sem=g_r.at[0],
            device_id={"lat": lt + 1}, device_id_type=MESH)

    def g_up():
        return pltpu.make_async_remote_copy(
            src_ref=G.at[0, core, :, :, 0:3 * CH], dst_ref=GH.at[1, core],
            send_sem=g_s.at[1], recv_sem=g_r.at[1],
            device_id={"lat": lt - 1}, device_id_type=MESH)

    def g_share(side, half):
        return pltpu.make_async_remote_copy(
            src_ref=GH.at[side, half], dst_ref=GH.at[side, half],
            send_sem=gf_s.at[side], recv_sem=gf_r.at[side],
            device_id={"lon": sibling}, device_id_type=MESH)

    def turned(load):
        his = []
        los = []
        for o in range(2):
            for ch in range(CHIPS):
                parts = []
                for value in load(o, ch):
                    re = value[0:8]
                    im = value[8:16]
                    new_re = re * cos - im * sin
                    new_im = re * sin + im * cos
                    if o == 1:
                        new_re = new_re * flip
                        new_im = new_im * flip
                    parts.append(jnp.concatenate([new_re, new_im], axis=0))
                hi, lo = split2(jnp.concatenate(parts, axis=1))
                his.append(hi)
                los.append(lo)
        hi = jnp.concatenate(his, axis=0)
        lo = jnp.concatenate(los, axis=0)
        return jnp.concatenate([hi, hi, lo], axis=0)

    def inverse(c, rhs):
        table = iv_v[...]
        lhs = jnp.concatenate([table, table[:, 0:256]], axis=1)
        return jnp.dot(lhs, rhs, preferred_element_type=F32)

    def result(c, l):
        return pltpu.make_async_copy(
            X.at[BLOCKS, 3 + l, pl.ds(3, 64)], out.at[l],
            in_sem.at[4 * c + l])

    x_pieces = ([(9, 11, 0)] + [(20 + 9 * k, 9, k + 1) for k in range(5)]
                + [(65, 5, 6), (0, 9, 7)])
    h_pieces = [(12, 14, 0), (26, 18, 1), (44, 14, 2), (58, 9, 3), (3, 9, 4)]
    x_start, x_forward, x_wait, x_done = halo_ways(
        X.at[0], X.at[0], RX, 4, 3, 7, lat_s, lat_r, -2, 2)
    h_start, h_forward, h_wait, h_done = halo_ways(
        H3.at[0], HH, RH, 1, 0, 3, h_s, h_r, 6, 0)
    g_start, g_wait, g_done = both_ways(g_down, g_up)

    def first_convolutions():
        x_start(*x_pieces[0])
        permute(20, 67)
        for piece in x_pieces[1:6]:
            x_start(*piece)
        permute(3, 9)
        pair = lon_pair(0, 3, 4, 0)
        for copy in pair:
            copy.start()
        lon_halo(0, pair, 3, 4)
        for piece in x_pieces[6:]:
            x_start(*piece)
        with scope("build"):
            build_weights()

        def chunk(k, _):
            @pl.when(k < 4)
            def _():
                x_forward(29 + 9 * k, 9, k + 2)

            for p in range(6, 8):
                @pl.when(k == p - 2)
                def _():
                    x_forward(*x_pieces[p])

            @pl.when(k == 6)
            def _():
                h_forward(*h_pieces[0])

            with scope("latwait"):
                @pl.when(k == 0)
                def _():
                    x_wait(*x_pieces[0])

                @pl.when(k == 1)
                def _():
                    x_wait(*x_pieces[1])

                @pl.when(jnp.logical_and(k > 1, k < 6))
                def _():
                    x_wait(11 + 9 * k, 9, k)

                @pl.when(k == 6)
                def _():
                    x_wait(*x_pieces[6])

                @pl.when(k == 7)
                def _():
                    x_wait(*x_pieces[7])

            for p in range(3):
                @pl.when(k == 2 * p + 2)
                def _():
                    h_start(*h_pieces[p])

            s1 = jnp.where(k < 6, 10 + 9 * k, jnp.where(k == 6, 60, 1))
            shift = jnp.where(k == 7, 1, -1)
            three(0, [s1], [s1 + shift], [s1 + 2 * shift], 9)
            return 0

        lax.fori_loop(0, 8, chunk, 0)

    def second_convolutions():
        own = lon_pair(1, 3, 4, 1)
        for copy in own:
            copy.start()
        with scope("gwait"):
            g_wait()
            for side, present in ((0, has_up), (1, has_down)):
                @pl.when(present)
                def _():
                    g_share(side, core).start()
        with scope("hwait"):
            for piece in h_pieces:
                h_wait(*piece)
        with scope("sharewait"):
            for side, present in ((0, has_up), (1, has_down)):
                @pl.when(present)
                def _():
                    g_share(side, 1 - core).wait_recv()
        rhs = turned(lambda o, ch: [
            GH[side, o, ch, :, l * CH:(l + 1) * CH].astype(F32)
            for side in range(2) for l in range(3)])

        def rows(c, _):
            spectral = inverse(c, rhs)
            tiles = pl.ds(3, 64)
            for side, present in ((0, has_up), (1, has_down)):
                @pl.when(present)
                def _():
                    for l in range(3):
                        x = X[0, 7 * side + l, tiles].reshape(1024, CH).astype(F32)
                        h = HH[3 * side + l, tiles].reshape(1024, CH).astype(F32)
                        lanes = slice((3 * side + l) * CH, (3 * side + l + 1) * CH)
                        value = jnp.tanh(x + h + spectral[:, lanes])
                        X[1, 7 * side + l, tiles] = value.astype(BF16).reshape(64, STRIPS, CH)
            return 0

        with scope("halorows"):
            rows(0, 0)
        top = lon_pair(1, 0, 3, 2)
        bottom = lon_pair(1, 7, 3, 3)
        for copy in top + bottom:
            copy.start()

        def chunk(c, _):
            @pl.when(c == 1)
            def _():
                lon_halo(1, own, 3, 4)
                lon_halo(1, top, 0, 3)
                lon_halo(1, bottom, 7, 3)

            first = 18 + 34 * c
            second = 35 - 34 * c
            shift = 2 * c - 1
            three(1, [first, second], [first - 1, second + shift],
                  [first - 2, second + 2 * shift], STEP)
            return 0

        lax.fori_loop(0, 2, chunk, 0)

    def spectral_part(b):
        with scope("dft"):
            for half in range(2):
                rhs = jnp.concatenate(
                    [H3[b, 2 * half + l, 3:67].reshape(COLS, CH) for l in range(2)], axis=1)
                both = jnp.dot(ft_v[...], rhs, preferred_element_type=F32)
                total = both[0:256] + both[256:512]
                for o in range(2):
                    for ch in range(CHIPS):
                        first = (o * CHIPS + ch) * 16
                        for l in range(2):
                            re = total[first:first + 8, l * CH:(l + 1) * CH]
                            im = total[first + 8:first + 16, l * CH:(l + 1) * CH]
                            new_re = re * cos + im * sin
                            new_im = im * cos - re * sin
                            if o == 1:
                                new_re = new_re * flip
                                new_im = new_im * flip
                            lanes = pl.ds((2 * half + l) * CH, CH)
                            PART[o, ch, 0:8, lanes] = new_re
                            PART[o, ch, 8:16, lanes] = new_im

        if b == 0:
            h_start(*h_pieces[3])
            h_start(*h_pieces[4])
            h_forward(*h_pieces[1])
        swap = pltpu.make_async_remote_copy(
            src_ref=PART.at[1 - core], dst_ref=DR.at[b],
            send_sem=d_s.at[0], recv_sem=d_r.at[b],
            device_id={"lon": sibling}, device_id_type=MESH)
        swap.start()
        with scope("swapwait"):
            swap.wait()
        RSEND[...] = PART[core] + DR[b]

        def scatter(dz, dx):
            peer = peer_at(dz, dx)
            return pltpu.make_async_remote_copy(
                src_ref=RSEND.at[peer], dst_ref=RRECV.at[b, 4 * dz + dx - 1],
                send_sem=rs_s.at[0], recv_sem=rs_r.at[b],
                device_id={"lon": peer * 2 + core}, device_id_type=MESH)

        for where in PEERS:
            scatter(*where).start()
        spectrum = RSEND[chip]
        if b == 1:
            for piece in x_pieces:
                x_done(*piece)
            for piece in h_pieces:
                h_done(*piece)
            g_done()
            for side, present in ((0, has_up), (1, has_down)):
                @pl.when(present)
                def _():
                    g_share(side, core).wait_send()
        with scope("rswait"):
            pltpu.make_async_remote_copy(
                src_ref=RSEND.at[0:CHIPS - 1], dst_ref=RRECV.at[b],
                send_sem=rs_s.at[0], recv_sem=rs_r.at[b],
                device_id={"lon": sibling}, device_id_type=MESH).wait()
        for j in range(1, CHIPS):
            spectrum = spectrum + RRECV[b, j - 1]

        if b == 0:
            for piece in h_pieces[2:]:
                h_forward(*piece)
        with scope("mix"):
            lhs = jnp.concatenate(
                [jnp.concatenate([spectrum[0:8, l * CH:(l + 1) * CH],
                                  spectrum[8:16, l * CH:(l + 1) * CH]], axis=1)
                 for l in range(ROWS)], axis=0)
            lhs = jnp.concatenate(split2(lhs), axis=0)
            mixed = jnp.zeros((ROWS * OWNED, 2 * CH), F32)
            for m in range(OWNED):
                both = jnp.dot(lhs, SW[b * OWNED + m], preferred_element_type=F32)
                mixed = jnp.where(sub == m, both[0:32] + both[32:64], mixed)
            for l in range(ROWS):
                G[b, core, chip, :, l * CH:(l + 1) * CH] = jnp.concatenate(
                    [mixed[8 * l:8 * l + 8, 0:CH], mixed[8 * l:8 * l + 8, CH:2 * CH]], axis=0
                ).astype(BF16)

        def gather(dz, dx):
            return pltpu.make_async_remote_copy(
                src_ref=G.at[b, core, chip], dst_ref=G.at[b, core, chip],
                send_sem=ag_s.at[0], recv_sem=ag_r.at[b],
                device_id={"lon": peer_at(dz, dx) * 2 + core}, device_id_type=MESH)

        for where in PEERS:
            gather(*where).start()

        gathered = pltpu.make_async_remote_copy(
            src_ref=G.at[b, core, 0:CHIPS - 1], dst_ref=G.at[b, core, 0:CHIPS - 1],
            send_sem=ag_s.at[0], recv_sem=ag_r.at[b],
            device_id={"lon": sibling}, device_id_type=MESH)
        with scope("agwait"):
            gathered.wait_recv()
        forward = pltpu.make_async_remote_copy(
            src_ref=G.at[b, core], dst_ref=G.at[b, core],
            send_sem=fw_s.at[0], recv_sem=fw_r.at[b],
            device_id={"lon": sibling}, device_id_type=MESH)
        forward.start()
        if b == 0:
            g_start()
        back = pltpu.make_async_remote_copy(
            src_ref=G.at[b, 1 - core], dst_ref=G.at[b, 1 - core],
            send_sem=fw_s.at[0], recv_sem=fw_r.at[b],
            device_id={"lon": sibling}, device_id_type=MESH)
        with scope("fwwait"):
            back.wait_recv()

        rhs = turned(lambda o, ch: [
            G[b, o, ch, :, l * CH:(l + 1) * CH].astype(F32) for l in range(ROWS)])

        def finish(c, _):
            spectral = inverse(c, rhs)
            for l in range(ROWS):
                x = X[b, 3 + l, pl.ds(3, 64)].reshape(1024, CH).astype(F32)
                h = H3[b, l, pl.ds(3, 64)].reshape(1024, CH).astype(F32)
                value = jnp.tanh(x + h + spectral[:, l * CH:(l + 1) * CH])
                X[b + 1, 3 + l, pl.ds(3, 64)] = value.astype(BF16).reshape(
                    64, STRIPS, CH)
                if b == BLOCKS - 1:
                    result(c, l).start()


            return 0

        with scope("finish"):
            finish(0, 0)

        gathered.wait_send()
        forward.wait_send()

    first_convolutions()
    spectral_part(0)
    second_convolutions()
    spectral_part(1)

    with scope("store"):
        for c in range(1):
            for l in range(ROWS):
                result(c, l).wait()


def restore(strips):
    return jnp.transpose(strips, (0, 2, 1, 3)).reshape(ROWS, COLS, CH)


def per_device(field, conv_weight, conv_bias, spec_real, spec_imag):
    forward, inverse, turn = tables()
    args = (field, conv_weight, jnp.transpose(conv_bias, (1, 0, 2)), spec_real, spec_imag,
            jnp.asarray(forward), jnp.asarray(inverse), jnp.asarray(turn))
    tile = (STRIPS, CH)
    dma = pltpu.SemaphoreType.DMA
    strips = pl.pallas_call(
        kernel,
        out_shape=jax.ShapeDtypeStruct((ROWS, TILES) + tile, BF16),
        in_specs=[pl.BlockSpec(memory_space=pl.ANY)] * len(args),
        out_specs=pl.BlockSpec(memory_space=pl.ANY),
        scratch_shapes=[pltpu.VMEM(a.shape, a.dtype) for a in args] + [
            pltpu.VMEM((BLOCKS * CONVS, 12 * CH, 2 * CH), BF16),
            pltpu.VMEM((BLOCKS * OWNED, 2 * CH, 2 * CH), BF16),
            pltpu.VMEM((BLOCKS + 1, 10, EXT) + tile, BF16),
            pltpu.VMEM((8, EXT) + tile, BF16),
            pltpu.VMEM((6, EXT) + tile, BF16),
            pltpu.VMEM((BLOCKS, 4, EXT) + tile, BF16),
            pltpu.VMEM((BLOCKS, 2, 10, 3) + tile, BF16),
            pltpu.VMEM((ROWS, COLS, CH), F32),
            pltpu.VMEM((2, CHIPS, 16, ROWS * CH), F32),
            pltpu.VMEM((BLOCKS, CHIPS, 16, ROWS * CH), F32),
            pltpu.VMEM((CHIPS, 16, ROWS * CH), F32),
            pltpu.VMEM((BLOCKS, CHIPS - 1, 16, ROWS * CH), F32),
            pltpu.VMEM((BLOCKS, 2, CHIPS, 16, ROWS * CH), BF16),
            pltpu.VMEM((6, EXT) + tile, BF16),
            pltpu.VMEM((2, 2, CHIPS, 16, 3 * CH), BF16),
            dma((8,)), dma((4, 2)), dma((4, 2)), dma((2, 8)), dma((2, 8)),
            dma((1,)), dma((BLOCKS,)),
            dma((1,)), dma((BLOCKS,)), dma((1,)), dma((BLOCKS,)),
            dma((1,)), dma((BLOCKS,)),
            dma((2, 5)), dma((2, 5)), dma((2,)), dma((2,)), dma((2,)), dma((2,)),
            pltpu.VMEM((EXT,) + tile, BF16), pltpu.VMEM((EXT,) + tile, BF16),
            dma((11,)), dma((11,)),
        ],
        compiler_params=pltpu.CompilerParams(
            collective_id=0, has_side_effects=True, vmem_limit_bytes=62 * 1024 * 1024),
    )(*args)
    return restore(strips)


def solution(mesh):
    return jax.shard_map(
        per_device,
        mesh=mesh,
        in_specs=(
            P("lat", "lon", None),
            P(),
            P(),
            P(None, "lon", None, None),
            P(None, "lon", None, None),
        ),
        out_specs=P("lat", "lon", None),
        check_vma=False,
    )
```

```python
import contextlib

import jax
import jax.numpy as jnp
import numpy as np
from jax import lax
from jax.experimental import pallas as pl
from jax.experimental.pallas import tpu as pltpu
from jax.sharding import PartitionSpec as P

BLOCKS = 2
CONVS = 3
LON_DEVICES = 16
LAT_DEVICES = 8
HALF = 4
CHIPS = 8
COLS = 1024
STRIPS = 16
TILES = 64
ROWS = 4
CH = 128
OWNED = 8
EXT = 70
STEP = 17
PEERS = ((1, 2), (0, 2), (1, 1), (1, 3), (0, 1), (0, 3), (1, 0))
F32 = jnp.float32
BF16 = jnp.bfloat16
MESH = pl.DeviceIdType.MESH


def scope(name):
    return contextlib.nullcontext()


def tables():
    total = LON_DEVICES * COLS
    tile, strip = np.meshgrid(np.arange(TILES), np.arange(STRIPS), indexing="ij")
    cell = (strip * TILES + tile).reshape(-1)
    core, chip, part, low = np.meshgrid(
        np.arange(2), np.arange(CHIPS), np.arange(2), np.arange(OWNED), indexing="ij"
    )
    mode = (OWNED * (2 * chip + core) + low).reshape(-1)
    part = part.reshape(-1)
    theta = 2.0 * np.pi / total * ((mode[:, None] * cell[None, :]) % total)
    full = np.where(part[:, None] == 0, np.cos(theta), -np.sin(theta))
    weight = np.where(mode == 0, 1.0, 2.0)[:, None] / total

    def split(table):
        table = table.astype(np.float32)
        hi = table.astype(jnp.bfloat16)
        return hi, (table - hi.astype(np.float32)).astype(jnp.bfloat16)

    forward = np.concatenate(split(full), axis=0)
    inverse = np.concatenate(split((full * weight).T), axis=1)
    phi = 2.0 * np.pi / 16.0 * ((np.arange(16)[:, None] * np.arange(OWNED)[None, :]) % 16)
    turn = np.stack([np.cos(phi), np.sin(phi)], axis=1).astype(np.float32)
    turn = np.broadcast_to(turn[..., None], (16, 2, OWNED, CH)).copy()
    return forward, inverse, turn


def split2(value):
    hi = value.astype(BF16)
    return hi, (value - hi.astype(F32)).astype(BF16)


def kernel(field, cw, cb, sr, si, ft, iv, tw, out,
           f_v, cw_v, cb_v, sr_v, si_v, ft_v, iv_v, tw_v, T, SW, X, H1, H2, H3, ST, S,
           PART, DR, RSEND, RRECV, G, HH, GH,
           in_sem, lon_s, lon_r, lat_s, lat_r, d_s, d_r, rs_s, rs_r, ag_s, ag_r, fw_s, fw_r,
           h_s, h_r, g_s, g_r, gf_s, gf_r,
           RX, RH, edge_s, edge_r):
    d = lax.axis_index("lon")
    lt = lax.axis_index("lat")
    core = lax.rem(d, 2)
    chip = lax.div(d, 2)
    sibling = chip * 2 + 1 - core
    right = lax.rem(d + 1, LON_DEVICES)
    left = lax.rem(d + LON_DEVICES - 1, LON_DEVICES)
    outer = jnp.where(core == 0, left, right)
    across = lax.rem(lt + HALF, LAT_DEVICES)
    wrap = jnp.where(lt < HALF, HALF - 1 - lt, 3 * HALF - 1 - lt)
    outermost = jnp.logical_or(lax.rem(lt, HALF) == 0, lax.rem(lt, HALF) == HALF - 1)
    has_up = lt > 0
    has_down = lt < LAT_DEVICES - 1

    loads = [
        pltpu.make_async_copy(src, dst, in_sem.at[i])
        for i, (src, dst) in enumerate(
            [(field, f_v), (cw, cw_v), (cb, cb_v), (sr, sr_v), (si, si_v), (ft, ft_v),
             (iv, iv_v), (tw, tw_v)]
        )
    ]
    for load in loads:
        load.start()

    barrier = pltpu.get_barrier_semaphore()
    pl.semaphore_signal(barrier, inc=1, device_id={"lon": sibling}, device_id_type=MESH)
    pl.semaphore_signal(barrier, inc=1, device_id={"lon": outer}, device_id_type=MESH)

    def peer_at(dz, dx):
        z = lax.div(chip, 4)
        return (1 - z if dz else z) * 4 + lax.rem(chip + dx, 4)

    for where in PEERS:
        pl.semaphore_signal(
            barrier, inc=1, device_id={"lon": peer_at(*where) * 2 + core}, device_id_type=MESH)

    @pl.when(has_up)
    def _():
        pl.semaphore_signal(barrier, inc=1, device_id={"lat": lt - 1}, device_id_type=MESH)

    @pl.when(has_down)
    def _():
        pl.semaphore_signal(barrier, inc=1, device_id={"lat": lt + 1}, device_id_type=MESH)

    @pl.when(outermost)
    def _():
        pl.semaphore_signal(barrier, inc=1, device_id={"lat": across}, device_id_type=MESH)
        pl.semaphore_signal(barrier, inc=1, device_id={"lat": wrap}, device_id_type=MESH)

    @pl.when(jnp.logical_not(has_up))
    def _():
        for b in range(BLOCKS):
            X[b, 0:3] = jnp.zeros((3, EXT, STRIPS, CH), BF16)

    @pl.when(jnp.logical_not(has_down))
    def _():
        for b in range(BLOCKS):
            X[b, 7:10] = jnp.zeros((3, EXT, STRIPS, CH), BF16)

    def permute(first, last):
        for row in range(ROWS):
            for t in range(first, last):
                X[0, 3 + row, t] = S[row, pl.ds(t - 3, STRIPS, stride=TILES), :].astype(BF16)

    with scope("permute_in"):
        loads[0].wait()
        for row in range(ROWS):
            S[row] = f_v[row].astype(F32)
        permute(9, 20)
    with scope("barrier"):
        pl.semaphore_wait(
            barrier, CHIPS + 1 + has_up.astype(jnp.int32) + has_down.astype(jnp.int32)
            + 2 * outermost.astype(jnp.int32)
        )

    def build_weights():
        loads[1].wait()
        loads[2].wait()
        zero = jnp.zeros((CH, CH), BF16)

        def build(i, _):
            b = lax.div(i, CONVS)
            layer = lax.rem(i, CONVS)
            for tap in range(3):
                w0, w1, w2 = (cw_v[b, layer, a, tap] for a in range(3))
                for r, (first, second) in enumerate(((w0, zero), (w1, w0), (w2, w1), (zero, w2))):
                    rows = pl.ds((tap * 4 + r) * CH, CH)
                    T[i, rows, 0:CH] = first
                    T[i, rows, CH:2 * CH] = second
            return 0

        lax.fori_loop(0, BLOCKS * CONVS, build, 0)

        loads[3].wait()
        loads[4].wait()

        def build_spec(i, _):
            b = lax.div(i, OWNED)
            m = lax.rem(i, OWNED)
            wr = sr_v[b, m]
            wi = si_v[b, m]
            SW[i, 0:CH, 0:CH] = wr
            SW[i, 0:CH, CH:2 * CH] = wi
            SW[i, CH:2 * CH, 0:CH] = -wi
            SW[i, CH:2 * CH, CH:2 * CH] = wr
            return 0

        lax.fori_loop(0, BLOCKS * OWNED, build_spec, 0)
        for load in loads[5:7]:
            load.wait()

    loads[7].wait()
    cos = tw_v[d, 0]
    sin = tw_v[d, 1]
    flip = (1 - 2 * core).astype(F32)
    up_mask = has_up.astype(F32)
    down_mask = has_down.astype(F32)
    strip = lax.broadcasted_iota(jnp.int32, (STRIPS, CH), 0)
    sub = lax.rem(lax.broadcasted_iota(jnp.int32, (ROWS * OWNED, 2 * CH), 0), OWNED)

    def convolve(source, target, b, layer, starts, step, pairs, masks):
        bias = cb_v[layer, b:b + 1, :]
        size = step * STRIPS
        for pair in range(pairs):
            lhs = jnp.concatenate(
                [jnp.concatenate(
                    [source(2 * pair + r, start - 1 + tap).reshape(size, CH)
                     for start in starts], axis=0)
                 for tap in range(3) for r in range(4)], axis=1)
            total = jnp.dot(lhs, T[b * CONVS + layer], preferred_element_type=F32)
            for o in range(2):
                half = 0.5 * (total[:, o * CH:(o + 1) * CH] + bias)
                value = half * jnp.tanh(half) + half
                mask = masks.get(2 * pair + o)
                if mask is not None:
                    value = value * mask
                value = value.astype(BF16)
                for i, start in enumerate(starts):
                    target[2 * pair + o, pl.ds(start, step)] = value[
                        i * size:(i + 1) * size].reshape(step, STRIPS, CH)

    def three(b, s1, s2, s3, step):
        with scope("conv"):
            convolve(lambda r, t: X[b, r, pl.ds(t, step)], H1, b, 0, s1, step, 4,
                     {0: up_mask, 1: up_mask, 6: down_mask, 7: down_mask})
            convolve(lambda r, t: H1[r, pl.ds(t, step)], H2, b, 1, s2, step, 3,
                     {0: up_mask, 5: down_mask})
            convolve(lambda r, t: H2[r, pl.ds(t, step)], H3.at[b], b, 2, s3, step, 2, {})

    def lon_pair(b, first, count, slot):
        rows = pl.ds(first, count)
        return (
            pltpu.make_async_remote_copy(
                src_ref=X.at[b, rows, 64:67], dst_ref=ST.at[b, 0, rows],
                send_sem=lon_s.at[slot, 0], recv_sem=lon_r.at[slot, 0],
                device_id={"lon": right}, device_id_type=MESH),
            pltpu.make_async_remote_copy(
                src_ref=X.at[b, rows, 3:6], dst_ref=ST.at[b, 1, rows],
                send_sem=lon_s.at[slot, 1], recv_sem=lon_r.at[slot, 1],
                device_id={"lon": left}, device_id_type=MESH),
        )

    def lon_halo(b, pair, first, count):
        with scope("lonwait"):
            for copy in pair:
                copy.wait()
        for row in range(first, first + count):
            for j in range(3):
                own = X[b, row, 64 + j].astype(F32)
                other = ST[b, 0, row, j].astype(F32)
                tile = jnp.where(strip == 0, pltpu.roll(other, 1, 0), pltpu.roll(own, 1, 0))
                X[b, row, j] = tile.astype(BF16)
                own = X[b, row, 3 + j].astype(F32)
                other = ST[b, 1, row, j].astype(F32)
                tile = jnp.where(
                    strip == STRIPS - 1,
                    pltpu.roll(other, STRIPS - 1, 0), pltpu.roll(own, STRIPS - 1, 0))
                X[b, row, 67 + j] = tile.astype(BF16)

    def both_ways(down, up):
        def start(*piece):
            @pl.when(has_down)
            def _():
                down(*piece).start()

            @pl.when(has_up)
            def _():
                up(*piece).start()

        def wait_recv(*piece):
            @pl.when(has_up)
            def _():
                down(*piece).wait_recv()

            @pl.when(has_down)
            def _():
                up(*piece).wait_recv()

        def wait_send(*piece):
            @pl.when(has_down)
            def _():
                down(*piece).wait_send()

            @pl.when(has_up)
            def _():
                up(*piece).wait_send()

        return start, wait_recv, wait_send

    def halo_ways(source, target, buffer, down_row, up_row, other_side, sends, recvs, base, skip):
        def direct(way, count, first, tiles, slot):
            at = up_row if way else down_row
            to = other_side if way else 0
            window = pl.ds(first, tiles)
            return pltpu.make_async_remote_copy(
                src_ref=source.at[pl.ds(at, count), window],
                dst_ref=target.at[pl.ds(to, count), window],
                send_sem=sends.at[way, slot], recv_sem=recvs.at[way, slot],
                device_id={"lat": lt + 1 - 2 * way}, device_id_type=MESH)

        def lend(way, first, tiles, slot):
            at = (up_row if way else down_row) + 2
            window = pl.ds(first, tiles)
            return pltpu.make_async_remote_copy(
                src_ref=source.at[at, window], dst_ref=buffer.at[window],
                send_sem=edge_s.at[base + slot], recv_sem=edge_r.at[base + slot],
                device_id={"lat": across}, device_id_type=MESH)

        def relay(way, first, tiles, slot):
            to = (other_side if way else 0) + 2
            window = pl.ds(first, tiles)
            return pltpu.make_async_remote_copy(
                src_ref=buffer.at[window], dst_ref=target.at[to, window],
                send_sem=edge_s.at[base + slot], recv_sem=edge_r.at[base + slot],
                device_id={"lat": wrap}, device_id_type=MESH)

        def plain(piece):
            return isinstance(piece[2], int) and piece[2] < skip

        def each(piece, down, down_split, up, up_split):
            if plain(piece):
                pl.when(has_down)(down)
                pl.when(has_up)(up)
                return
            pl.when(jnp.logical_and(has_down, lt != HALF - 1))(down)
            pl.when(lt == HALF - 1)(down_split)
            pl.when(jnp.logical_and(has_up, lt != HALF))(up)
            pl.when(lt == HALF)(up_split)

        def start(*piece):
            def split(way):
                direct(way, 2, *piece).start()
                lend(way, *piece).start()

            each(piece, lambda: direct(0, 3, *piece).start(), lambda: split(0),
                 lambda: direct(1, 3, *piece).start(), lambda: split(1))

        def forward(*piece):
            @pl.when(lt == LAT_DEVICES - 1)
            def _():
                lend(0, *piece).wait_recv()
                relay(0, *piece).start()

            @pl.when(lt == 0)
            def _():
                lend(1, *piece).wait_recv()
                relay(1, *piece).start()

        def wait_recv(*piece):
            def split(way):
                direct(way, 2, *piece).wait_recv()
                relay(way, *piece).wait_recv()

            each(piece, lambda: direct(1, 3, *piece).wait_recv(), lambda: split(1),
                 lambda: direct(0, 3, *piece).wait_recv(), lambda: split(0))

        def wait_send(*piece):
            def split(way):
                direct(way, 2, *piece).wait_send()
                lend(way, *piece).wait_send()

            each(piece, lambda: direct(0, 3, *piece).wait_send(), lambda: split(0),
                 lambda: direct(1, 3, *piece).wait_send(), lambda: split(1))
            if not plain(piece):
                @pl.when(lt == LAT_DEVICES - 1)
                def _():
                    relay(0, *piece).wait_send()

                @pl.when(lt == 0)
                def _():
                    relay(1, *piece).wait_send()

        return start, forward, wait_recv, wait_send

    def g_down():
        return pltpu.make_async_remote_copy(
            src_ref=G.at[0, core, :, :, CH:4 * CH], dst_ref=GH.at[0, core],
            send_sem=g_s.at[0], recv_sem=g_r.at[0],
            device_id={"lat": lt + 1}, device_id_type=MESH)

    def g_up():
        return pltpu.make_async_remote_copy(
            src_ref=G.at[0, core, :, :, 0:3 * CH], dst_ref=GH.at[1, core],
            send_sem=g_s.at[1], recv_sem=g_r.at[1],
            device_id={"lat": lt - 1}, device_id_type=MESH)

    def g_share(side, half):
        return pltpu.make_async_remote_copy(
            src_ref=GH.at[side, half], dst_ref=GH.at[side, half],
            send_sem=gf_s.at[side], recv_sem=gf_r.at[side],
            device_id={"lon": sibling}, device_id_type=MESH)

    def turned(load):
        his = []
        los = []
        for o in range(2):
            for ch in range(CHIPS):
                parts = []
                for value in load(o, ch):
                    re = value[0:8]
                    im = value[8:16]
                    new_re = re * cos - im * sin
                    new_im = re * sin + im * cos
                    if o == 1:
                        new_re = new_re * flip
                        new_im = new_im * flip
                    parts.append(jnp.concatenate([new_re, new_im], axis=0))
                hi, lo = split2(jnp.concatenate(parts, axis=1))
                his.append(hi)
                los.append(lo)
        hi = jnp.concatenate(his, axis=0)
        lo = jnp.concatenate(los, axis=0)
        return jnp.concatenate([hi, hi, lo], axis=0)

    def inverse(c, rhs):
        table = iv_v[pl.ds(c * 512, 512), :]
        lhs = jnp.concatenate([table, table[:, 0:256]], axis=1)
        return jnp.dot(lhs, rhs, preferred_element_type=F32)

    def result(c):
        return pltpu.make_async_copy(
            X.at[BLOCKS, 3:7, pl.ds(3 + 32 * c, 32)], out.at[:, pl.ds(32 * c, 32)], in_sem.at[c])

    x_pieces = ([(9, 11, 0)] + [(20 + 9 * k, 9, k + 1) for k in range(5)]
                + [(65, 5, 6), (0, 9, 7)])
    h_pieces = [(12, 14, 0), (26, 18, 1), (44, 14, 2), (58, 9, 3), (3, 9, 4)]
    x_start, x_forward, x_wait, x_done = halo_ways(
        X.at[0], X.at[0], RX, 4, 3, 7, lat_s, lat_r, -2, 2)
    h_start, h_forward, h_wait, h_done = halo_ways(
        H3.at[0], HH, RH, 1, 0, 3, h_s, h_r, 6, 0)
    g_start, g_wait, g_done = both_ways(g_down, g_up)

    def first_convolutions():
        x_start(*x_pieces[0])
        permute(20, 67)
        for piece in x_pieces[1:6]:
            x_start(*piece)
        permute(3, 9)
        pair = lon_pair(0, 3, 4, 0)
        for copy in pair:
            copy.start()
        lon_halo(0, pair, 3, 4)
        for piece in x_pieces[6:]:
            x_start(*piece)
        with scope("build"):
            build_weights()

        def chunk(k, _):
            @pl.when(k < 4)
            def _():
                x_forward(29 + 9 * k, 9, k + 2)

            for p in range(6, 8):
                @pl.when(k == p - 2)
                def _():
                    x_forward(*x_pieces[p])

            @pl.when(k == 6)
            def _():
                h_forward(*h_pieces[0])

            with scope("latwait"):
                @pl.when(k == 0)
                def _():
                    x_wait(*x_pieces[0])

                @pl.when(k == 1)
                def _():
                    x_wait(*x_pieces[1])

                @pl.when(jnp.logical_and(k > 1, k < 6))
                def _():
                    x_wait(11 + 9 * k, 9, k)

                @pl.when(k == 6)
                def _():
                    x_wait(*x_pieces[6])

                @pl.when(k == 7)
                def _():
                    x_wait(*x_pieces[7])

            for p in range(3):
                @pl.when(k == 2 * p + 2)
                def _():
                    h_start(*h_pieces[p])

            s1 = jnp.where(k < 6, 10 + 9 * k, jnp.where(k == 6, 60, 1))
            shift = jnp.where(k == 7, 1, -1)
            three(0, [s1], [s1 + shift], [s1 + 2 * shift], 9)
            return 0

        lax.fori_loop(0, 8, chunk, 0)

    def second_convolutions():
        own = lon_pair(1, 3, 4, 1)
        for copy in own:
            copy.start()
        with scope("gwait"):
            g_wait()
            for side, present in ((0, has_up), (1, has_down)):
                @pl.when(present)
                def _():
                    g_share(side, core).start()
        with scope("hwait"):
            for piece in h_pieces:
                h_wait(*piece)
        with scope("sharewait"):
            for side, present in ((0, has_up), (1, has_down)):
                @pl.when(present)
                def _():
                    g_share(side, 1 - core).wait_recv()
        rhs = turned(lambda o, ch: [
            GH[side, o, ch, :, l * CH:(l + 1) * CH].astype(F32)
            for side in range(2) for l in range(3)])

        def rows(c, _):
            spectral = inverse(c, rhs)
            tiles = pl.ds(3 + 32 * c, 32)
            for side, present in ((0, has_up), (1, has_down)):
                @pl.when(present)
                def _():
                    for l in range(3):
                        x = X[0, 7 * side + l, tiles].reshape(512, CH).astype(F32)
                        h = HH[3 * side + l, tiles].reshape(512, CH).astype(F32)
                        lanes = slice((3 * side + l) * CH, (3 * side + l + 1) * CH)
                        value = jnp.tanh(x + h + spectral[:, lanes])
                        X[1, 7 * side + l, tiles] = value.astype(BF16).reshape(32, STRIPS, CH)
            return 0

        with scope("halorows"):
            lax.fori_loop(0, 2, rows, 0)
        top = lon_pair(1, 0, 3, 2)
        bottom = lon_pair(1, 7, 3, 3)
        for copy in top + bottom:
            copy.start()

        def chunk(c, _):
            @pl.when(c == 1)
            def _():
                lon_halo(1, own, 3, 4)
                lon_halo(1, top, 0, 3)
                lon_halo(1, bottom, 7, 3)

            first = 18 + 34 * c
            second = 35 - 34 * c
            shift = 2 * c - 1
            three(1, [first, second], [first - 1, second + shift],
                  [first - 2, second + 2 * shift], STEP)
            return 0

        lax.fori_loop(0, 2, chunk, 0)

    def spectral_part(b):
        with scope("dft"):
            for half in range(2):
                rhs = jnp.concatenate(
                    [H3[b, 2 * half + l, 3:67].reshape(COLS, CH) for l in range(2)], axis=1)
                both = jnp.dot(ft_v[...], rhs, preferred_element_type=F32)
                total = both[0:256] + both[256:512]
                for o in range(2):
                    for ch in range(CHIPS):
                        first = (o * CHIPS + ch) * 16
                        for l in range(2):
                            re = total[first:first + 8, l * CH:(l + 1) * CH]
                            im = total[first + 8:first + 16, l * CH:(l + 1) * CH]
                            new_re = re * cos + im * sin
                            new_im = im * cos - re * sin
                            if o == 1:
                                new_re = new_re * flip
                                new_im = new_im * flip
                            lanes = pl.ds((2 * half + l) * CH, CH)
                            PART[o, ch, 0:8, lanes] = new_re
                            PART[o, ch, 8:16, lanes] = new_im

        if b == 0:
            h_start(*h_pieces[3])
            h_start(*h_pieces[4])
            h_forward(*h_pieces[1])
        swap = pltpu.make_async_remote_copy(
            src_ref=PART.at[1 - core], dst_ref=DR.at[b],
            send_sem=d_s.at[0], recv_sem=d_r.at[b],
            device_id={"lon": sibling}, device_id_type=MESH)
        swap.start()
        with scope("swapwait"):
            swap.wait()
        RSEND[...] = PART[core] + DR[b]

        def scatter(dz, dx):
            peer = peer_at(dz, dx)
            return pltpu.make_async_remote_copy(
                src_ref=RSEND.at[peer], dst_ref=RRECV.at[b, 4 * dz + dx - 1],
                send_sem=rs_s.at[0], recv_sem=rs_r.at[b],
                device_id={"lon": peer * 2 + core}, device_id_type=MESH)

        for where in PEERS:
            scatter(*where).start()
        spectrum = RSEND[chip]
        if b == 1:
            for piece in x_pieces:
                x_done(*piece)
            for piece in h_pieces:
                h_done(*piece)
            g_done()
            for side, present in ((0, has_up), (1, has_down)):
                @pl.when(present)
                def _():
                    g_share(side, core).wait_send()
        with scope("rswait"):
            pltpu.make_async_remote_copy(
                src_ref=RSEND.at[0:CHIPS - 1], dst_ref=RRECV.at[b],
                send_sem=rs_s.at[0], recv_sem=rs_r.at[b],
                device_id={"lon": sibling}, device_id_type=MESH).wait()
        for j in range(1, CHIPS):
            spectrum = spectrum + RRECV[b, j - 1]

        if b == 0:
            for piece in h_pieces[2:]:
                h_forward(*piece)
        with scope("mix"):
            lhs = jnp.concatenate(
                [jnp.concatenate([spectrum[0:8, l * CH:(l + 1) * CH],
                                  spectrum[8:16, l * CH:(l + 1) * CH]], axis=1)
                 for l in range(ROWS)], axis=0)
            lhs = jnp.concatenate(split2(lhs), axis=0)
            mixed = jnp.zeros((ROWS * OWNED, 2 * CH), F32)
            for m in range(OWNED):
                both = jnp.dot(lhs, SW[b * OWNED + m], preferred_element_type=F32)
                mixed = jnp.where(sub == m, both[0:32] + both[32:64], mixed)
            for l in range(ROWS):
                G[b, core, chip, :, l * CH:(l + 1) * CH] = jnp.concatenate(
                    [mixed[8 * l:8 * l + 8, 0:CH], mixed[8 * l:8 * l + 8, CH:2 * CH]], axis=0
                ).astype(BF16)

        def gather(dz, dx):
            return pltpu.make_async_remote_copy(
                src_ref=G.at[b, core, chip], dst_ref=G.at[b, core, chip],
                send_sem=ag_s.at[0], recv_sem=ag_r.at[b],
                device_id={"lon": peer_at(dz, dx) * 2 + core}, device_id_type=MESH)

        for where in PEERS:
            gather(*where).start()

        gathered = pltpu.make_async_remote_copy(
            src_ref=G.at[b, core, 0:CHIPS - 1], dst_ref=G.at[b, core, 0:CHIPS - 1],
            send_sem=ag_s.at[0], recv_sem=ag_r.at[b],
            device_id={"lon": sibling}, device_id_type=MESH)
        with scope("agwait"):
            gathered.wait_recv()
        forward = pltpu.make_async_remote_copy(
            src_ref=G.at[b, core], dst_ref=G.at[b, core],
            send_sem=fw_s.at[0], recv_sem=fw_r.at[b],
            device_id={"lon": sibling}, device_id_type=MESH)
        if b == 0:
            g_start()
        forward.start()
        back = pltpu.make_async_remote_copy(
            src_ref=G.at[b, 1 - core], dst_ref=G.at[b, 1 - core],
            send_sem=fw_s.at[0], recv_sem=fw_r.at[b],
            device_id={"lon": sibling}, device_id_type=MESH)
        with scope("fwwait"):
            back.wait_recv()

        rhs = turned(lambda o, ch: [
            G[b, o, ch, :, l * CH:(l + 1) * CH].astype(F32) for l in range(ROWS)])

        def finish(c, _):
            spectral = inverse(c, rhs)
            for l in range(ROWS):
                x = X[b, 3 + l, pl.ds(3 + 32 * c, 32)].reshape(512, CH).astype(F32)
                h = H3[b, l, pl.ds(3 + 32 * c, 32)].reshape(512, CH).astype(F32)
                value = jnp.tanh(x + h + spectral[:, l * CH:(l + 1) * CH])
                X[b + 1, 3 + l, pl.ds(3 + 32 * c, 32)] = value.astype(BF16).reshape(
                    32, STRIPS, CH)

            if b == BLOCKS - 1:
                result(c).start()

            return 0

        with scope("finish"):
            lax.fori_loop(0, 2, finish, 0)

        gathered.wait_send()
        forward.wait_send()

    first_convolutions()
    spectral_part(0)
    second_convolutions()
    spectral_part(1)

    with scope("store"):
        for c in range(2):
            result(c).wait()


def restore(strips):
    return jnp.transpose(strips, (0, 2, 1, 3)).reshape(ROWS, COLS, CH)


def per_device(field, conv_weight, conv_bias, spec_real, spec_imag):
    forward, inverse, turn = tables()
    args = (field, conv_weight, jnp.transpose(conv_bias, (1, 0, 2)), spec_real, spec_imag,
            jnp.asarray(forward), jnp.asarray(inverse), jnp.asarray(turn))
    tile = (STRIPS, CH)
    dma = pltpu.SemaphoreType.DMA
    strips = pl.pallas_call(
        kernel,
        out_shape=jax.ShapeDtypeStruct((ROWS, TILES) + tile, BF16),
        in_specs=[pl.BlockSpec(memory_space=pl.ANY)] * len(args),
        out_specs=pl.BlockSpec(memory_space=pl.ANY),
        scratch_shapes=[pltpu.VMEM(a.shape, a.dtype) for a in args] + [
            pltpu.VMEM((BLOCKS * CONVS, 12 * CH, 2 * CH), BF16),
            pltpu.VMEM((BLOCKS * OWNED, 2 * CH, 2 * CH), BF16),
            pltpu.VMEM((BLOCKS + 1, 10, EXT) + tile, BF16),
            pltpu.VMEM((8, EXT) + tile, BF16),
            pltpu.VMEM((6, EXT) + tile, BF16),
            pltpu.VMEM((BLOCKS, 4, EXT) + tile, BF16),
            pltpu.VMEM((BLOCKS, 2, 10, 3) + tile, BF16),
            pltpu.VMEM((ROWS, COLS, CH), F32),
            pltpu.VMEM((2, CHIPS, 16, ROWS * CH), F32),
            pltpu.VMEM((BLOCKS, CHIPS, 16, ROWS * CH), F32),
            pltpu.VMEM((CHIPS, 16, ROWS * CH), F32),
            pltpu.VMEM((BLOCKS, CHIPS - 1, 16, ROWS * CH), F32),
            pltpu.VMEM((BLOCKS, 2, CHIPS, 16, ROWS * CH), BF16),
            pltpu.VMEM((6, EXT) + tile, BF16),
            pltpu.VMEM((2, 2, CHIPS, 16, 3 * CH), BF16),
            dma((8,)), dma((4, 2)), dma((4, 2)), dma((2, 8)), dma((2, 8)),
            dma((1,)), dma((BLOCKS,)),
            dma((1,)), dma((BLOCKS,)), dma((1,)), dma((BLOCKS,)),
            dma((1,)), dma((BLOCKS,)),
            dma((2, 5)), dma((2, 5)), dma((2,)), dma((2,)), dma((2,)), dma((2,)),
            pltpu.VMEM((EXT,) + tile, BF16), pltpu.VMEM((EXT,) + tile, BF16),
            dma((11,)), dma((11,)),
        ],
        compiler_params=pltpu.CompilerParams(
            collective_id=0, has_side_effects=True, vmem_limit_bytes=62 * 1024 * 1024),
    )(*args)
    return restore(strips)


def solution(mesh):
    return jax.shard_map(
        per_device,
        mesh=mesh,
        in_specs=(
            P("lat", "lon", None),
            P(),
            P(),
            P(None, "lon", None, None),
            P(None, "lon", None, None),
        ),
        out_specs=P("lat", "lon", None),
        check_vma=False,
    )
```
